32 devices in a mesh: tile: 8 (over z, y), chan: 4 (over x, core).
Axes of the slice: x: 2, y: 2, z: 4, core: 2. Of those that a mesh axis runs over, the one named last changes fastest.
Arguments:
- feat: bfloat16 [128, 64, 256], P('tile', 'chan'), may hold values from -6 to 6
- lift: float32 [64], replicated, may hold values from -3 to 3
- dilation4_weight: bfloat16 [3, 3, 64, 64], replicated, may hold values from -0.25 to 0.25
- dilation8_weight: bfloat16 [3, 3, 64, 64], replicated, may hold values from -0.25 to 0.25
- entry_fraction: bfloat16 [2048, 128], P('tile'), may hold values from 0.019897461 to 0.19921875
- entry_target_tile: int32 [2048, 1], P('tile'), may hold values from 0 to 7; in each aligned block of 256 rows (0 to 255, 256 to 511, ...) at most 64 rows name the same one
- entry_owner_tile: int32 [2048], P('tile'), may hold values from 0 to 31
- entry_local_net: int32 [2048], P('tile'), may hold values from 0 to 63
- pin_demand_weight: float32 [2048], P('tile'), may hold values from 0.2 to 2
- pin_local_net: int32 [2048], P('tile'), may hold values from 0 to 63
- pin_global_cell: int32 [2048], P('tile'), may hold values from 0 to 511
Outputs:
- cell_grad: float32 [512], P('tile')
The draws below stay inside these ranges and needn't reach their ends.
Inputs may be any that keep to these rules, and one draw needn't show every extreme that they name: `entry_target_tile`: among the entries of one tile index, at most 64 name the same destination, and in some tile index exactly 64 do.
All inputs are finite; a program needn't handle non-finite values.
Results may differ from the reference program's by a relative error of at most 0.0003.
Values may be sent and summed in bfloat16 or wider, within the bound.
A program may use at most 64 MiB of HBM per device.

```python
import math
import jax
import jax.numpy as jnp
import numpy as np
from jax import lax

FEATURE_CHANNELS = 64
ROWS_DEV = 16
W = 256
ENT_DEV = 256
NET_DEV = 64
PIN_DEV = 256
TILE_DEV = 32
CAP = 64
HEIGHT = 128
TILES = 256
ENTRIES = 2048
NETS = 512
PINS = 2048
CELLS = 512
N_TILE = 8


def touch_ends(values, key, smallest, top_value):
    dims = values.shape
    index_at = [jax.random.randint(jax.random.fold_in(key, axis), (), 0, dims[axis]) for axis in range(len(dims))]
    values = values.at[tuple(index_at)].set(smallest)
    longest = dims.index(max(dims))
    index_at[longest] = (index_at[longest] + 1) % dims[longest]
    return values.at[tuple(index_at)].set(top_value)


def levels(key, extent, cuts, least, top_value):
    factor_of = 1.0
    for dim, parts in cuts:
        steps = jax.random.uniform(jax.random.fold_in(jax.random.fold_in(key, 6), dim), (parts,), jnp.float32, least / len(cuts), top_value / len(cuts))
        factor_of = factor_of * jnp.repeat(jnp.exp(steps), extent[dim] // parts).reshape((-1,) + (1,) * (len(extent) - 1 - dim))
    return factor_of


def assign_block(key, own, number, rows, count, top, reach, skew):
    sequence = jax.random.permutation(key, count)
    heavy_load, ordinary = portions_of(count, rows * top, reach, skew, True), portions_of(count, rows * top, reach, skew, False)
    places = jnp.arange(count)

    def named(lengths, rotation):
        used = int((lengths > 0).sum())
        fixed = max(1, used // 4)
        passed = fixed + (places - fixed + rotation * (used - fixed)) % max(1, count - fixed)
        return jnp.zeros((count,), jnp.int32).at[sequence[jnp.where(places < fixed, places, passed)]].set(jnp.asarray(lengths, jnp.int32))

    lengths = jnp.where(number % 4 == 0, named(heavy_load, number // 4), named(ordinary, number - number // 4 - 1))
    mixed = jax.random.permutation(jax.random.fold_in(own, 3), count)
    donor, receiver = mixed[0:count // 2 * 2:2], mixed[1:count // 2 * 2:2]
    slack = jnp.minimum(lengths[donor] - 1, reach - lengths[receiver]) // 2
    slack = jnp.where((donor == sequence[0]) | (receiver == sequence[0]) | (lengths[receiver] == 0), 0, jnp.maximum(slack, 0))
    passed = jax.random.randint(jax.random.fold_in(own, 4), (count // 2,), 0, 1 << 20) % (slack + 1)
    lengths = lengths.at[donor].add(-passed).at[receiver].add(passed)
    items = jnp.searchsorted(jnp.cumsum(lengths), jnp.arange(rows * top), side="right").astype(jnp.int32)
    grid = items.reshape(top, rows).T
    grid = grid[jax.random.permutation(jax.random.fold_in(own, 1), rows)]
    rotation = jax.random.randint(jax.random.fold_in(own, 2), (rows, 1), 0, top)
    return jnp.take_along_axis(grid, (jnp.arange(top)[None, :] + rotation) % top, axis=1)


def portions_of(amount, total, limit, skew, full):
    weights = [(1 << 20) // math.isqrt(standing ** skew) + 1 for standing in range(1, amount + 1)]
    largest = limit if full else min(limit, max(-(-total // amount), total * weights[0] // sum(weights)))
    least = 1 if total - largest >= amount - 1 else 0
    holding, surplus = [largest] + [least] * (amount - 1), total - largest - least * (amount - 1)
    while surplus > 0:
        movable = [i for i in range(1, amount) if holding[i] < largest] or [i for i in range(1, amount) if holding[i] < limit]
        mass, budget = sum([weights[i] for i in movable]), surplus
        for i in movable:
            extra = min(limit - holding[i], max(1, budget * weights[i] // mass), surplus)
            holding[i] = holding[i] + extra
            surplus = surplus - extra
    return np.array(holding)


def scatter_about(own_key, extent, scale, bound, pieces=(), held_as=jnp.bfloat16):
    array = scale * jax.random.normal(own_key, extent, jnp.float32)
    if pieces:
        array = array * levels(own_key, extent, pieces, -0.22, 0.18)
    return jnp.clip(array, -bound, bound).astype(held_as)


def setup_inputs(seed: int = 0) -> dict:
    seeds = jax.random.split(jax.random.key(seed), 12)
    feat = scatter_about(seeds[0], (HEIGHT, FEATURE_CHANNELS, W), 1.0, 6.0, ((0, 8), (1, 4)))
    lift = scatter_about(seeds[1], (FEATURE_CHANNELS,), 0.5, 3.0, (), jnp.float32)
    dilation4_weight = scatter_about(seeds[2], (3, 3, FEATURE_CHANNELS, FEATURE_CHANNELS), (9 * FEATURE_CHANNELS) ** -0.5, 0.25)
    dilation8_weight = scatter_about(seeds[3], (3, 3, FEATURE_CHANNELS, FEATURE_CHANNELS), (9 * FEATURE_CHANNELS) ** -0.5, 0.25)
    entry_fraction = jnp.clip(jnp.exp(math.log(0.19921875) - 2.3038113 * jax.random.uniform(seeds[4], (ENTRIES, 128), jnp.float32) ** levels(seeds[4], (ENTRIES, 128), ((0, 8),), -0.2, 0.2)), 0.019897461, 0.19921875).astype(jnp.bfloat16)
    entry_target_tile_keys = jax.random.split(jax.random.fold_in(seeds[5], 1), ENTRIES // ENT_DEV)
    entry_target_tile_turns = jax.random.permutation(jax.random.fold_in(seeds[5], 3), ENTRIES // ENT_DEV)
    entry_target_tile = jax.vmap(lambda own, number: assign_block(jax.random.fold_in(seeds[5], 2), own, number, ENT_DEV, N_TILE, 1, CAP, 2))(entry_target_tile_keys, entry_target_tile_turns).reshape((ENTRIES, 1))
    entry_owner_tile = touch_ends(jax.random.randint(seeds[6], (ENTRIES,), 0, TILE_DEV), jax.random.fold_in(seeds[6], 1), 0, TILE_DEV - 1).astype(jnp.int32)
    entry_local_net = touch_ends(jax.random.randint(seeds[7], (ENTRIES,), 0, NET_DEV), jax.random.fold_in(seeds[7], 1), 0, NET_DEV - 1).astype(jnp.int32)
    pin_demand_weight = jnp.clip(jnp.exp(math.log(2.0) - 2.3025851 * jax.random.uniform(seeds[8], (PINS,), jnp.float32) ** levels(seeds[8], (PINS,), ((0, 8),), -0.2, 0.2)), 0.2, 2.0)
    pin_local_net = touch_ends(jax.random.randint(seeds[9], (PINS,), 0, NET_DEV), jax.random.fold_in(seeds[9], 1), 0, NET_DEV - 1).astype(jnp.int32)
    pin_global_cell = touch_ends(jax.random.randint(seeds[10], (PINS,), 0, CELLS), jax.random.fold_in(seeds[10], 1), 0, CELLS - 1).astype(jnp.int32)
    return dict(feat=feat, lift=lift, dilation4_weight=dilation4_weight, dilation8_weight=dilation8_weight, entry_fraction=entry_fraction, entry_target_tile=entry_target_tile, entry_owner_tile=entry_owner_tile, entry_local_net=entry_local_net, pin_demand_weight=pin_demand_weight, pin_local_net=pin_local_net, pin_global_cell=pin_global_cell)


def dilated_result(source, kernel_in, dilation):
    row_total, col_count = source.shape[0], source.shape[1]
    chan_out = kernel_in.shape[3]
    padded = jnp.pad(source, ((dilation, dilation), (dilation, dilation), (0, 0)))
    kernel = kernel_in.astype(jnp.float32)

    def one_block(block_id):
        offset = (block_id * ROWS_DEV).astype(jnp.int32)
        window = lax.dynamic_slice_in_dim(padded, offset, ROWS_DEV + 2 * dilation, 0).astype(jnp.float32)
        running = jnp.zeros((ROWS_DEV, col_count, chan_out), jnp.float32)
        for row_tap in range(3):
            for col_tap in range(3):
                part_in = window[row_tap * dilation:row_tap * dilation + ROWS_DEV, col_tap * dilation:col_tap * dilation + col_count]
                running = running + jnp.einsum("rwc,co->rwo", part_in, kernel[row_tap, col_tap])
        return running

    result = lax.map(one_block, jnp.arange(row_total // ROWS_DEV, dtype=jnp.int32))
    return result.reshape(row_total, col_count, chan_out)


def flipped_kernel(kernel):
    return jnp.transpose(kernel[::-1, ::-1], (0, 1, 3, 2))


def reference(feat, lift, dilation4_weight, dilation8_weight, entry_fraction, entry_target_tile, entry_owner_tile, entry_local_net, pin_demand_weight, pin_local_net, pin_global_cell):
    feat_rows = jnp.transpose(feat, (0, 2, 1))
    pin_owner = (jnp.arange(PINS) // PIN_DEV).astype(jnp.int32)
    net_of_pin = pin_local_net + pin_owner * NET_DEV
    strength = jax.ops.segment_sum(pin_demand_weight, net_of_pin, num_segments=NETS)
    entry_owner = (jnp.arange(ENTRIES) // ENT_DEV).astype(jnp.int32)
    net_of_entry = entry_local_net + entry_owner * NET_DEV
    tile_of_entry = entry_target_tile[:, 0] * TILE_DEV + entry_owner_tile
    frac = entry_fraction.astype(jnp.float32)
    payload = strength[net_of_entry][:, None] * frac
    tiles = jax.ops.segment_sum(payload, tile_of_entry, num_segments=TILES)
    demand = tiles.reshape(N_TILE, ROWS_DEV // 8, W // 16, 8, 16).transpose(0, 1, 3, 2, 4).reshape(HEIGHT, W)
    input_features = (feat_rows.astype(jnp.float32) + demand[:, :, None] * lift[None, None, :]).astype(jnp.bfloat16)
    first_preactivation = dilated_result(input_features, dilation4_weight, 4)
    hidden_features = jax.nn.silu(first_preactivation).astype(jnp.bfloat16)
    second_output = dilated_result(hidden_features, dilation8_weight, 8)
    second_gradient = jax.nn.sigmoid(second_output).astype(jnp.bfloat16)
    hidden_gradient = dilated_result(second_gradient, flipped_kernel(dilation8_weight), 8)
    sigmoid_pre = jax.nn.sigmoid(first_preactivation)
    preactivation_gradient = (hidden_gradient * sigmoid_pre * (1.0 + first_preactivation * (1.0 - sigmoid_pre))).astype(jnp.bfloat16)
    inputs_gradient = dilated_result(preactivation_gradient, flipped_kernel(dilation4_weight), 4)
    grad_demand = jnp.sum(inputs_gradient * lift[None, None, :], axis=2)
    grad_tiles = grad_demand.reshape(N_TILE, ROWS_DEV // 8, 8, W // 16, 16).transpose(0, 1, 3, 2, 4).reshape(TILES, 128)
    entry_grad = jnp.sum(grad_tiles[tile_of_entry] * frac, axis=1)
    grad_net = jax.ops.segment_sum(entry_grad, net_of_entry, num_segments=NETS)
    return jax.ops.segment_sum(grad_net[net_of_pin], pin_global_cell, num_segments=CELLS)
```

```python
import functools

import jax
import jax.numpy as jnp
from jax import lax
from jax.experimental import pallas as pl
from jax.experimental.pallas import tpu as pltpu
from jax.sharding import PartitionSpec as P

MESH = pl.DeviceIdType.MESH
CELL_DEV = 64
TILE_ROWS = 8
TILE_COLS = 16
LANES = 128
HALO = 24
GROUP = 4
META = 16
SPREAD = 4096
RIMS = ("A0", "B0", "F", "A1", "B1", "R")
F32 = jnp.float32
BF16 = jnp.bfloat16


def split(x, terms):
    parts = []
    for _ in range(terms):
        part = x.astype(BF16)
        parts.append(part)
        x = x - part.astype(F32)
    return parts


def kernel(
    tiles, chans,
    feat_in, lift_in, w4_in, w8_in, frac_in, target_in, owner_in, net_e_in, weight_in, net_p_in,
    cell_in,
    out,
    feat, lift, w4, w8, frac, target, owner, net_e, weight, net_p, cell, load_sem,
    win, gath, inp, pre, hid, sec, gpre, wm1, wm2, wm3, wm4,
    fmask, dbuf, dsend, drecv, demand, gown, esend, erecv, to_cell, tile_hot, csend, crecv,
    fsend_sem, frecv_sem, own_sem, hsend_sem, hrecv_sem, dsend_sem, drecv_sem,
    esend_sem, erecv_sem, csend_sem, crecv_sem,
):
    ti = lax.axis_index("tile")
    ci = lax.axis_index("chan")
    rows, chan_own, cols = feat.shape
    chan = chan_own * chans
    own_cols = cols // chans
    margin = (LANES - own_cols) // 2
    half = rows // 2
    in_rows = rows + 2 * HALO
    others = tiles * chans - 1
    entries, pins = frac.shape[0], weight.shape[1]
    cap = esend.shape[1] - META
    per = LANES // cap
    height = rows * tiles

    par = ci % 2
    alike = ti % 2 == par
    wt = ti - ti % 2 + par
    wc = ci - par + ti % 2
    near = 2 * par - 1
    top = wt * rows

    def at_work(t, c):
        return (t - t % 2 + c % 2, c - c % 2 + t % 2)

    loads = [
        pltpu.make_async_copy(src, dst, load_sem.at[n])
        for n, (src, dst) in enumerate(
            [
                (feat_in, feat), (target_in, target), (owner_in, owner), (net_e_in, net_e),
                (weight_in, weight), (net_p_in, net_p), (frac_in, frac), (lift_in, lift),
                (cell_in, cell), (w4_in, w4), (w8_in, w8),
            ]
        )
    ]
    for load in loads:
        load.start()

    barrier = pltpu.get_barrier_semaphore()

    def wrap(number, count):
        return jnp.where(number >= count, number - count, number)

    def inside(strip):
        return (strip >= 0) & (strip < tiles)

    def each(lo, hi, fn):
        if hi - lo <= 32:
            for step in range(lo, hi):
                fn(step)
        else:
            def body(step, carry):
                fn(step)
                return carry
            lax.fori_loop(lo, hi, body, 0)

    def each_peer(fn):
        def along(back):
            hop = tiles - 1 - back
            for turn in range(chans):
                fn(hop * chans + turn, (wrap(ti + hop, tiles), wrap(ci + turn, chans)))
        each(0, tiles - 1, along)
        for turn in range(1, chans):
            fn(turn, (ti, wrap(ci + turn, chans)))

    each_peer(
        lambda n, who: pl.semaphore_signal(barrier, inc=1, device_id=who, device_id_type=MESH)
    )

    loads[0].wait()

    flat = feat[...].astype(F32).reshape(rows * chan_own, cols)
    lane = lax.broadcasted_iota(jnp.int32, (1, LANES), 1)
    for k in range(chans):
        first_col = k * own_cols - margin
        turned = pltpu.roll(flat, (-first_col) % cols, 1)[:, :LANES]
        on_map = (lane + first_col >= 0) & (lane + first_col < cols)
        win[k] = jnp.where(on_map, turned, 0.0).astype(BF16).reshape(rows, chan_own, LANES)

    def span(delta):
        low = max(0, rows * delta - HALO)
        high = min(rows, rows * delta + HALO + rows)
        return low, high - low, HALO - rows * delta + low

    for delta in (1, -1, 2, -2):
        @pl.when(jnp.logical_not(inside(wt - delta)))
        def _(delta=delta):
            _, count, at = span(delta)
            inp[at : at + count] = jnp.zeros((count, chan, LANES), BF16)

    for load in loads[1:]:
        load.wait()
    per_row = cols // TILE_COLS
    own, cell_no = owner[...], cell[...]
    target_row = target[...].astype(F32)
    table = jnp.concatenate(
        [
            (target[...] * (rows // TILE_ROWS) + own // per_row).astype(F32),
            (own % per_row).astype(F32),
            net_e[...].astype(F32),
            weight[...],
            net_p[...].astype(F32),
            target_row,
            jnp.zeros((2, entries), F32),
        ],
        axis=0,
    )
    columns = jnp.transpose(table)
    wpin_col, net_p_col = columns[:, 3:4], columns[:, 4:5]
    strength = jnp.sum(
        jnp.where(net_p_col == table[2:3, :], wpin_col, 0.0), axis=0, keepdims=True
    )
    src_j = lax.broadcasted_iota(jnp.int32, (LANES, TILE_ROWS * LANES), 0)
    dst_j = lax.broadcasted_iota(jnp.int32, (LANES, TILE_ROWS * LANES), 1)
    pick = src_j == (dst_j // LANES) * TILE_COLS + dst_j % TILE_COLS
    spread = jnp.dot(
        frac[...], jnp.where(pick, 1.0, 0.0).astype(BF16), preferred_element_type=F32
    )
    wide = lax.broadcasted_iota(jnp.int32, (1, TILE_ROWS * LANES), 1) % LANES
    block = (wide + ci * own_cols - margin + TILE_COLS * LANES) // TILE_COLS - LANES
    fmask[...] = jnp.where(columns[:, 1:2] == block.astype(F32), spread, 0.0).astype(BF16)
    blocks = height // TILE_ROWS
    block_row = lax.broadcasted_iota(jnp.int32, (blocks, entries), 0).astype(F32)
    placed = jnp.where(block_row == table[0:1, :], strength, 0.0)
    left = jnp.concatenate(split(placed, 2), axis=0)
    partial = jnp.dot(left, fmask[...], preferred_element_type=F32)
    partial = partial[:blocks] + partial[blocks:]
    for i in range(TILE_ROWS):
        dbuf[pl.ds(i, blocks, stride=TILE_ROWS), :] = partial[:, i * LANES : (i + 1) * LANES]
    dsend[...] = dbuf[...].astype(BF16)

    lift_row = lift[...]
    lift_col = jnp.transpose(jnp.broadcast_to(lift_row, (LANES, chan)))
    for u in range(3):
        for v in range(3):
            at_v, at_u = slice(v * chan, (v + 1) * chan), slice(u * chan, (u + 1) * chan)
            wm1[at_v, at_u] = jnp.transpose(w4[u, v].astype(F32)).astype(BF16)
            wm2[at_v, at_u] = jnp.transpose(w8[u, v].astype(F32)).astype(BF16)
            wm3[at_v, at_u] = w8[2 - u, 2 - v]
    taps = []
    for v in range(3):
        taps.append(
            jnp.concatenate(
                [
                    jnp.sum(
                        w4[2 - u, 2 - v].astype(F32) * lift_col[:, :chan], axis=0, keepdims=True
                    )
                    for u in range(3)
                ],
                axis=1,
            )
        )
    tap_rows = jnp.concatenate(taps + [jnp.zeros((5, 3 * chan), F32)], axis=0)
    hi, mid, low_part = [p.astype(F32) for p in split(tap_rows, 3)]
    wm4[...] = jnp.concatenate(
        [hi, mid, low_part, jnp.zeros((8, 3 * chan), F32)], axis=0
    ).astype(BF16)

    def feat_copy(turn, q, mine=False):
        h = ti % 2 if q == 0 else 1 - ti % 2
        to = wrap(ci + turn, chans)
        src = win.at[to, pl.ds(h * half, half)]
        dst = gath.at[
            pl.ds(h * half, half), pl.ds(pl.multiple_of(ci * chan_own, chan_own), chan_own)
        ]
        if mine:
            return pltpu.make_async_copy(src, dst, own_sem.at[q])
        return pltpu.make_async_remote_copy(
            src_ref=src, dst_ref=dst,
            send_sem=fsend_sem.at[q, turn], recv_sem=frecv_sem.at[q, turn],
            device_id=at_work(ti, to), device_id_type=MESH,
        )

    def feat_arrival(turn, q):
        h = par if q == 0 else 1 - par
        come = wrap(wc + chans - turn, chans)
        dst = gath.at[
            pl.ds(h * half, half), pl.ds(pl.multiple_of(come * chan_own, chan_own), chan_own)
        ]
        return pltpu.make_async_remote_copy(
            src_ref=dst, dst_ref=dst,
            send_sem=fsend_sem.at[q, turn], recv_sem=frecv_sem.at[q, turn],
            device_id=(ti, wrap(ci + 1, chans)), device_id_type=MESH,
        )

    def unless_mine(fn):
        @pl.when(jnp.logical_not(alike))
        def _():
            fn(False)

        @pl.when(alike)
        def _():
            fn(True)

    def feat_send(turn, q):
        if turn:
            feat_copy(turn, q).start()
        else:
            unless_mine(lambda mine: feat_copy(0, q, mine).start())

    def feat_wait(q):
        for turn in range(chans):
            if turn:
                feat_arrival(turn, q).wait_recv()
            else:
                unless_mine(
                    lambda mine: feat_copy(0, q, True).wait()
                    if mine else feat_arrival(0, q).wait_recv()
                )

    def demand_copy(step, mine=False):
        to = wrap(ti + step, tiles)
        src = dsend.at[pl.ds(pl.multiple_of(to * rows, rows), rows)]
        if mine:
            return pltpu.make_async_copy(src, drecv.at[step], own_sem.at[2])
        return pltpu.make_async_remote_copy(
            src_ref=src, dst_ref=drecv.at[step],
            send_sem=dsend_sem.at[step], recv_sem=drecv_sem.at[step],
            device_id=at_work(to, ci), device_id_type=MESH,
        )

    def entry_copy(step, mine=False):
        to = wrap(ti + step, tiles)
        if mine:
            return pltpu.make_async_copy(esend.at[to], erecv.at[ti], own_sem.at[3])
        return pltpu.make_async_remote_copy(
            src_ref=esend.at[to], dst_ref=erecv.at[ti],
            send_sem=esend_sem.at[step], recv_sem=erecv_sem.at[step],
            device_id=at_work(to, ci), device_id_type=MESH,
        )

    def entry_arrival(step):
        dst = erecv.at[wrap(wt + tiles - step, tiles)]
        return pltpu.make_async_remote_copy(
            src_ref=dst, dst_ref=dst,
            send_sem=esend_sem.at[step], recv_sem=erecv_sem.at[step],
            device_id=(ti, wrap(ci + 1, chans)), device_id_type=MESH,
        )

    pl.semaphore_wait(barrier, others)
    each(1, tiles, lambda s: demand_copy(s).start())
    unless_mine(lambda mine: demand_copy(0, mine).start())
    for q in range(2):
        for turn in range(chans - 1, -1, -1):
            feat_send(turn, q)

    before = lax.broadcasted_iota(jnp.int32, (entries, entries), 0) < lax.broadcasted_iota(
        jnp.int32, (entries, entries), 1
    )
    rank = jnp.sum(
        jnp.where((columns[:, 5:6] == target_row) & before, 1.0, 0.0), axis=0, keepdims=True
    )
    key = target_row * float(cap) + rank
    pin_rows = [
        row[:, n * LANES : (n + 1) * LANES]
        for row in (table[4:5, :], (cell_no // LANES).astype(F32), (cell_no % LANES).astype(F32))
        for n in range(pins // LANES)
    ]
    fixed = jnp.concatenate(
        [jnp.zeros((2, LANES), F32)] + pin_rows
        + [jnp.zeros((META - 2 - len(pin_rows), LANES), F32)],
        axis=0,
    )
    loose = jnp.concatenate(
        [table[2:3, :], own.astype(F32), jnp.zeros((META - 2, entries), F32)], axis=0
    ).astype(BF16)
    slot = lax.broadcasted_iota(jnp.int32, (cap, entries), 0).astype(F32)
    wide_slot = lax.broadcasted_iota(jnp.int32, (LANES, entries), 0) - (ti % per) * cap
    wide_slot = jnp.where(
        (wide_slot >= 0) & (wide_slot < cap), wide_slot, -(cap * tiles + 1)
    ).astype(F32)

    def pack(to):
        base = jnp.asarray(to * cap, F32) if isinstance(to, int) else (to * cap).astype(F32)
        hot = jnp.where(slot + base == key, 1.0, 0.0).astype(BF16)
        esend[to, :cap] = jnp.dot(hot, frac[...], preferred_element_type=F32).astype(BF16)
        hot = jnp.where(wide_slot + base == key, 1.0, 0.0).astype(BF16)
        meta = lax.dot_general(
            loose, hot, (((1,), (1,)), ((), ())), preferred_element_type=F32
        )
        esend[to, cap:] = (meta + fixed).astype(BF16)

    each(0, tiles, pack)
    each(1, tiles, lambda s: entry_copy(s).start())
    unless_mine(lambda mine: entry_copy(0, mine).start())

    def rim(role, sending):
        if role == "A0":
            to, h = wt + near, par
        elif role == "A1":
            to, h = wt + near, 1 - par
        elif role == "B0":
            to, h = wt - near, par
        elif role == "B1":
            to, h = wt - near, 1 - par
        else:
            to, h = wt - 2 * near, 1 - par
        n = RIMS.index(role)
        if sending:
            start = HALO + h * half
            if role == "R":
                start, to = HALO + rows * near + half * (1 - par), wt - near
                at = HALO + 2 * rows * near + half * (1 - par)
                there = inside(to) & inside(wt + near)
            else:
                at = HALO + (wt - to) * rows + h * half
                there = inside(to)
            copy = pltpu.make_async_remote_copy(
                src_ref=inp.at[pl.ds(start, half)], dst_ref=inp.at[pl.ds(at, half)],
                send_sem=hsend_sem.at[n], recv_sem=hrecv_sem.at[n],
                device_id=at_work(to, wc), device_id_type=MESH,
            )
        else:
            come, at = {
                "A0": (wt + near, HALO + rows * near + half * (1 - par)),
                "A1": (wt + near, HALO + rows * near + half * par),
                "B0": (wt - near, HALO - rows * near + half * (1 - par)),
                "B1": (wt - near, HALO - rows * near + half * par),
                "F": (wt + 2 * near, HALO + 2 * rows * near + half * (1 - par)),
                "R": (wt - 2 * near, HALO - 2 * rows * near + half * par),
            }[role]
            there = inside(come)
            dst = inp.at[pl.ds(at, half)]
            copy = pltpu.make_async_remote_copy(
                src_ref=dst, dst_ref=dst,
                send_sem=hsend_sem.at[n], recv_sem=hrecv_sem.at[n],
                device_id=(ti, wrap(ci + 1, chans)), device_id_type=MESH,
            )
        return there, copy

    def rim_start(role):
        there, copy = rim(role, True)

        @pl.when(there)
        def _():
            copy.start()

    def rim_sent(role):
        there, copy = rim(role, True)

        @pl.when(there)
        def _():
            copy.wait_send()

    def rim_wait(role):
        there, copy = rim(role, False)

        @pl.when(there)
        def _():
            copy.wait_recv()

    each(1, tiles, lambda s: demand_copy(s).wait())
    unless_mine(lambda mine: demand_copy(0, mine).wait())
    demand[...] = lax.fori_loop(
        1, tiles, lambda s, t: t + drecv[s].astype(F32), drecv[0].astype(F32)
    )

    def fill(h):
        for j in range(half):
            row = h * half + j
            add = lift_col * demand[pl.ds(row, 1), :]
            inp[HALO + row] = (gath[row].astype(F32) + add).astype(BF16)

    feat_wait(0)
    fill(par)
    rim_start("A0")
    rim_start("B0")
    feat_wait(1)
    fill(1 - par)
    rim_start("F")
    rim_start("A1")
    rim_start("B1")

    def in_map(row):
        return (row >= 0) & (row < height)

    col = lane + wc * own_cols - margin
    col_ok = ((col >= 0) & (col < cols)).astype(F32)

    def gathered(ref, at, dilation):
        return jnp.concatenate(
            [
                jnp.concatenate([ref[at + j + u * dilation] for u in range(3)], axis=0)
                for j in range(GROUP)
            ],
            axis=1,
        )

    def conv(ref, at, weights, dilation):
        result = jnp.dot(weights[...], gathered(ref, at, dilation), preferred_element_type=F32)
        parts = []
        for j in range(GROUP):
            one = result[:, j * LANES : (j + 1) * LANES]
            parts.append(
                one[chan : 2 * chan]
                + pltpu.roll(one[:chan], dilation, 1)
                + pltpu.roll(one[2 * chan :], LANES - dilation, 1)
            )
        return parts

    def keep_of(row):
        return col_ok * in_map(row).astype(F32)

    def first(at):
        keep = keep_of(top - 20 + at)
        for j, value in enumerate(conv(inp, at, wm1, 4)):
            pre[at + j] = value
            hid[at + j] = (value * jax.nn.sigmoid(value) * keep).astype(BF16)

    def second(at):
        keep = keep_of(top - 12 + at)
        for j, value in enumerate(conv(hid, at, wm2, 8)):
            sec[at + j] = (jax.nn.sigmoid(value) * keep).astype(BF16)

    def third(at):
        keep = keep_of(top - 4 + at)
        for j, value in enumerate(conv(sec, at, wm3, 8)):
            p = pre[at + j + 16]
            s = jax.nn.sigmoid(p)
            gpre[at + j] = (value * s * (1.0 + p * (1.0 - s)) * keep).astype(BF16)

    owned = ((lane >= margin) & (lane < margin + own_cols)).astype(F32)

    def fourth(at):
        result = jnp.dot(wm4[...], gathered(gpre, at, 4), preferred_element_type=F32)
        result = result[0:8] + result[8:16] + result[16:24]
        for j in range(GROUP):
            one = result[:, j * LANES : (j + 1) * LANES]
            line = (
                one[1:2]
                + pltpu.roll(one, 4, 1)[0:1]
                + pltpu.roll(one, LANES - 4, 1)[2:3]
            )
            gown[at + j : at + j + 1, :] = line * owned

    def groups(*work):
        for side in range(2):
            @pl.when(par == side)
            def _(side=side):
                for fn, count, which in work:
                    for g in which:
                        fn(count - GROUP - GROUP * g if side else GROUP * g)

    def stage(ones, twos=(), threes=(), fours=()):
        groups(
            (first, rows + 40, ones), (second, rows + 24, twos),
            (third, rows + 8, threes), (fourth, rows, fours),
        )

    each(1, tiles, lambda s: entry_arrival(s).wait_recv())
    unless_mine(
        lambda mine: entry_copy(0, True).wait() if mine else entry_arrival(0).wait_recv()
    )

    per_tile = rows // TILE_ROWS
    n_tiles = tile_hot.shape[0]
    lane_of = lax.broadcasted_iota(jnp.int32, (1, LANES), 1)
    block_q = min(to_cell.shape[1], 4 * LANES)

    def cells_of(g):
        known = [erecv[g * per + n, cap:, :].astype(F32) for n in range(per)]
        meta = known[0]
        for k in known[1:]:
            meta = meta + k
        net_row = meta[0:1, :] + (lane_of // cap * SPREAD).astype(F32)
        mine = meta[1:2, :].astype(jnp.int32)
        across = mine % per_row - wc * (own_cols // TILE_COLS)
        which = across * per_tile + mine // per_row
        which = jnp.where((across >= 0) & (across < own_cols // TILE_COLS), which, -1)
        at_g = pl.multiple_of(g * LANES, LANES)
        tile_hot[:, pl.ds(at_g, LANES)] = jnp.where(
            lax.broadcasted_iota(jnp.int32, (n_tiles, LANES), 0) == which, 1.0, 0.0
        )
        count = pins // LANES

        def pin_row(n, at):
            return jnp.concatenate([known[n][2 + at + m : 3 + at + m, :] for m in range(count)], axis=1)

        net_pin = jnp.concatenate([pin_row(n, 0) + float(n * SPREAD) for n in range(per)], axis=1)
        cell_row = jnp.concatenate(
            [pin_row(n, count) * float(LANES) + pin_row(n, 2 * count) for n in range(per)], axis=1
        )
        net_col = jnp.transpose(jnp.broadcast_to(net_row, (8, LANES)))[:, 0:1]
        same = jnp.where(net_col == net_pin, 1.0, 0.0).astype(BF16)

        def some(q):
            at_q = pl.multiple_of(q * block_q, LANES)
            number = (lax.broadcasted_iota(jnp.int32, (block_q, per * pins), 0) + q * block_q).astype(F32)
            hot = jnp.where(number == cell_row, 1.0, 0.0).astype(BF16)
            to_cell[pl.ds(at_g, LANES), pl.ds(at_q, block_q)] = lax.dot_general(
                same, hot, (((1,), (1,)), ((), ())), preferred_element_type=F32
            ).astype(BF16)

        loop(to_cell.shape[1] // block_q, some)

    def loop(count, fn):
        if count <= 4:
            for n in range(count):
                fn(n)
        else:
            def body(n, carry):
                fn(n)
                return carry
            lax.fori_loop(0, count, body, 0)

    loop(tiles // per, cells_of)

    rim_wait("B0")
    rim_wait("B1")
    stage(range(6, 12))
    rim_wait("A0")
    rim_start("R")
    stage(range(4, 6))
    rim_wait("R")
    stage(range(12, 14), range(4, 10), range(4, 6))
    rim_wait("A1")
    stage(range(2, 4), range(2, 4), range(2, 4), range(2, 4))
    rim_wait("F")
    stage(range(0, 2), range(0, 2), range(0, 2), range(0, 2))

    grads = gown[...]
    right = lax.broadcasted_iota(jnp.int32, (TILE_ROWS, LANES), 0) == (
        lax.broadcasted_iota(jnp.int32, (TILE_ROWS, LANES), 1) // TILE_COLS
    )
    leaning = [
        pltpu.roll(
            grads[a * TILE_ROWS : (a + 1) * TILE_ROWS], 0, 1, stride=TILE_COLS, stride_axis=0
        )
        for a in range(per_tile)
    ]
    parts = []
    for b in range(own_cols // TILE_COLS):
        for a in range(per_tile):
            moved = pltpu.roll(leaning[a], (-margin - b * TILE_COLS) % LANES, 1)
            parts.append(jnp.sum(jnp.where(right, moved, 0.0), axis=0, keepdims=True))
    by_tile = jnp.concatenate(
        [p.astype(F32) for p in split(jnp.concatenate(parts, axis=0), 3)], axis=0
    ).astype(BF16)
    all_frac = erecv[:, :cap, :].reshape(tiles * cap, LANES)
    found = lax.dot_general(
        by_tile, all_frac, (((1,), (1,)), ((), ())), preferred_element_type=F32
    )
    found = found[:n_tiles] + found[n_tiles : 2 * n_tiles] + found[2 * n_tiles :]
    entry_grad = jnp.sum(found * tile_hot[...], axis=0, keepdims=True)
    pieces = jnp.concatenate(
        [p.astype(F32) for p in split(entry_grad, 3)] + [jnp.zeros((5, tiles * cap), F32)], axis=0
    ).astype(BF16)
    cells = jnp.dot(pieces, to_cell[...], preferred_element_type=F32)
    cells = cells[0:1] + cells[1:2] + cells[2:3]
    for u in range(csend.shape[0]):
        csend[u] = cells[:, u * LANES : (u + 1) * LANES]

    share = LANES // CELL_DEV

    def cell_copy(step, to):
        return pltpu.make_async_remote_copy(
            src_ref=csend.at[to[0] // share], dst_ref=crecv.at[step],
            send_sem=csend_sem, recv_sem=crecv_sem,
            device_id=to, device_id_type=MESH,
        )

    each_peer(lambda n, who: cell_copy(n, who).start())

    for q in range(2):
        for turn in range(chans):
            if turn:
                feat_copy(turn, q).wait_send()
            else:
                @pl.when(jnp.logical_not(alike))
                def _(q=q):
                    feat_copy(0, q).wait_send()
    each(1, tiles, lambda s: entry_copy(s).wait_send())

    @pl.when(jnp.logical_not(alike))
    def _():
        entry_copy(0).wait_send()

    for role in RIMS:
        rim_sent(role)
    arrived = crecv.at[pl.ds(1, others)]
    pltpu.make_async_remote_copy(
        src_ref=arrived, dst_ref=arrived, send_sem=csend_sem, recv_sem=crecv_sem,
        device_id=(ti, wrap(ci + 1, chans)), device_id_type=MESH,
    ).wait()
    total = csend[ti // share] + jnp.sum(crecv[1:], axis=0)
    for n in range(1, share):
        total = jnp.where(ti % share == n, pltpu.roll(total, LANES - n * CELL_DEV, 1), total)
    out[...] = total


def solution(mesh):
    tiles, chans = mesh.shape["tile"], mesh.shape["chan"]

    def local(
        feat, lift, w4, w8, frac, target, owner, net_e, weight, net_p, cell,
    ):
        rows, chan_own, cols = feat.shape
        chan = chan_own * chans
        entries = frac.shape[0]
        pins = weight.shape[0]
        in_rows = rows + 2 * HALO
        height = rows * tiles
        cap = -(-(2 * entries // tiles) // META) * META
        n_tiles = rows // TILE_ROWS * (cols // chans // TILE_COLS)
        vm = pltpu.VMEM
        dma = pltpu.SemaphoreType.DMA
        result = pl.pallas_call(
            functools.partial(kernel, tiles, chans),
            out_shape=jax.ShapeDtypeStruct((1, LANES), F32),
            in_specs=[pl.BlockSpec(memory_space=pltpu.HBM)] * 11,
            out_specs=pl.BlockSpec(memory_space=pltpu.VMEM),
            scratch_shapes=[
                vm(feat.shape, BF16),
                vm((1, chan), F32),
                vm(w4.shape, BF16),
                vm(w8.shape, BF16),
                vm(frac.shape, BF16),
                vm((1, entries), jnp.int32),
                vm((1, entries), jnp.int32),
                vm((1, entries), jnp.int32),
                vm((1, pins), F32),
                vm((1, pins), jnp.int32),
                vm((1, pins), jnp.int32),
                dma((11,)),
                vm((chans, rows, chan_own, LANES), BF16),
                vm((rows, chan, LANES), BF16),
                vm((in_rows, chan, LANES), BF16),
                vm((rows + 40, chan, LANES), F32),
                vm((rows + 40, chan, LANES), BF16),
                vm((rows + 24, chan, LANES), BF16),
                vm((rows + 8, chan, LANES), BF16),
                vm((3 * chan, 3 * chan), BF16),
                vm((3 * chan, 3 * chan), BF16),
                vm((3 * chan, 3 * chan), BF16),
                vm((32, 3 * chan), BF16),
                vm((entries, TILE_ROWS * LANES), BF16),
                vm((height, LANES), F32),
                vm((height, LANES), BF16),
                vm((tiles, rows, LANES), BF16),
                vm((rows, LANES), F32),
                vm((rows, LANES), F32),
                vm((tiles, cap + META, LANES), BF16),
                vm((tiles, cap + META, LANES), BF16),
                vm((tiles * cap, tiles * CELL_DEV), BF16),
                vm((n_tiles, tiles * cap), F32),
                vm((tiles * CELL_DEV // LANES, 1, LANES), F32),
                vm((tiles * chans, 1, LANES), F32),
                dma((2, chans)),
                dma((2, chans)),
                dma((4,)),
                dma((len(RIMS),)),
                dma((len(RIMS),)),
                dma((tiles,)),
                dma((tiles,)),
                dma((tiles,)),
                dma((tiles,)),
                dma(()),
                dma(()),
            ],
            compiler_params=pltpu.CompilerParams(collective_id=0, has_side_effects=True),
        )(
            feat, lift.reshape(1, chan), w4, w8, frac, target.reshape(1, entries),
            owner.reshape(1, entries), net_e.reshape(1, entries), weight.reshape(1, pins),
            net_p.reshape(1, pins), cell.reshape(1, pins),
        )
        return result[0, :CELL_DEV]

    in_specs = (
        P("tile", "chan", None), P(), P(), P(),
        P("tile", None), P("tile", None),
        P("tile"), P("tile"), P("tile"), P("tile"), P("tile"),
    )
    return jax.shard_map(
        local, mesh=mesh, in_specs=in_specs, out_specs=P("tile"), check_vma=False
    )
```

```python
import functools

import jax
import jax.numpy as jnp
from jax import lax
from jax.experimental import pallas as pl
from jax.experimental.pallas import tpu as pltpu
from jax.sharding import PartitionSpec as P

MESH = pl.DeviceIdType.MESH
CELL_DEV = 64
TILE_ROWS = 8
TILE_COLS = 16
LANES = 128
HALO = 24
GROUP = 4
META = 16
SPREAD = 4096
RIMS = ("A0", "B0", "F", "A1", "B1", "R")
FEAT, DEMAND, ENTRY, RIM, CELL = range(5)
PART = 256
F32 = jnp.float32
BF16 = jnp.bfloat16


def split(x, terms):
    parts = []
    for _ in range(terms):
        part = x.astype(BF16)
        parts.append(part)
        x = x - part.astype(F32)
    return parts


def kernel(
    tiles, chans,
    feat_in, lift_in, w4_in, w8_in, frac_in, target_in, owner_in, net_e_in, weight_in, net_p_in,
    cell_in,
    out,
    feat, lift, w4, w8, frac, numbers, weight, load_sem,
    win, gath, inp, pre, hid, sec, gpre, wm1, wm2, wm3, wm4,
    fmask, dbuf, dsend, drecv, demand, gown, esend, erecv, to_cell, tile_hot, csend, crecv,
    send_sem, frecv_sem, hrecv_sem, drecv_sem, erecv_sem, crecv_sem,
):
    ti = lax.axis_index("tile")
    ci = lax.axis_index("chan")
    rows, chan_own, cols = feat.shape
    chan = chan_own * chans
    own_cols = cols // chans
    margin = (LANES - own_cols) // 2
    half = rows // 2
    in_rows = rows + 2 * HALO
    others = tiles * chans - 1
    entries, pins = frac.shape[0], weight.shape[1]
    cap = esend.shape[1] - META
    per = LANES // cap
    height = rows * tiles

    par = ci % 2
    alike = ti % 2 == par
    wt = ti - ti % 2 + par
    wc = ci - par + ti % 2
    near = 2 * par - 1
    top = wt * rows

    def at_work(t, c):
        return (t - t % 2 + c % 2, c - c % 2 + t % 2)

    target, owner, net_e, net_p, cell = (numbers.at[n] for n in range(5))
    loads = [
        pltpu.make_async_copy(src, dst, load_sem.at[n])
        for n, (src, dst) in enumerate(
            [
                (feat_in, feat), (weight_in, weight), (frac_in, frac), (lift_in, lift),
                (w4_in, w4), (w8_in, w8),
            ]
        )
    ]
    for load in loads:
        load.start()
    for src, dst in (
        (target_in, target), (owner_in, owner), (net_e_in, net_e), (net_p_in, net_p),
        (cell_in, cell),
    ):
        pltpu.make_async_copy(src, dst, load_sem.at[len(loads)]).start()

    barrier = pltpu.get_barrier_semaphore()

    def wrap(number, count):
        return jnp.where(number >= count, number - count, number)

    def inside(strip):
        return (strip >= 0) & (strip < tiles)

    def each(lo, hi, fn):
        if hi - lo <= 32:
            for step in range(lo, hi):
                fn(step)
        else:
            def body(step, carry):
                fn(step)
                return carry
            lax.fori_loop(lo, hi, body, 0)

    def each_peer(fn):
        def along(back):
            hop = tiles - 1 - back
            for turn in range(chans):
                fn(hop * chans + turn, (wrap(ti + hop, tiles), wrap(ci + turn, chans)))
        each(0, tiles - 1, along)
        for turn in range(1, chans):
            fn(turn, (ti, wrap(ci + turn, chans)))

    each_peer(
        lambda n, who: pl.semaphore_signal(barrier, inc=1, device_id=who, device_id_type=MESH)
    )

    loads[0].wait()

    flat = feat[...].astype(F32).reshape(rows * chan_own, cols)
    lane = lax.broadcasted_iota(jnp.int32, (1, LANES), 1)
    for k in range(chans):
        first_col = k * own_cols - margin
        turned = pltpu.roll(flat, (-first_col) % cols, 1)[:, :LANES]
        on_map = (lane + first_col >= 0) & (lane + first_col < cols)
        win[k] = jnp.where(on_map, turned, 0.0).astype(BF16).reshape(rows, chan_own, LANES)

    def span(delta):
        low = max(0, rows * delta - HALO)
        high = min(rows, rows * delta + HALO + rows)
        return low, high - low, HALO - rows * delta + low

    for delta in (1, -1, 2, -2):
        @pl.when(jnp.logical_not(inside(wt - delta)))
        def _(delta=delta):
            _, count, at = span(delta)
            inp[at : at + count] = jnp.zeros((count, chan, LANES), BF16)

    for load in loads[1:]:
        load.wait()
    pltpu.make_async_copy(numbers, numbers, load_sem.at[len(loads)]).wait()
    per_row = cols // TILE_COLS
    own, cell_no = owner[...], cell[...]
    target_row = target[...].astype(F32)
    table = jnp.concatenate(
        [
            (target[...] * (rows // TILE_ROWS) + own // per_row).astype(F32),
            (own % per_row).astype(F32),
            net_e[...].astype(F32),
            weight[...],
            net_p[...].astype(F32),
            target_row,
            jnp.zeros((2, entries), F32),
        ],
        axis=0,
    )
    columns = jnp.transpose(table)
    wpin_col, net_p_col = columns[:, 3:4], columns[:, 4:5]
    strength = jnp.sum(
        jnp.where(net_p_col == table[2:3, :], wpin_col, 0.0), axis=0, keepdims=True
    )
    src_j = lax.broadcasted_iota(jnp.int32, (LANES, TILE_ROWS * LANES), 0)
    dst_j = lax.broadcasted_iota(jnp.int32, (LANES, TILE_ROWS * LANES), 1)
    pick = src_j == (dst_j // LANES) * TILE_COLS + dst_j % TILE_COLS
    spread = jnp.dot(
        frac[...], jnp.where(pick, 1.0, 0.0).astype(BF16), preferred_element_type=F32
    )
    wide = lax.broadcasted_iota(jnp.int32, (1, TILE_ROWS * LANES), 1) % LANES
    block = (wide + ci * own_cols - margin + TILE_COLS * LANES) // TILE_COLS - LANES
    fmask[...] = jnp.where(columns[:, 1:2] == block.astype(F32), spread, 0.0).astype(BF16)
    blocks = height // TILE_ROWS
    block_row = lax.broadcasted_iota(jnp.int32, (blocks, entries), 0).astype(F32)
    placed = jnp.where(block_row == table[0:1, :], strength, 0.0)
    left = jnp.concatenate(split(placed, 2), axis=0)
    partial = jnp.dot(left, fmask[...], preferred_element_type=F32)
    partial = partial[:blocks] + partial[blocks:]
    for i in range(TILE_ROWS):
        dbuf[pl.ds(i, blocks, stride=TILE_ROWS), :] = partial[:, i * LANES : (i + 1) * LANES]
    dsend[...] = dbuf[...].astype(BF16)

    lift_row = lift[...]
    lift_col = jnp.transpose(jnp.broadcast_to(lift_row, (LANES, chan)))
    for u in range(3):
        for v in range(3):
            at_v, at_u = slice(v * chan, (v + 1) * chan), slice(u * chan, (u + 1) * chan)
            wm1[at_v, at_u] = jnp.transpose(w4[u, v].astype(F32)).astype(BF16)
            wm2[at_v, at_u] = jnp.transpose(w8[u, v].astype(F32)).astype(BF16)
            wm3[at_v, at_u] = w8[2 - u, 2 - v]
    taps = []
    for v in range(3):
        taps.append(
            jnp.concatenate(
                [
                    jnp.sum(
                        w4[2 - u, 2 - v].astype(F32) * lift_col[:, :chan], axis=0, keepdims=True
                    )
                    for u in range(3)
                ],
                axis=1,
            )
        )
    tap_rows = jnp.concatenate(taps + [jnp.zeros((5, 3 * chan), F32)], axis=0)
    hi, mid, low_part = [p.astype(F32) for p in split(tap_rows, 3)]
    wm4[...] = jnp.concatenate(
        [hi, mid, low_part, jnp.zeros((8, 3 * chan), F32)], axis=0
    ).astype(BF16)

    def feat_copy(turn, q, mine=False):
        h = ti % 2 if q == 0 else 1 - ti % 2
        to = wrap(ci + turn, chans)
        src = win.at[to, pl.ds(h * half, half)]
        dst = gath.at[
            pl.ds(h * half, half), pl.ds(pl.multiple_of(ci * chan_own, chan_own), chan_own)
        ]
        if mine:
            return pltpu.make_async_copy(src, dst, frecv_sem.at[q])
        return pltpu.make_async_remote_copy(
            src_ref=src, dst_ref=dst,
            send_sem=send_sem.at[FEAT], recv_sem=frecv_sem.at[q],
            device_id=at_work(ti, to), device_id_type=MESH,
        )

    def came(dst, sem, n):
        return pltpu.make_async_remote_copy(
            src_ref=dst, dst_ref=dst, send_sem=send_sem.at[n], recv_sem=sem,
            device_id=(ti, wrap(ci + 1, chans)), device_id_type=MESH,
        )

    def unless_mine(fn):
        @pl.when(jnp.logical_not(alike))
        def _():
            fn(False)

        @pl.when(alike)
        def _():
            fn(True)

    def feat_send(turn, q):
        if turn:
            feat_copy(turn, q).start()
        else:
            unless_mine(lambda mine: feat_copy(0, q, mine).start())

    def feat_wait(q):
        h = par if q == 0 else 1 - par
        came(gath.at[pl.ds(h * half, half)], frecv_sem.at[q], FEAT).wait_recv()

    def demand_copy(step, mine=False):
        to = wrap(ti + step, tiles)
        src = dsend.at[pl.ds(pl.multiple_of(to * rows, rows), rows)]
        if mine:
            return pltpu.make_async_copy(src, drecv.at[step], drecv_sem)
        return pltpu.make_async_remote_copy(
            src_ref=src, dst_ref=drecv.at[step],
            send_sem=send_sem.at[DEMAND], recv_sem=drecv_sem,
            device_id=at_work(to, ci), device_id_type=MESH,
        )

    def entry_copy(step, mine=False):
        to = wrap(ti + step, tiles)
        if mine:
            return pltpu.make_async_copy(esend.at[to], erecv.at[ti], erecv_sem)
        return pltpu.make_async_remote_copy(
            src_ref=esend.at[to], dst_ref=erecv.at[ti],
            send_sem=send_sem.at[ENTRY], recv_sem=erecv_sem,
            device_id=at_work(to, ci), device_id_type=MESH,
        )

    pl.semaphore_wait(barrier, others)
    each(1, tiles, lambda s: demand_copy(s).start())
    unless_mine(lambda mine: demand_copy(0, mine).start())
    for q in range(2):
        for turn in range(chans - 1, -1, -1):
            feat_send(turn, q)

    before = lax.broadcasted_iota(jnp.int32, (entries, entries), 0) < lax.broadcasted_iota(
        jnp.int32, (entries, entries), 1
    )
    rank = jnp.sum(
        jnp.where((columns[:, 5:6] == target_row) & before, 1.0, 0.0), axis=0, keepdims=True
    )
    key = target_row * float(cap) + rank
    pin_rows = [
        row[:, n * LANES : (n + 1) * LANES]
        for row in (table[4:5, :], (cell_no // PART).astype(F32), (cell_no % PART).astype(F32))
        for n in range(pins // LANES)
    ]
    fixed = jnp.concatenate(
        [jnp.zeros((2, LANES), F32)] + pin_rows
        + [jnp.zeros((META - 2 - len(pin_rows), LANES), F32)],
        axis=0,
    )
    loose = jnp.concatenate(
        [table[2:3, :], own.astype(F32), jnp.zeros((META - 2, entries), F32)], axis=0
    ).astype(BF16)
    slot = lax.broadcasted_iota(jnp.int32, (cap, entries), 0).astype(F32)
    wide_slot = lax.broadcasted_iota(jnp.int32, (LANES, entries), 0) - (ti % per) * cap
    wide_slot = jnp.where(
        (wide_slot >= 0) & (wide_slot < cap), wide_slot, -(cap * tiles + 1)
    ).astype(F32)

    def pack(to):
        base = jnp.asarray(to * cap, F32) if isinstance(to, int) else (to * cap).astype(F32)
        hot = jnp.where(slot + base == key, 1.0, 0.0).astype(BF16)
        esend[to, :cap] = jnp.dot(hot, frac[...], preferred_element_type=F32).astype(BF16)
        hot = jnp.where(wide_slot + base == key, 1.0, 0.0).astype(BF16)
        meta = lax.dot_general(
            loose, hot, (((1,), (1,)), ((), ())), preferred_element_type=F32
        )
        esend[to, cap:] = (meta + fixed).astype(BF16)

    each(0, tiles, pack)
    each(1, tiles, lambda s: entry_copy(s).start())
    unless_mine(lambda mine: entry_copy(0, mine).start())

    def rim(role, sending):
        if role == "A0":
            to, h = wt + near, par
        elif role == "A1":
            to, h = wt + near, 1 - par
        elif role == "B0":
            to, h = wt - near, par
        elif role == "B1":
            to, h = wt - near, 1 - par
        else:
            to, h = wt - 2 * near, 1 - par
        n = RIMS.index(role)
        if sending:
            start = HALO + h * half
            if role == "R":
                start, to = HALO + rows * near + half * (1 - par), wt - near
                at = HALO + 2 * rows * near + half * (1 - par)
                there = inside(to) & inside(wt + near)
            else:
                at = HALO + (wt - to) * rows + h * half
                there = inside(to)
            copy = pltpu.make_async_remote_copy(
                src_ref=inp.at[pl.ds(start, half)], dst_ref=inp.at[pl.ds(at, half)],
                send_sem=send_sem.at[RIM], recv_sem=hrecv_sem.at[n],
                device_id=at_work(to, wc), device_id_type=MESH,
            )
        else:
            come, at = {
                "A0": (wt + near, HALO + rows * near + half * (1 - par)),
                "A1": (wt + near, HALO + rows * near + half * par),
                "B0": (wt - near, HALO - rows * near + half * (1 - par)),
                "B1": (wt - near, HALO - rows * near + half * par),
                "F": (wt + 2 * near, HALO + 2 * rows * near + half * (1 - par)),
                "R": (wt - 2 * near, HALO - 2 * rows * near + half * par),
            }[role]
            there = inside(come)
            copy = came(inp.at[pl.ds(at, half)], hrecv_sem.at[n], RIM)
        return there, copy

    def rim_start(role):
        there, copy = rim(role, True)

        @pl.when(there)
        def _():
            copy.start()

    def rim_wait(role):
        there, copy = rim(role, False)

        @pl.when(there)
        def _():
            copy.wait_recv()

    came(drecv, drecv_sem, DEMAND).wait_recv()
    demand[...] = lax.fori_loop(
        1, tiles, lambda s, t: t + drecv[s].astype(F32), drecv[0].astype(F32)
    )

    def fill(h):
        for j in range(half):
            row = h * half + j
            add = lift_col * demand[pl.ds(row, 1), :]
            inp[HALO + row] = (gath[row].astype(F32) + add).astype(BF16)

    feat_wait(0)
    fill(par)
    rim_start("A0")
    rim_start("B0")
    feat_wait(1)
    fill(1 - par)
    rim_start("F")
    rim_start("A1")
    rim_start("B1")

    def in_map(row):
        return (row >= 0) & (row < height)

    col = lane + wc * own_cols - margin
    col_ok = ((col >= 0) & (col < cols)).astype(F32)

    def gathered(ref, at, dilation):
        return jnp.concatenate(
            [
                jnp.concatenate([ref[at + j + u * dilation] for u in range(3)], axis=0)
                for j in range(GROUP)
            ],
            axis=1,
        )

    def conv(ref, at, weights, dilation):
        result = jnp.dot(weights[...], gathered(ref, at, dilation), preferred_element_type=F32)
        parts = []
        for j in range(GROUP):
            one = result[:, j * LANES : (j + 1) * LANES]
            parts.append(
                one[chan : 2 * chan]
                + pltpu.roll(one[:chan], dilation, 1)
                + pltpu.roll(one[2 * chan :], LANES - dilation, 1)
            )
        return parts

    def keep_of(row):
        return col_ok * in_map(row).astype(F32)

    def first(at):
        keep = keep_of(top - 20 + at)
        for j, value in enumerate(conv(inp, at, wm1, 4)):
            pre[at + j] = value
            hid[at + j] = (value * jax.nn.sigmoid(value) * keep).astype(BF16)

    def second(at):
        keep = keep_of(top - 12 + at)
        for j, value in enumerate(conv(hid, at, wm2, 8)):
            sec[at + j] = (jax.nn.sigmoid(value) * keep).astype(BF16)

    def third(at):
        keep = keep_of(top - 4 + at)
        for j, value in enumerate(conv(sec, at, wm3, 8)):
            p = pre[at + j + 16]
            s = jax.nn.sigmoid(p)
            gpre[at + j] = (value * s * (1.0 + p * (1.0 - s)) * keep).astype(BF16)

    owned = ((lane >= margin) & (lane < margin + own_cols)).astype(F32)

    def fourth(at):
        result = jnp.dot(wm4[...], gathered(gpre, at, 4), preferred_element_type=F32)
        result = result[0:8] + result[8:16] + result[16:24]
        for j in range(GROUP):
            one = result[:, j * LANES : (j + 1) * LANES]
            line = (
                one[1:2]
                + pltpu.roll(one, 4, 1)[0:1]
                + pltpu.roll(one, LANES - 4, 1)[2:3]
            )
            gown[at + j : at + j + 1, :] = line * owned

    def groups(*work):
        for side in range(2):
            @pl.when(par == side)
            def _(side=side):
                for fn, count, which in work:
                    for g in which:
                        fn(count - GROUP - GROUP * g if side else GROUP * g)

    def stage(ones, twos=(), threes=(), fours=()):
        groups(
            (first, rows + 40, ones), (second, rows + 24, twos),
            (third, rows + 8, threes), (fourth, rows, fours),
        )

    per_tile = rows // TILE_ROWS
    n_tiles = tile_hot.shape[0]
    lane_of = lax.broadcasted_iota(jnp.int32, (1, LANES), 1)
    counted = lax.broadcasted_iota(jnp.int32, (PART, LANES), 0).astype(F32).astype(BF16)

    def cells_of(g):
        known = [erecv[g * per + n, cap:, :].astype(F32) for n in range(per)]
        meta = known[0]
        for k in known[1:]:
            meta = meta + k
        net_row = meta[0:1, :] + (lane_of // cap * SPREAD).astype(F32)
        mine = meta[1:2, :].astype(jnp.int32)
        across = mine % per_row - wc * (own_cols // TILE_COLS)
        which = across * per_tile + mine // per_row
        which = jnp.where((across >= 0) & (across < own_cols // TILE_COLS), which, -1)
        at_g = pl.multiple_of(g * LANES, LANES)
        tile_hot[:, pl.ds(at_g, LANES)] = jnp.where(
            lax.broadcasted_iota(jnp.int32, (n_tiles, LANES), 0) == which, 1.0, 0.0
        )
        count = pins // LANES

        def pin_row(n, at):
            return jnp.concatenate([known[n][2 + at + m : 3 + at + m, :] for m in range(count)], axis=1)

        net_pin = jnp.concatenate([pin_row(n, 0) + float(n * SPREAD) for n in range(per)], axis=1)
        cell_part = jnp.concatenate([pin_row(n, count) for n in range(per)], axis=1)
        cell_row = jnp.concatenate([pin_row(n, 2 * count) for n in range(per)], axis=1)
        net_col = jnp.transpose(jnp.broadcast_to(net_row, (8, LANES)))[:, 0:1]
        same = jnp.where(net_col == net_pin, 1.0, 0.0).astype(BF16)

        def some(q):
            at_q = pl.multiple_of(q * PART, PART)
            part = jnp.asarray(q, F32) if isinstance(q, int) else q.astype(F32)
            row = jnp.where(cell_part == part, cell_row, -1.0)
            hot = jnp.concatenate(
                [
                    jnp.where(
                        counted == row[:, n * LANES : (n + 1) * LANES].astype(BF16),
                        jnp.ones((), BF16), jnp.zeros((), BF16),
                    )
                    for n in range(row.shape[1] // LANES)
                ],
                axis=1,
            )
            to_cell[pl.ds(at_g, LANES), pl.ds(at_q, PART)] = lax.dot_general(
                same, hot, (((1,), (1,)), ((), ())), preferred_element_type=F32
            ).astype(BF16)

        loop(to_cell.shape[1] // PART, some)

    def loop(count, fn):
        if count <= 4:
            for n in range(count):
                fn(n)
        else:
            def body(n, carry):
                fn(n)
                return carry
            lax.fori_loop(0, count, body, 0)

    rim_wait("B0")
    rim_wait("B1")
    stage(range(6, 12))
    rim_wait("A0")
    rim_start("R")
    stage(range(4, 6))
    came(erecv, erecv_sem, ENTRY).wait_recv()
    loop(tiles // per, cells_of)
    rim_wait("R")
    stage(range(12, 14), range(4, 10), range(4, 6))
    rim_wait("A1")
    rim_wait("F")
    stage(range(0, 4), range(0, 4), range(0, 4), range(0, 4))

    grads = gown[...]
    right = lax.broadcasted_iota(jnp.int32, (TILE_ROWS, LANES), 0) == (
        lax.broadcasted_iota(jnp.int32, (TILE_ROWS, LANES), 1) // TILE_COLS
    )
    leaning = [
        pltpu.roll(
            grads[a * TILE_ROWS : (a + 1) * TILE_ROWS], 0, 1, stride=TILE_COLS, stride_axis=0
        )
        for a in range(per_tile)
    ]
    parts = []
    for b in range(own_cols // TILE_COLS):
        for a in range(per_tile):
            moved = pltpu.roll(leaning[a], (-margin - b * TILE_COLS) % LANES, 1)
            parts.append(jnp.sum(jnp.where(right, moved, 0.0), axis=0, keepdims=True))
    by_tile = jnp.concatenate(
        [p.astype(F32) for p in split(jnp.concatenate(parts, axis=0), 3)], axis=0
    ).astype(BF16)
    all_frac = erecv[:, :cap, :].reshape(tiles * cap, LANES)
    found = lax.dot_general(
        by_tile, all_frac, (((1,), (1,)), ((), ())), preferred_element_type=F32
    )
    found = found[:n_tiles] + found[n_tiles : 2 * n_tiles] + found[2 * n_tiles :]
    entry_grad = jnp.sum(found * tile_hot[...], axis=0, keepdims=True)
    pieces = jnp.concatenate(
        [p.astype(F32) for p in split(entry_grad, 3)] + [jnp.zeros((5, tiles * cap), F32)], axis=0
    ).astype(BF16)
    cells = jnp.dot(pieces, to_cell[...], preferred_element_type=F32)
    cells = cells[0:1] + cells[1:2] + cells[2:3]
    for u in range(csend.shape[0]):
        csend[u] = cells[:, u * LANES : (u + 1) * LANES]

    share = LANES // CELL_DEV

    def cell_copy(step, to):
        return pltpu.make_async_remote_copy(
            src_ref=csend.at[to[0] // share], dst_ref=crecv.at[step],
            send_sem=send_sem.at[CELL], recv_sem=crecv_sem,
            device_id=to, device_id_type=MESH,
        )

    each_peer(lambda n, who: cell_copy(n, who).start())

    def sent(n, ref):
        came(ref, crecv_sem, n).wait_send()

    unless_mine(lambda mine: sent(FEAT, win.at[pl.ds(0, chans - mine)]))
    unless_mine(lambda mine: sent(DEMAND, dsend.at[pl.ds(0, (tiles - mine) * rows)]))
    unless_mine(lambda mine: sent(ENTRY, esend.at[pl.ds(0, tiles - mine)]))
    ahead, behind = inside(wt + near), inside(wt - 2 * near)
    for there, count in (
        (ahead & behind, 6), (ahead & jnp.logical_not(behind), 5),
        (jnp.logical_not(ahead) & behind, 3), (jnp.logical_not(ahead | behind), 2),
    ):
        @pl.when(there)
        def _(count=count):
            sent(RIM, inp.at[pl.ds(0, count * half)])
    arrived = crecv.at[pl.ds(1, others)]
    came(arrived, crecv_sem, CELL).wait()
    total = csend[ti // share] + jnp.sum(crecv[1:], axis=0)
    for n in range(1, share):
        total = jnp.where(ti % share == n, pltpu.roll(total, LANES - n * CELL_DEV, 1), total)
    out[...] = total


def solution(mesh):
    tiles, chans = mesh.shape["tile"], mesh.shape["chan"]

    def local(
        feat, lift, w4, w8, frac, target, owner, net_e, weight, net_p, cell,
    ):
        rows, chan_own, cols = feat.shape
        chan = chan_own * chans
        entries = frac.shape[0]
        pins = weight.shape[0]
        in_rows = rows + 2 * HALO
        height = rows * tiles
        cap = -(-(2 * entries // tiles) // META) * META
        n_tiles = rows // TILE_ROWS * (cols // chans // TILE_COLS)
        vm = pltpu.VMEM
        dma = pltpu.SemaphoreType.DMA
        result = pl.pallas_call(
            functools.partial(kernel, tiles, chans),
            out_shape=pltpu.VMEM((1, LANES), F32),
            in_specs=[pl.BlockSpec(memory_space=pltpu.HBM)] * 11,
            out_specs=pl.BlockSpec(memory_space=pltpu.VMEM),
            scratch_shapes=[
                vm(feat.shape, BF16),
                vm((1, chan), F32),
                vm(w4.shape, BF16),
                vm(w8.shape, BF16),
                vm(frac.shape, BF16),
                vm((5, 1, entries), jnp.int32),
                vm((1, pins), F32),
                dma((7,)),
                vm((chans, rows, chan_own, LANES), BF16),
                vm((rows, chan, LANES), BF16),
                vm((in_rows, chan, LANES), BF16),
                vm((rows + 40, chan, LANES), F32),
                vm((rows + 40, chan, LANES), BF16),
                vm((rows + 24, chan, LANES), BF16),
                vm((rows + 8, chan, LANES), BF16),
                vm((3 * chan, 3 * chan), BF16),
                vm((3 * chan, 3 * chan), BF16),
                vm((3 * chan, 3 * chan), BF16),
                vm((32, 3 * chan), BF16),
                vm((entries, TILE_ROWS * LANES), BF16),
                vm((height, LANES), F32),
                vm((height, LANES), BF16),
                vm((tiles, rows, LANES), BF16),
                vm((rows, LANES), F32),
                vm((rows, LANES), F32),
                vm((tiles, cap + META, LANES), BF16),
                vm((tiles, cap + META, LANES), BF16),
                vm((tiles * cap, tiles * CELL_DEV), BF16),
                vm((n_tiles, tiles * cap), F32),
                vm((tiles * CELL_DEV // LANES, 1, LANES), F32),
                vm((tiles * chans, 1, LANES), F32),
                dma((5,)),
                dma((2,)),
                dma((len(RIMS),)),
                dma(()),
                dma(()),
                dma(()),
            ],
            compiler_params=pltpu.CompilerParams(collective_id=0, has_side_effects=True),
        )(
            feat, lift.reshape(1, chan), w4, w8, frac, target.reshape(1, entries),
            owner.reshape(1, entries), net_e.reshape(1, entries), weight.reshape(1, pins),
            net_p.reshape(1, pins), cell.reshape(1, pins),
        )
        return result[0, :CELL_DEV]

    in_specs = (
        P("tile", "chan", None), P(), P(), P(),
        P("tile", None), P("tile", None),
        P("tile"), P("tile"), P("tile"), P("tile"), P("tile"),
    )
    return jax.shard_map(
        local, mesh=mesh, in_specs=in_specs, out_specs=P("tile"), check_vma=False
    )
```

```python
import functools

import jax
import jax.numpy as jnp
from jax import lax
from jax.experimental import pallas as pl
from jax.experimental.pallas import tpu as pltpu
from jax.sharding import PartitionSpec as P

MESH = pl.DeviceIdType.MESH
CELL_DEV = 64
TILE_ROWS = 8
TILE_COLS = 16
LANES = 128
HALO = 24
GROUP = 4
META = 8
SPREAD = 4096
RIMS = ("A0", "B0", "F", "A1", "B1", "R")
FEAT, DEMAND, ENTRY, RIM, CELL = range(5)
PART = 256
F32 = jnp.float32
BF16 = jnp.bfloat16


def split(x, terms):
    parts = []
    for _ in range(terms):
        part = x.astype(BF16)
        parts.append(part)
        x = x - part.astype(F32)
    return parts


def kernel(
    tiles, chans,
    feat_in, lift_in, w4_in, w8_in, frac_in, target_in, owner_in, net_e_in, weight_in, net_p_in,
    cell_in,
    out,
    feat, lift, w4, w8, frac, numbers, weight, load_sem,
    win, gath, inp, pre, hid, sec, gpre, wm1, wm2, wm3, wm4,
    fmask, dbuf, dsend, drecv, demand, gown, esend, erecv, to_cell, tile_hot, csend, crecv,
    send_sem, frecv_sem, hrecv_sem, drecv_sem, erecv_sem, crecv_sem,
):
    ti = lax.axis_index("tile")
    ci = lax.axis_index("chan")
    rows, chan_own, cols = feat.shape
    chan = chan_own * chans
    own_cols = cols // chans
    margin = (LANES - own_cols) // 2
    half = rows // 2
    in_rows = rows + 2 * HALO
    others = tiles * chans - 1
    entries, pins = frac.shape[0], weight.shape[1]
    cap = esend.shape[1] - META
    per = LANES // cap
    height = rows * tiles

    par = ci % 2
    alike = ti % 2 == par
    wt = ti - ti % 2 + par
    wc = ci - par + ti % 2
    near = 2 * par - 1
    top = wt * rows

    def at_work(t, c):
        return (t - t % 2 + c % 2, c - c % 2 + t % 2)

    target, owner, net_e, net_p, cell = (numbers.at[n] for n in range(5))
    loads = [
        pltpu.make_async_copy(src, dst, load_sem.at[n])
        for n, (src, dst) in enumerate(
            [
                (feat_in, feat), (weight_in, weight), (frac_in, frac), (lift_in, lift),
                (w4_in, w4), (w8_in, w8),
            ]
        )
    ]
    for load in loads:
        load.start()
    for src, dst in (
        (target_in, target), (owner_in, owner), (net_e_in, net_e), (net_p_in, net_p),
        (cell_in, cell),
    ):
        pltpu.make_async_copy(src, dst, load_sem.at[len(loads)]).start()

    barrier = pltpu.get_barrier_semaphore()

    def wrap(number, count):
        return jnp.where(number >= count, number - count, number)

    def inside(strip):
        return (strip >= 0) & (strip < tiles)

    def each(lo, hi, fn):
        if hi - lo <= 32:
            for step in range(lo, hi):
                fn(step)
        else:
            def body(step, carry):
                fn(step)
                return carry
            lax.fori_loop(lo, hi, body, 0)

    def each_peer(fn):
        def along(back):
            hop = tiles - 1 - back
            for turn in range(chans):
                fn(hop * chans + turn, (wrap(ti + hop, tiles), wrap(ci + turn, chans)))
        each(0, tiles - 1, along)
        for turn in range(1, chans):
            fn(turn, (ti, wrap(ci + turn, chans)))

    each_peer(
        lambda n, who: pl.semaphore_signal(barrier, inc=1, device_id=who, device_id_type=MESH)
    )

    loads[0].wait()

    flat = feat[...].astype(F32).reshape(rows * chan_own, cols)
    lane = lax.broadcasted_iota(jnp.int32, (1, LANES), 1)
    for k in range(chans):
        first_col = k * own_cols - margin
        turned = pltpu.roll(flat, (-first_col) % cols, 1)[:, :LANES]
        on_map = (lane + first_col >= 0) & (lane + first_col < cols)
        win[k] = jnp.where(on_map, turned, 0.0).astype(BF16).reshape(rows, chan_own, LANES)

    def span(delta):
        low = max(0, rows * delta - HALO)
        high = min(rows, rows * delta + HALO + rows)
        return low, high - low, HALO - rows * delta + low

    for delta in (1, -1, 2, -2):
        @pl.when(jnp.logical_not(inside(wt - delta)))
        def _(delta=delta):
            _, count, at = span(delta)
            inp[at : at + count] = jnp.zeros((count, chan, LANES), BF16)

    for load in loads[1:]:
        load.wait()
    pltpu.make_async_copy(numbers, numbers, load_sem.at[len(loads)]).wait()
    per_row = cols // TILE_COLS
    own, cell_no = owner[...], cell[...]
    target_row = target[...].astype(F32)
    table = jnp.concatenate(
        [
            (target[...] * (rows // TILE_ROWS) + own // per_row).astype(F32),
            (own % per_row).astype(F32),
            net_e[...].astype(F32),
            weight[...],
            net_p[...].astype(F32),
            target_row,
            jnp.zeros((2, entries), F32),
        ],
        axis=0,
    )
    columns = jnp.transpose(table)
    wpin_col, net_p_col = columns[:, 3:4], columns[:, 4:5]
    strength = jnp.sum(
        jnp.where(net_p_col == table[2:3, :], wpin_col, 0.0), axis=0, keepdims=True
    )
    src_j = lax.broadcasted_iota(jnp.int32, (LANES, TILE_ROWS * LANES), 0)
    dst_j = lax.broadcasted_iota(jnp.int32, (LANES, TILE_ROWS * LANES), 1)
    pick = src_j == (dst_j // LANES) * TILE_COLS + dst_j % TILE_COLS
    spread = jnp.dot(
        frac[...], jnp.where(pick, 1.0, 0.0).astype(BF16), preferred_element_type=F32
    )
    wide = lax.broadcasted_iota(jnp.int32, (1, TILE_ROWS * LANES), 1) % LANES
    block = (wide + ci * own_cols - margin + TILE_COLS * LANES) // TILE_COLS - LANES
    fmask[...] = jnp.where(columns[:, 1:2] == block.astype(F32), spread, 0.0).astype(BF16)
    blocks = height // TILE_ROWS
    block_row = lax.broadcasted_iota(jnp.int32, (blocks, entries), 0).astype(F32)
    placed = jnp.where(block_row == table[0:1, :], strength, 0.0)
    left = jnp.concatenate(split(placed, 2), axis=0)
    partial = jnp.dot(left, fmask[...], preferred_element_type=F32)
    partial = partial[:blocks] + partial[blocks:]
    for i in range(TILE_ROWS):
        dbuf[pl.ds(i, blocks, stride=TILE_ROWS), :] = partial[:, i * LANES : (i + 1) * LANES]
    dsend[...] = dbuf[...].astype(BF16)

    def feat_copy(turn, q, mine=False):
        h = ti % 2 if q == 0 else 1 - ti % 2
        to = wrap(ci + turn, chans)
        src = win.at[to, pl.ds(h * half, half)]
        dst = gath.at[
            pl.ds(h * half, half), pl.ds(pl.multiple_of(ci * chan_own, chan_own), chan_own)
        ]
        if mine:
            return pltpu.make_async_copy(src, dst, frecv_sem.at[q])
        return pltpu.make_async_remote_copy(
            src_ref=src, dst_ref=dst,
            send_sem=send_sem.at[FEAT], recv_sem=frecv_sem.at[q],
            device_id=at_work(ti, to), device_id_type=MESH,
        )

    def came(dst, sem, n):
        return pltpu.make_async_remote_copy(
            src_ref=dst, dst_ref=dst, send_sem=send_sem.at[n], recv_sem=sem,
            device_id=(ti, wrap(ci + 1, chans)), device_id_type=MESH,
        )

    def unless_mine(fn):
        @pl.when(jnp.logical_not(alike))
        def _():
            fn(False)

        @pl.when(alike)
        def _():
            fn(True)

    def feat_send(turn, q):
        if turn:
            feat_copy(turn, q).start()
        else:
            unless_mine(lambda mine: feat_copy(0, q, mine).start())

    def feat_wait(q):
        h = par if q == 0 else 1 - par
        came(gath.at[pl.ds(h * half, half)], frecv_sem.at[q], FEAT).wait_recv()

    def demand_copy(step, mine=False):
        to = wrap(ti + step, tiles)
        src = dsend.at[pl.ds(pl.multiple_of(to * rows, rows), rows)]
        if mine:
            return pltpu.make_async_copy(src, drecv.at[step], drecv_sem)
        return pltpu.make_async_remote_copy(
            src_ref=src, dst_ref=drecv.at[step],
            send_sem=send_sem.at[DEMAND], recv_sem=drecv_sem,
            device_id=at_work(to, ci), device_id_type=MESH,
        )

    def entry_copy(step, mine=False):
        to = wrap(ti + step, tiles)
        if mine:
            return pltpu.make_async_copy(esend.at[to], erecv.at[ti], erecv_sem)
        return pltpu.make_async_remote_copy(
            src_ref=esend.at[to], dst_ref=erecv.at[ti],
            send_sem=send_sem.at[ENTRY], recv_sem=erecv_sem,
            device_id=at_work(to, ci), device_id_type=MESH,
        )

    pl.semaphore_wait(barrier, others)
    each(1, tiles, lambda s: demand_copy(s).start())
    unless_mine(lambda mine: demand_copy(0, mine).start())
    for q in range(2):
        for turn in range(chans - 1, -1, -1):
            feat_send(turn, q)

    lift_row = lift[...]
    lift_col = jnp.transpose(jnp.broadcast_to(lift_row, (LANES, chan)))
    for u in range(3):
        for v in range(3):
            at_v, at_u = slice(v * chan, (v + 1) * chan), slice(u * chan, (u + 1) * chan)
            wm1[at_v, at_u] = jnp.transpose(w4[u, v].astype(F32)).astype(BF16)
            wm2[at_v, at_u] = jnp.transpose(w8[u, v].astype(F32)).astype(BF16)
            wm3[at_v, at_u] = w8[2 - u, 2 - v]
    taps = []
    for v in range(3):
        taps.append(
            jnp.concatenate(
                [
                    jnp.sum(
                        w4[2 - u, 2 - v].astype(F32) * lift_col[:, :chan], axis=0, keepdims=True
                    )
                    for u in range(3)
                ],
                axis=1,
            )
        )
    tap_rows = jnp.concatenate(taps + [jnp.zeros((5, 3 * chan), F32)], axis=0)
    hi, mid, low_part = [p.astype(F32) for p in split(tap_rows, 3)]
    wm4[...] = jnp.concatenate(
        [hi, mid, low_part, jnp.zeros((8, 3 * chan), F32)], axis=0
    ).astype(BF16)

    before = lax.broadcasted_iota(jnp.int32, (entries, entries), 0) < lax.broadcasted_iota(
        jnp.int32, (entries, entries), 1
    )
    rank = jnp.sum(
        jnp.where((columns[:, 5:6] == target_row) & before, 1.0, 0.0), axis=0, keepdims=True
    )
    key = target_row * float(cap) + rank
    pin_rows = [
        row[:, n * LANES : (n + 1) * LANES]
        for row in (table[4:5, :], (cell_no // PART).astype(F32), (cell_no % PART).astype(F32))
        for n in range(pins // LANES)
    ]
    fixed = jnp.concatenate(
        [jnp.zeros((2, LANES), F32)] + pin_rows
        + [jnp.zeros((1, LANES), F32)] * (META - 2 - len(pin_rows)),
        axis=0,
    )
    loose = jnp.concatenate(
        [table[2:3, :], own.astype(F32), jnp.zeros((META - 2, entries), F32)], axis=0
    ).astype(BF16)
    slot = lax.broadcasted_iota(jnp.int32, (cap, entries), 0).astype(F32)
    wide_slot = lax.broadcasted_iota(jnp.int32, (LANES, entries), 0) - (ti % per) * cap
    wide_slot = jnp.where(
        (wide_slot >= 0) & (wide_slot < cap), wide_slot, -(cap * tiles + 1)
    ).astype(F32)

    def pack(to):
        base = jnp.asarray(to * cap, F32) if isinstance(to, int) else (to * cap).astype(F32)
        hot = jnp.where(slot + base == key, 1.0, 0.0).astype(BF16)
        esend[to, :cap] = jnp.dot(hot, frac[...], preferred_element_type=F32).astype(BF16)
        hot = jnp.where(wide_slot + base == key, 1.0, 0.0).astype(BF16)
        meta = lax.dot_general(
            loose, hot, (((1,), (1,)), ((), ())), preferred_element_type=F32
        )
        esend[to, cap:] = (meta + fixed).astype(BF16)

    each(0, tiles, pack)
    each(1, tiles, lambda s: entry_copy(s).start())
    unless_mine(lambda mine: entry_copy(0, mine).start())

    def rim(role, sending):
        if role == "A0":
            to, h = wt + near, par
        elif role == "A1":
            to, h = wt + near, 1 - par
        elif role == "B0":
            to, h = wt - near, par
        elif role == "B1":
            to, h = wt - near, 1 - par
        else:
            to, h = wt - 2 * near, 1 - par
        n = RIMS.index(role)
        if sending:
            start = HALO + h * half
            if role == "R":
                start, to = HALO + rows * near + half * (1 - par), wt - near
                at = HALO + 2 * rows * near + half * (1 - par)
                there = inside(to) & inside(wt + near)
            else:
                at = HALO + (wt - to) * rows + h * half
                there = inside(to)
            copy = pltpu.make_async_remote_copy(
                src_ref=inp.at[pl.ds(start, half)], dst_ref=inp.at[pl.ds(at, half)],
                send_sem=send_sem.at[RIM], recv_sem=hrecv_sem.at[n],
                device_id=at_work(to, wc), device_id_type=MESH,
            )
        else:
            come, at = {
                "A0": (wt + near, HALO + rows * near + half * (1 - par)),
                "A1": (wt + near, HALO + rows * near + half * par),
                "B0": (wt - near, HALO - rows * near + half * (1 - par)),
                "B1": (wt - near, HALO - rows * near + half * par),
                "F": (wt + 2 * near, HALO + 2 * rows * near + half * (1 - par)),
                "R": (wt - 2 * near, HALO - 2 * rows * near + half * par),
            }[role]
            there = inside(come)
            copy = came(inp.at[pl.ds(at, half)], hrecv_sem.at[n], RIM)
        return there, copy

    def rim_start(role):
        there, copy = rim(role, True)

        @pl.when(there)
        def _():
            copy.start()

    def rim_wait(role):
        there, copy = rim(role, False)

        @pl.when(there)
        def _():
            copy.wait_recv()

    came(drecv, drecv_sem, DEMAND).wait_recv()
    demand[...] = lax.fori_loop(
        1, tiles, lambda s, t: t + drecv[s].astype(F32), drecv[0].astype(F32)
    )

    def fill(h):
        for j in range(half):
            row = h * half + j
            add = lift_col * demand[pl.ds(row, 1), :]
            inp[HALO + row] = (gath[row].astype(F32) + add).astype(BF16)

    feat_wait(0)
    fill(par)
    rim_start("A0")
    rim_start("B0")
    feat_wait(1)
    fill(1 - par)
    rim_start("A1")
    rim_start("B1")

    def in_map(row):
        return (row >= 0) & (row < height)

    col = lane + wc * own_cols - margin
    col_ok = ((col >= 0) & (col < cols)).astype(F32)

    def gathered(ref, at, dilation):
        return jnp.concatenate(
            [
                jnp.concatenate([ref[at + j + u * dilation] for u in range(3)], axis=0)
                for j in range(GROUP)
            ],
            axis=1,
        )

    def conv(ref, at, weights, dilation):
        result = jnp.dot(weights[...], gathered(ref, at, dilation), preferred_element_type=F32)
        parts = []
        for j in range(GROUP):
            one = result[:, j * LANES : (j + 1) * LANES]
            parts.append(
                one[chan : 2 * chan]
                + pltpu.roll(one[:chan], dilation, 1)
                + pltpu.roll(one[2 * chan :], LANES - dilation, 1)
            )
        return parts

    def keep_of(row):
        return col_ok * in_map(row).astype(F32)

    def first(at):
        keep = keep_of(top - 20 + at)
        for j, value in enumerate(conv(inp, at, wm1, 4)):
            pre[at + j] = value
            hid[at + j] = (value * jax.nn.sigmoid(value) * keep).astype(BF16)

    def second(at):
        keep = keep_of(top - 12 + at)
        for j, value in enumerate(conv(hid, at, wm2, 8)):
            sec[at + j] = (jax.nn.sigmoid(value) * keep).astype(BF16)

    def third(at):
        keep = keep_of(top - 4 + at)
        for j, value in enumerate(conv(sec, at, wm3, 8)):
            p = pre[at + j + 16]
            s = jax.nn.sigmoid(p)
            gpre[at + j] = (value * s * (1.0 + p * (1.0 - s)) * keep).astype(BF16)

    owned = ((lane >= margin) & (lane < margin + own_cols)).astype(F32)

    def fourth(at):
        result = jnp.dot(wm4[...], gathered(gpre, at, 4), preferred_element_type=F32)
        result = result[0:8] + result[8:16] + result[16:24]
        for j in range(GROUP):
            one = result[:, j * LANES : (j + 1) * LANES]
            line = (
                one[1:2]
                + pltpu.roll(one, 4, 1)[0:1]
                + pltpu.roll(one, LANES - 4, 1)[2:3]
            )
            gown[at + j : at + j + 1, :] = line * owned

    def groups(*work):
        for side in range(2):
            @pl.when(par == side)
            def _(side=side):
                for fn, count, which in work:
                    for g in which:
                        fn(count - GROUP - GROUP * g if side else GROUP * g)

    def stage(ones, twos=(), threes=(), fours=()):
        groups(
            (first, rows + 40, ones), (second, rows + 24, twos),
            (third, rows + 8, threes), (fourth, rows, fours),
        )

    per_tile = rows // TILE_ROWS
    n_tiles = tile_hot.shape[0]
    lane_of = lax.broadcasted_iota(jnp.int32, (1, LANES), 1)
    counted = lax.broadcasted_iota(jnp.int32, (PART, LANES), 0).astype(F32).astype(BF16)

    def cells_of(g):
        known = [erecv[g * per + n, cap:, :].astype(F32) for n in range(per)]
        meta = known[0]
        for k in known[1:]:
            meta = meta + k
        net_row = meta[0:1, :] + (lane_of // cap * SPREAD).astype(F32)
        mine = meta[1:2, :].astype(jnp.int32)
        across = mine % per_row - wc * (own_cols // TILE_COLS)
        which = across * per_tile + mine // per_row
        which = jnp.where((across >= 0) & (across < own_cols // TILE_COLS), which, -1)
        at_g = pl.multiple_of(g * LANES, LANES)
        tile_hot[:, pl.ds(at_g, LANES)] = jnp.where(
            lax.broadcasted_iota(jnp.int32, (n_tiles, LANES), 0) == which, 1.0, 0.0
        )
        count = pins // LANES

        def pin_row(n, at):
            return jnp.concatenate([known[n][2 + at + m : 3 + at + m, :] for m in range(count)], axis=1)

        net_pin = jnp.concatenate([pin_row(n, 0) + float(n * SPREAD) for n in range(per)], axis=1)
        cell_part = jnp.concatenate([pin_row(n, count) for n in range(per)], axis=1)
        cell_row = jnp.concatenate([pin_row(n, 2 * count) for n in range(per)], axis=1)
        net_col = jnp.transpose(jnp.broadcast_to(net_row, (8, LANES)))[:, 0:1]
        same = jnp.where(net_col == net_pin, 1.0, 0.0).astype(BF16)

        def some(q):
            at_q = pl.multiple_of(q * PART, PART)
            part = jnp.asarray(q, F32) if isinstance(q, int) else q.astype(F32)
            row = jnp.where(cell_part == part, cell_row, -1.0)
            hot = jnp.concatenate(
                [
                    jnp.where(
                        counted == row[:, n * LANES : (n + 1) * LANES].astype(BF16),
                        jnp.ones((), BF16), jnp.zeros((), BF16),
                    )
                    for n in range(row.shape[1] // LANES)
                ],
                axis=1,
            )
            to_cell[pl.ds(at_g, LANES), pl.ds(at_q, PART)] = lax.dot_general(
                same, hot, (((1,), (1,)), ((), ())), preferred_element_type=F32
            ).astype(BF16)

        loop(to_cell.shape[1] // PART, some)

    def loop(count, fn):
        if count <= 4:
            for n in range(count):
                fn(n)
        else:
            def body(n, carry):
                fn(n)
                return carry
            lax.fori_loop(0, count, body, 0)

    rim_wait("B0")
    rim_wait("B1")
    rim_start("F")
    stage(range(6, 12))
    came(erecv, erecv_sem, ENTRY).wait_recv()
    loop(tiles // per, cells_of)
    rim_wait("A0")
    rim_start("R")
    stage(range(4, 6))
    rim_wait("R")
    stage(range(12, 14), range(4, 10), range(4, 6))
    rim_wait("A1")
    rim_wait("F")
    stage(range(0, 4), range(0, 4), range(0, 4), range(0, 4))

    grads = gown[...]
    right = lax.broadcasted_iota(jnp.int32, (TILE_ROWS, LANES), 0) == (
        lax.broadcasted_iota(jnp.int32, (TILE_ROWS, LANES), 1) // TILE_COLS
    )
    leaning = [
        pltpu.roll(
            grads[a * TILE_ROWS : (a + 1) * TILE_ROWS], 0, 1, stride=TILE_COLS, stride_axis=0
        )
        for a in range(per_tile)
    ]
    parts = []
    for b in range(own_cols // TILE_COLS):
        for a in range(per_tile):
            moved = pltpu.roll(leaning[a], (-margin - b * TILE_COLS) % LANES, 1)
            parts.append(jnp.sum(jnp.where(right, moved, 0.0), axis=0, keepdims=True))
    by_tile = jnp.concatenate(
        [p.astype(F32) for p in split(jnp.concatenate(parts, axis=0), 3)], axis=0
    ).astype(BF16)
    all_frac = erecv[:, :cap, :].reshape(tiles * cap, LANES)
    found = lax.dot_general(
        by_tile, all_frac, (((1,), (1,)), ((), ())), preferred_element_type=F32
    )
    found = found[:n_tiles] + found[n_tiles : 2 * n_tiles] + found[2 * n_tiles :]
    entry_grad = jnp.sum(found * tile_hot[...], axis=0, keepdims=True)
    pieces = jnp.concatenate(
        [p.astype(F32) for p in split(entry_grad, 3)] + [jnp.zeros((5, tiles * cap), F32)], axis=0
    ).astype(BF16)
    cells = jnp.dot(pieces, to_cell[...], preferred_element_type=F32)
    cells = cells[0:1] + cells[1:2] + cells[2:3]
    for u in range(csend.shape[0]):
        csend[u] = cells[:, u * LANES : (u + 1) * LANES]

    share = LANES // CELL_DEV

    def cell_copy(step, to):
        return pltpu.make_async_remote_copy(
            src_ref=csend.at[to[0] // share], dst_ref=crecv.at[step],
            send_sem=send_sem.at[CELL], recv_sem=crecv_sem,
            device_id=to, device_id_type=MESH,
        )

    each_peer(lambda n, who: cell_copy(n, who).start())

    def sent(n, ref):
        came(ref, crecv_sem, n).wait_send()

    unless_mine(lambda mine: sent(FEAT, win.at[pl.ds(0, chans - mine)]))
    unless_mine(lambda mine: sent(DEMAND, dsend.at[pl.ds(0, (tiles - mine) * rows)]))
    unless_mine(lambda mine: sent(ENTRY, esend.at[pl.ds(0, tiles - mine)]))
    ahead, behind = inside(wt + near), inside(wt - 2 * near)
    for there, count in (
        (ahead & behind, 6), (ahead & jnp.logical_not(behind), 5),
        (jnp.logical_not(ahead) & behind, 3), (jnp.logical_not(ahead | behind), 2),
    ):
        @pl.when(there)
        def _(count=count):
            sent(RIM, inp.at[pl.ds(0, count * half)])
    arrived = crecv.at[pl.ds(1, others)]
    came(arrived, crecv_sem, CELL).wait()
    total = csend[ti // share] + jnp.sum(crecv[1:], axis=0)
    for n in range(1, share):
        total = jnp.where(ti % share == n, pltpu.roll(total, LANES - n * CELL_DEV, 1), total)
    out[...] = total


def solution(mesh):
    tiles, chans = mesh.shape["tile"], mesh.shape["chan"]

    def local(
        feat, lift, w4, w8, frac, target, owner, net_e, weight, net_p, cell,
    ):
        rows, chan_own, cols = feat.shape
        chan = chan_own * chans
        entries = frac.shape[0]
        pins = weight.shape[0]
        in_rows = rows + 2 * HALO
        height = rows * tiles
        cap = -(-(2 * entries // tiles) // 16) * 16
        n_tiles = rows // TILE_ROWS * (cols // chans // TILE_COLS)
        vm = pltpu.VMEM
        dma = pltpu.SemaphoreType.DMA
        result = pl.pallas_call(
            functools.partial(kernel, tiles, chans),
            out_shape=pltpu.VMEM((1, LANES), F32),
            in_specs=[pl.BlockSpec(memory_space=pltpu.HBM)] * 11,
            out_specs=pl.BlockSpec(memory_space=pltpu.VMEM),
            scratch_shapes=[
                vm(feat.shape, BF16),
                vm((1, chan), F32),
                vm(w4.shape, BF16),
                vm(w8.shape, BF16),
                vm(frac.shape, BF16),
                vm((5, 1, entries), jnp.int32),
                vm((1, pins), F32),
                dma((7,)),
                vm((chans, rows, chan_own, LANES), BF16),
                vm((rows, chan, LANES), BF16),
                vm((in_rows, chan, LANES), BF16),
                vm((rows + 40, chan, LANES), F32),
                vm((rows + 40, chan, LANES), BF16),
                vm((rows + 24, chan, LANES), BF16),
                vm((rows + 8, chan, LANES), BF16),
                vm((3 * chan, 3 * chan), BF16),
                vm((3 * chan, 3 * chan), BF16),
                vm((3 * chan, 3 * chan), BF16),
                vm((32, 3 * chan), BF16),
                vm((entries, TILE_ROWS * LANES), BF16),
                vm((height, LANES), F32),
                vm((height, LANES), BF16),
                vm((tiles, rows, LANES), BF16),
                vm((rows, LANES), F32),
                vm((rows, LANES), F32),
                vm((tiles, cap + META, LANES), BF16),
                vm((tiles, cap + META, LANES), BF16),
                vm((tiles * cap, tiles * CELL_DEV), BF16),
                vm((n_tiles, tiles * cap), F32),
                vm((tiles * CELL_DEV // LANES, 1, LANES), F32),
                vm((tiles * chans, 1, LANES), F32),
                dma((5,)),
                dma((2,)),
                dma((len(RIMS),)),
                dma(()),
                dma(()),
                dma(()),
            ],
            compiler_params=pltpu.CompilerParams(collective_id=0, has_side_effects=True),
        )(
            feat, lift.reshape(1, chan), w4, w8, frac, target.reshape(1, entries),
            owner.reshape(1, entries), net_e.reshape(1, entries), weight.reshape(1, pins),
            net_p.reshape(1, pins), cell.reshape(1, pins),
        )
        return result[0, :CELL_DEV]

    in_specs = (
        P("tile", "chan", None), P(), P(), P(),
        P("tile", None), P("tile", None),
        P("tile"), P("tile"), P("tile"), P("tile"), P("tile"),
    )
    return jax.shard_map(
        local, mesh=mesh, in_specs=in_specs, out_specs=P("tile"), check_vma=False
    )
```

```python
import functools

import jax
import jax.numpy as jnp
from jax import lax
from jax.experimental import pallas as pl
from jax.experimental.pallas import tpu as pltpu
from jax.sharding import PartitionSpec as P

MESH = pl.DeviceIdType.MESH
CELL_DEV = 64
TILE_ROWS = 8
TILE_COLS = 16
LANES = 128
HALO = 24
GROUP = 4
META = 8
SPREAD = 4096
RIMS = ("A0", "B0", "F", "A1", "B1", "R")
FEAT, DEMAND, ENTRY, RIM, CELL = range(5)
PART = 256
PIECES = 4
F32 = jnp.float32
BF16 = jnp.bfloat16


def split(x, terms):
    parts = []
    for _ in range(terms):
        part = x.astype(BF16)
        parts.append(part)
        x = x - part.astype(F32)
    return parts


def kernel(
    tiles, chans,
    feat_in, lift_in, w4_in, w8_in, frac_in, target_in, owner_in, net_e_in, weight_in, net_p_in,
    cell_in,
    out,
    feat, lift, w4, w8, frac, numbers, weight, load_sem,
    win, gath, inp, pre, hid, sec, gpre, wm1, wm2, wm3, wm4,
    fmask, dbuf, dsend, drecv, demand, gown, esend, erecv, to_cell, tile_hot, csend, crecv,
    send_sem, frecv_sem, hrecv_sem, drecv_sem, erecv_sem, crecv_sem,
):
    ti = lax.axis_index("tile")
    ci = lax.axis_index("chan")
    rows, chan_own, cols = feat.shape
    chan = chan_own * chans
    own_cols = cols // chans
    margin = (LANES - own_cols) // 2
    half = rows // 2
    some_rows = rows // PIECES
    in_rows = rows + 2 * HALO
    others = tiles * chans - 1
    entries, pins = frac.shape[0], weight.shape[1]
    cap = esend.shape[1] - META
    per = LANES // cap
    height = rows * tiles

    par = ci % 2
    alike = ti % 2 == par
    wt = ti - ti % 2 + par
    wc = ci - par + ti % 2
    near = 2 * par - 1
    top = wt * rows

    def at_work(t, c):
        return (t - t % 2 + c % 2, c - c % 2 + t % 2)

    target, owner, net_e, net_p, cell = (numbers.at[n] for n in range(5))
    loads = [
        pltpu.make_async_copy(src, dst, load_sem.at[n])
        for n, (src, dst) in enumerate(
            [
                (feat_in, feat), (weight_in, weight), (frac_in, frac), (lift_in, lift),
                (w4_in, w4), (w8_in, w8),
            ]
        )
    ]
    for load in loads:
        load.start()
    for src, dst in (
        (target_in, target), (owner_in, owner), (net_e_in, net_e), (net_p_in, net_p),
        (cell_in, cell),
    ):
        pltpu.make_async_copy(src, dst, load_sem.at[len(loads)]).start()

    barrier = pltpu.get_barrier_semaphore()

    def wrap(number, count):
        return jnp.where(number >= count, number - count, number)

    def inside(strip):
        return (strip >= 0) & (strip < tiles)

    def each(lo, hi, fn):
        if hi - lo <= 32:
            for step in range(lo, hi):
                fn(step)
        else:
            def body(step, carry):
                fn(step)
                return carry
            lax.fori_loop(lo, hi, body, 0)

    def each_peer(fn):
        def along(back):
            hop = tiles - 1 - back
            for turn in range(chans):
                fn(hop * chans + turn, (wrap(ti + hop, tiles), wrap(ci + turn, chans)))
        each(0, tiles - 1, along)
        for turn in range(1, chans):
            fn(turn, (ti, wrap(ci + turn, chans)))

    each_peer(
        lambda n, who: pl.semaphore_signal(barrier, inc=1, device_id=who, device_id_type=MESH)
    )

    loads[0].wait()

    flat = feat[...].astype(F32).reshape(rows * chan_own, cols)
    lane = lax.broadcasted_iota(jnp.int32, (1, LANES), 1)
    for k in range(chans):
        first_col = k * own_cols - margin
        turned = pltpu.roll(flat, (-first_col) % cols, 1)[:, :LANES]
        on_map = (lane + first_col >= 0) & (lane + first_col < cols)
        win[k] = jnp.where(on_map, turned, 0.0).astype(BF16).reshape(rows, chan_own, LANES)

    def span(delta):
        low = max(0, rows * delta - HALO)
        high = min(rows, rows * delta + HALO + rows)
        return low, high - low, HALO - rows * delta + low

    for delta in (1, -1, 2, -2):
        @pl.when(jnp.logical_not(inside(wt - delta)))
        def _(delta=delta):
            _, count, at = span(delta)
            inp[at : at + count] = jnp.zeros((count, chan, LANES), BF16)

    for load in loads[1:]:
        load.wait()
    pltpu.make_async_copy(numbers, numbers, load_sem.at[len(loads)]).wait()
    per_row = cols // TILE_COLS
    own, cell_no = owner[...], cell[...]
    target_row = target[...].astype(F32)
    table = jnp.concatenate(
        [
            (target[...] * (rows // TILE_ROWS) + own // per_row).astype(F32),
            (own % per_row).astype(F32),
            net_e[...].astype(F32),
            weight[...],
            net_p[...].astype(F32),
            target_row,
            jnp.zeros((2, entries), F32),
        ],
        axis=0,
    )
    columns = jnp.transpose(table)
    wpin_col, net_p_col = columns[:, 3:4], columns[:, 4:5]
    strength = jnp.sum(
        jnp.where(net_p_col == table[2:3, :], wpin_col, 0.0), axis=0, keepdims=True
    )
    src_j = lax.broadcasted_iota(jnp.int32, (LANES, TILE_ROWS * LANES), 0)
    dst_j = lax.broadcasted_iota(jnp.int32, (LANES, TILE_ROWS * LANES), 1)
    pick = src_j == (dst_j // LANES) * TILE_COLS + dst_j % TILE_COLS
    spread = jnp.dot(
        frac[...], jnp.where(pick, 1.0, 0.0).astype(BF16), preferred_element_type=F32
    )
    wide = lax.broadcasted_iota(jnp.int32, (1, TILE_ROWS * LANES), 1) % LANES
    block = (wide + ci * own_cols - margin + TILE_COLS * LANES) // TILE_COLS - LANES
    fmask[...] = jnp.where(columns[:, 1:2] == block.astype(F32), spread, 0.0).astype(BF16)
    blocks = height // TILE_ROWS
    block_row = lax.broadcasted_iota(jnp.int32, (blocks, entries), 0).astype(F32)
    placed = jnp.where(block_row == table[0:1, :], strength, 0.0)
    left = jnp.concatenate(split(placed, 2), axis=0)
    partial = jnp.dot(left, fmask[...], preferred_element_type=F32)
    partial = partial[:blocks] + partial[blocks:]
    for i in range(TILE_ROWS):
        dbuf[pl.ds(i, blocks, stride=TILE_ROWS), :] = partial[:, i * LANES : (i + 1) * LANES]
    dsend[...] = dbuf[...].astype(BF16)

    def piece(side, q):
        return (q + side * (PIECES - 1 - 2 * q)) * some_rows

    def feat_copy(turn, q, mine=False):
        low = piece(ti % 2, q)
        to = wrap(ci + turn, chans)
        src = win.at[to, pl.ds(low, some_rows)]
        dst = gath.at[
            pl.ds(low, some_rows), pl.ds(pl.multiple_of(ci * chan_own, chan_own), chan_own)
        ]
        if mine:
            return pltpu.make_async_copy(src, dst, frecv_sem.at[q])
        return pltpu.make_async_remote_copy(
            src_ref=src, dst_ref=dst,
            send_sem=send_sem.at[FEAT], recv_sem=frecv_sem.at[q],
            device_id=at_work(ti, to), device_id_type=MESH,
        )

    def came(dst, sem, n):
        return pltpu.make_async_remote_copy(
            src_ref=dst, dst_ref=dst, send_sem=send_sem.at[n], recv_sem=sem,
            device_id=(ti, wrap(ci + 1, chans)), device_id_type=MESH,
        )

    def unless_mine(fn):
        @pl.when(jnp.logical_not(alike))
        def _():
            fn(False)

        @pl.when(alike)
        def _():
            fn(True)

    def feat_send(turn, q):
        if turn:
            feat_copy(turn, q).start()
        else:
            unless_mine(lambda mine: feat_copy(0, q, mine).start())

    def feat_wait(q):
        came(gath.at[pl.ds(piece(par, q), some_rows)], frecv_sem.at[q], FEAT).wait_recv()

    def demand_copy(step, mine=False):
        to = wrap(ti + step, tiles)
        src = dsend.at[pl.ds(pl.multiple_of(to * rows, rows), rows)]
        if mine:
            return pltpu.make_async_copy(src, drecv.at[step], drecv_sem)
        return pltpu.make_async_remote_copy(
            src_ref=src, dst_ref=drecv.at[step],
            send_sem=send_sem.at[DEMAND], recv_sem=drecv_sem,
            device_id=at_work(to, ci), device_id_type=MESH,
        )

    def entry_copy(step, mine=False):
        to = wrap(ti + step, tiles)
        if mine:
            return pltpu.make_async_copy(esend.at[to], erecv.at[ti], erecv_sem)
        return pltpu.make_async_remote_copy(
            src_ref=esend.at[to], dst_ref=erecv.at[ti],
            send_sem=send_sem.at[ENTRY], recv_sem=erecv_sem,
            device_id=at_work(to, ci), device_id_type=MESH,
        )

    pl.semaphore_wait(barrier, others)
    each(1, tiles, lambda s: demand_copy(s).start())
    unless_mine(lambda mine: demand_copy(0, mine).start())
    for q in range(PIECES):
        for turn in range(chans - 1, -1, -1):
            feat_send(turn, q)

    lift_row = lift[...]
    lift_col = jnp.transpose(jnp.broadcast_to(lift_row, (LANES, chan)))
    for u in range(3):
        for v in range(3):
            at_v, at_u = slice(v * chan, (v + 1) * chan), slice(u * chan, (u + 1) * chan)
            wm1[at_v, at_u] = jnp.transpose(w4[u, v].astype(F32)).astype(BF16)
            wm2[at_v, at_u] = jnp.transpose(w8[u, v].astype(F32)).astype(BF16)
            wm3[at_v, at_u] = w8[2 - u, 2 - v]
    taps = []
    for v in range(3):
        taps.append(
            jnp.concatenate(
                [
                    jnp.sum(
                        w4[2 - u, 2 - v].astype(F32) * lift_col[:, :chan], axis=0, keepdims=True
                    )
                    for u in range(3)
                ],
                axis=1,
            )
        )
    tap_rows = jnp.concatenate(taps + [jnp.zeros((5, 3 * chan), F32)], axis=0)
    hi, mid, low_part = [p.astype(F32) for p in split(tap_rows, 3)]
    wm4[...] = jnp.concatenate(
        [hi, mid, low_part, jnp.zeros((8, 3 * chan), F32)], axis=0
    ).astype(BF16)

    before = lax.broadcasted_iota(jnp.int32, (entries, entries), 0) < lax.broadcasted_iota(
        jnp.int32, (entries, entries), 1
    )
    rank = jnp.sum(
        jnp.where((columns[:, 5:6] == target_row) & before, 1.0, 0.0), axis=0, keepdims=True
    )
    key = target_row * float(cap) + rank
    pin_rows = [
        row[:, n * LANES : (n + 1) * LANES]
        for row in (table[4:5, :], (cell_no // PART).astype(F32), (cell_no % PART).astype(F32))
        for n in range(pins // LANES)
    ]
    fixed = jnp.concatenate(
        [jnp.zeros((2, LANES), F32)] + pin_rows
        + [jnp.zeros((1, LANES), F32)] * (META - 2 - len(pin_rows)),
        axis=0,
    )
    loose = jnp.concatenate(
        [table[2:3, :], own.astype(F32), jnp.zeros((META - 2, entries), F32)], axis=0
    ).astype(BF16)
    slot = lax.broadcasted_iota(jnp.int32, (cap, entries), 0).astype(F32)
    wide_slot = lax.broadcasted_iota(jnp.int32, (LANES, entries), 0) - (ti % per) * cap
    wide_slot = jnp.where(
        (wide_slot >= 0) & (wide_slot < cap), wide_slot, -(cap * tiles + 1)
    ).astype(F32)

    def pack(to):
        base = jnp.asarray(to * cap, F32) if isinstance(to, int) else (to * cap).astype(F32)
        hot = jnp.where(slot + base == key, 1.0, 0.0).astype(BF16)
        esend[to, :cap] = jnp.dot(hot, frac[...], preferred_element_type=F32).astype(BF16)
        hot = jnp.where(wide_slot + base == key, 1.0, 0.0).astype(BF16)
        meta = lax.dot_general(
            loose, hot, (((1,), (1,)), ((), ())), preferred_element_type=F32
        )
        esend[to, cap:] = (meta + fixed).astype(BF16)

    each(0, tiles, pack)
    each(1, tiles, lambda s: entry_copy(s).start())
    unless_mine(lambda mine: entry_copy(0, mine).start())

    def rim(role, sending):
        to, h = wt - 2 * near, 1 - par
        n = RIMS.index(role)
        if sending:
            start = HALO + h * half
            if role == "R":
                start, to = HALO + rows * near + half * (1 - par), wt - near
                at = HALO + 2 * rows * near + half * (1 - par)
                there = inside(to) & inside(wt + near)
            else:
                at = HALO + (wt - to) * rows + h * half
                there = inside(to)
            copy = pltpu.make_async_remote_copy(
                src_ref=inp.at[pl.ds(start, half)], dst_ref=inp.at[pl.ds(at, half)],
                send_sem=send_sem.at[RIM], recv_sem=hrecv_sem.at[n],
                device_id=at_work(to, wc), device_id_type=MESH,
            )
        else:
            come, at = {
                "A0": (wt + near, HALO + rows * near + half * (1 - par)),
                "A1": (wt + near, HALO + rows * near + half * par),
                "B0": (wt - near, HALO - rows * near + half * (1 - par)),
                "B1": (wt - near, HALO - rows * near + half * par),
                "F": (wt + 2 * near, HALO + 2 * rows * near + half * (1 - par)),
                "R": (wt - 2 * near, HALO - 2 * rows * near + half * par),
            }[role]
            there = inside(come)
            copy = came(inp.at[pl.ds(at, half)], hrecv_sem.at[n], RIM)
        return there, copy

    def rim_start(role):
        there, copy = rim(role, True)

        @pl.when(there)
        def _():
            copy.start()

    def rim_wait(role):
        there, copy = rim(role, False)

        @pl.when(there)
        def _():
            copy.wait_recv()

    came(drecv, drecv_sem, DEMAND).wait_recv()
    demand[...] = lax.fori_loop(
        1, tiles, lambda s, t: t + drecv[s].astype(F32), drecv[0].astype(F32)
    )

    def fill(q):
        for j in range(some_rows):
            row = piece(par, q) + j
            add = lift_col * demand[pl.ds(row, 1), :]
            inp[HALO + row] = (gath[row].astype(F32) + add).astype(BF16)

    def near_start(q):
        low = piece(par, q)
        n = 2 * q // PIECES
        for role, to in (("A", wt + near), ("B", wt - near)):
            @pl.when(inside(to))
            def _(role=role, to=to):
                pltpu.make_async_remote_copy(
                    src_ref=inp.at[pl.ds(HALO + low, some_rows)],
                    dst_ref=inp.at[pl.ds(HALO + (wt - to) * rows + low, some_rows)],
                    send_sem=send_sem.at[RIM], recv_sem=hrecv_sem.at[RIMS.index(role + str(n))],
                    device_id=at_work(to, wc), device_id_type=MESH,
                ).start()

    for q in range(PIECES):
        feat_wait(q)
        fill(q)
        near_start(q)

    def in_map(row):
        return (row >= 0) & (row < height)

    col = lane + wc * own_cols - margin
    col_ok = ((col >= 0) & (col < cols)).astype(F32)

    def gathered(ref, at, dilation):
        return jnp.concatenate(
            [
                jnp.concatenate([ref[at + j + u * dilation] for u in range(3)], axis=0)
                for j in range(GROUP)
            ],
            axis=1,
        )

    def conv(ref, at, weights, dilation):
        result = jnp.dot(weights[...], gathered(ref, at, dilation), preferred_element_type=F32)
        parts = []
        for j in range(GROUP):
            one = result[:, j * LANES : (j + 1) * LANES]
            parts.append(
                one[chan : 2 * chan]
                + pltpu.roll(one[:chan], dilation, 1)
                + pltpu.roll(one[2 * chan :], LANES - dilation, 1)
            )
        return parts

    def keep_of(row):
        return col_ok * in_map(row).astype(F32)

    def first(at):
        keep = keep_of(top - 20 + at)
        for j, value in enumerate(conv(inp, at, wm1, 4)):
            pre[at + j] = value
            hid[at + j] = (value * jax.nn.sigmoid(value) * keep).astype(BF16)

    def second(at):
        keep = keep_of(top - 12 + at)
        for j, value in enumerate(conv(hid, at, wm2, 8)):
            sec[at + j] = (jax.nn.sigmoid(value) * keep).astype(BF16)

    def third(at):
        keep = keep_of(top - 4 + at)
        for j, value in enumerate(conv(sec, at, wm3, 8)):
            p = pre[at + j + 16]
            s = jax.nn.sigmoid(p)
            gpre[at + j] = (value * s * (1.0 + p * (1.0 - s)) * keep).astype(BF16)

    owned = ((lane >= margin) & (lane < margin + own_cols)).astype(F32)

    def fourth(at):
        result = jnp.dot(wm4[...], gathered(gpre, at, 4), preferred_element_type=F32)
        result = result[0:8] + result[8:16] + result[16:24]
        for j in range(GROUP):
            one = result[:, j * LANES : (j + 1) * LANES]
            line = (
                one[1:2]
                + pltpu.roll(one, 4, 1)[0:1]
                + pltpu.roll(one, LANES - 4, 1)[2:3]
            )
            gown[at + j : at + j + 1, :] = line * owned

    def groups(*work):
        for side in range(2):
            @pl.when(par == side)
            def _(side=side):
                for fn, count, which in work:
                    for g in which:
                        fn(count - GROUP - GROUP * g if side else GROUP * g)

    def stage(ones, twos=(), threes=(), fours=()):
        groups(
            (first, rows + 40, ones), (second, rows + 24, twos),
            (third, rows + 8, threes), (fourth, rows, fours),
        )

    per_tile = rows // TILE_ROWS
    n_tiles = tile_hot.shape[0]
    lane_of = lax.broadcasted_iota(jnp.int32, (1, LANES), 1)
    counted = lax.broadcasted_iota(jnp.int32, (PART, LANES), 0).astype(F32).astype(BF16)

    def cells_of(g):
        known = [erecv[g * per + n, cap:, :].astype(F32) for n in range(per)]
        meta = known[0]
        for k in known[1:]:
            meta = meta + k
        net_row = meta[0:1, :] + (lane_of // cap * SPREAD).astype(F32)
        mine = meta[1:2, :].astype(jnp.int32)
        across = mine % per_row - wc * (own_cols // TILE_COLS)
        which = across * per_tile + mine // per_row
        which = jnp.where((across >= 0) & (across < own_cols // TILE_COLS), which, -1)
        at_g = pl.multiple_of(g * LANES, LANES)
        tile_hot[:, pl.ds(at_g, LANES)] = jnp.where(
            lax.broadcasted_iota(jnp.int32, (n_tiles, LANES), 0) == which, 1.0, 0.0
        )
        count = pins // LANES

        def pin_row(n, at):
            return jnp.concatenate([known[n][2 + at + m : 3 + at + m, :] for m in range(count)], axis=1)

        net_pin = jnp.concatenate([pin_row(n, 0) + float(n * SPREAD) for n in range(per)], axis=1)
        cell_part = jnp.concatenate([pin_row(n, count) for n in range(per)], axis=1)
        cell_row = jnp.concatenate([pin_row(n, 2 * count) for n in range(per)], axis=1)
        net_col = jnp.transpose(jnp.broadcast_to(net_row, (8, LANES)))[:, 0:1]
        same = jnp.where(net_col == net_pin, 1.0, 0.0).astype(BF16)

        def some(q):
            at_q = pl.multiple_of(q * PART, PART)
            part = jnp.asarray(q, F32) if isinstance(q, int) else q.astype(F32)
            row = jnp.where(cell_part == part, cell_row, -1.0)
            hot = jnp.concatenate(
                [
                    jnp.where(
                        counted == row[:, n * LANES : (n + 1) * LANES].astype(BF16),
                        jnp.ones((), BF16), jnp.zeros((), BF16),
                    )
                    for n in range(row.shape[1] // LANES)
                ],
                axis=1,
            )
            to_cell[pl.ds(at_g, LANES), pl.ds(at_q, PART)] = lax.dot_general(
                same, hot, (((1,), (1,)), ((), ())), preferred_element_type=F32
            ).astype(BF16)

        loop(to_cell.shape[1] // PART, some)

    def loop(count, fn):
        if count <= 4:
            for n in range(count):
                fn(n)
        else:
            def body(n, carry):
                fn(n)
                return carry
            lax.fori_loop(0, count, body, 0)


    @pl.when(alike)
    def _():
        came(erecv, erecv_sem, ENTRY).wait_recv()
        loop(tiles // per, cells_of)

    rim_wait("B0")
    rim_wait("B1")
    rim_start("F")
    stage(range(6, 12))

    @pl.when(jnp.logical_not(alike))
    def _():
        came(erecv, erecv_sem, ENTRY).wait_recv()
        loop(tiles // per, cells_of)

    rim_wait("A0")
    rim_start("R")
    stage(range(4, 6), range(4, 8))
    rim_wait("R")
    stage(range(12, 14), range(8, 10), range(4, 6))
    rim_wait("A1")
    rim_wait("F")
    stage(range(0, 4), range(0, 4), range(0, 4), range(0, 4))

    grads = gown[...]
    right = lax.broadcasted_iota(jnp.int32, (TILE_ROWS, LANES), 0) == (
        lax.broadcasted_iota(jnp.int32, (TILE_ROWS, LANES), 1) // TILE_COLS
    )
    leaning = [
        pltpu.roll(
            grads[a * TILE_ROWS : (a + 1) * TILE_ROWS], 0, 1, stride=TILE_COLS, stride_axis=0
        )
        for a in range(per_tile)
    ]
    parts = []
    for b in range(own_cols // TILE_COLS):
        for a in range(per_tile):
            moved = pltpu.roll(leaning[a], (-margin - b * TILE_COLS) % LANES, 1)
            parts.append(jnp.sum(jnp.where(right, moved, 0.0), axis=0, keepdims=True))
    by_tile = jnp.concatenate(
        [p.astype(F32) for p in split(jnp.concatenate(parts, axis=0), 3)], axis=0
    ).astype(BF16)
    all_frac = erecv[:, :cap, :].reshape(tiles * cap, LANES)
    found = lax.dot_general(
        by_tile, all_frac, (((1,), (1,)), ((), ())), preferred_element_type=F32
    )
    found = found[:n_tiles] + found[n_tiles : 2 * n_tiles] + found[2 * n_tiles :]
    entry_grad = jnp.sum(found * tile_hot[...], axis=0, keepdims=True)
    pieces = jnp.concatenate(
        [p.astype(F32) for p in split(entry_grad, 3)] + [jnp.zeros((5, tiles * cap), F32)], axis=0
    ).astype(BF16)
    cells = jnp.dot(pieces, to_cell[...], preferred_element_type=F32)
    cells = cells[0:1] + cells[1:2] + cells[2:3]
    for u in range(csend.shape[0]):
        csend[u] = cells[:, u * LANES : (u + 1) * LANES]

    share = LANES // CELL_DEV

    def cell_copy(step, to):
        return pltpu.make_async_remote_copy(
            src_ref=csend.at[to[0] // share], dst_ref=crecv.at[step],
            send_sem=send_sem.at[CELL], recv_sem=crecv_sem,
            device_id=to, device_id_type=MESH,
        )

    each_peer(lambda n, who: cell_copy(n, who).start())

    def sent(n, ref):
        came(ref, crecv_sem, n).wait_send()

    unless_mine(lambda mine: sent(FEAT, win.at[pl.ds(0, chans - mine)]))
    unless_mine(lambda mine: sent(DEMAND, dsend.at[pl.ds(0, (tiles - mine) * rows)]))
    unless_mine(lambda mine: sent(ENTRY, esend.at[pl.ds(0, tiles - mine)]))
    ahead, behind = inside(wt + near), inside(wt - 2 * near)
    for there, count in (
        (ahead & behind, 6), (ahead & jnp.logical_not(behind), 5),
        (jnp.logical_not(ahead) & behind, 3), (jnp.logical_not(ahead | behind), 2),
    ):
        @pl.when(there)
        def _(count=count):
            sent(RIM, inp.at[pl.ds(0, count * half)])
    arrived = crecv.at[pl.ds(1, others)]
    came(arrived, crecv_sem, CELL).wait()
    total = csend[ti // share] + jnp.sum(crecv[1:], axis=0)
    for n in range(1, share):
        total = jnp.where(ti % share == n, pltpu.roll(total, LANES - n * CELL_DEV, 1), total)
    out[...] = total


def solution(mesh):
    tiles, chans = mesh.shape["tile"], mesh.shape["chan"]

    def local(
        feat, lift, w4, w8, frac, target, owner, net_e, weight, net_p, cell,
    ):
        rows, chan_own, cols = feat.shape
        chan = chan_own * chans
        entries = frac.shape[0]
        pins = weight.shape[0]
        in_rows = rows + 2 * HALO
        height = rows * tiles
        cap = -(-(2 * entries // tiles) // 16) * 16
        n_tiles = rows // TILE_ROWS * (cols // chans // TILE_COLS)
        vm = pltpu.VMEM
        dma = pltpu.SemaphoreType.DMA
        result = pl.pallas_call(
            functools.partial(kernel, tiles, chans),
            out_shape=pltpu.VMEM((1, LANES), F32),
            in_specs=[pl.BlockSpec(memory_space=pltpu.HBM)] * 11,
            out_specs=pl.BlockSpec(memory_space=pltpu.VMEM),
            scratch_shapes=[
                vm(feat.shape, BF16),
                vm((1, chan), F32),
                vm(w4.shape, BF16),
                vm(w8.shape, BF16),
                vm(frac.shape, BF16),
                vm((5, 1, entries), jnp.int32),
                vm((1, pins), F32),
                dma((7,)),
                vm((chans, rows, chan_own, LANES), BF16),
                vm((rows, chan, LANES), BF16),
                vm((in_rows, chan, LANES), BF16),
                vm((rows + 40, chan, LANES), F32),
                vm((rows + 40, chan, LANES), BF16),
                vm((rows + 24, chan, LANES), BF16),
                vm((rows + 8, chan, LANES), BF16),
                vm((3 * chan, 3 * chan), BF16),
                vm((3 * chan, 3 * chan), BF16),
                vm((3 * chan, 3 * chan), BF16),
                vm((32, 3 * chan), BF16),
                vm((entries, TILE_ROWS * LANES), BF16),
                vm((height, LANES), F32),
                vm((height, LANES), BF16),
                vm((tiles, rows, LANES), BF16),
                vm((rows, LANES), F32),
                vm((rows, LANES), F32),
                vm((tiles, cap + META, LANES), BF16),
                vm((tiles, cap + META, LANES), BF16),
                vm((tiles * cap, tiles * CELL_DEV), BF16),
                vm((n_tiles, tiles * cap), F32),
                vm((tiles * CELL_DEV // LANES, 1, LANES), F32),
                vm((tiles * chans, 1, LANES), F32),
                dma((5,)),
                dma((PIECES,)),
                dma((len(RIMS),)),
                dma(()),
                dma(()),
                dma(()),
            ],
            compiler_params=pltpu.CompilerParams(collective_id=0, has_side_effects=True),
        )(
            feat, lift.reshape(1, chan), w4, w8, frac, target.reshape(1, entries),
            owner.reshape(1, entries), net_e.reshape(1, entries), weight.reshape(1, pins),
            net_p.reshape(1, pins), cell.reshape(1, pins),
        )
        return result[0, :CELL_DEV]

    in_specs = (
        P("tile", "chan", None), P(), P(), P(),
        P("tile", None), P("tile", None),
        P("tile"), P("tile"), P("tile"), P("tile"), P("tile"),
    )
    return jax.shard_map(
        local, mesh=mesh, in_specs=in_specs, out_specs=P("tile"), check_vma=False
    )
```

```python
import functools

import jax
import jax.numpy as jnp
from jax import lax
from jax.experimental import pallas as pl
from jax.experimental.pallas import tpu as pltpu
from jax.sharding import PartitionSpec as P

MESH = pl.DeviceIdType.MESH
CELL_DEV = 64
TILE_ROWS = 8
TILE_COLS = 16
LANES = 128
HALO = 24
GROUP = 4
META = 8
SPREAD = 4096
RIMS = ("A0", "B0", "F", "A1", "B1", "R")
FEAT, DEMAND, ENTRY, RIM, CELL = range(5)
PART = 256
PIECES = 4
F32 = jnp.float32
BF16 = jnp.bfloat16


def split(x, terms):
    parts = []
    for _ in range(terms):
        part = x.astype(BF16)
        parts.append(part)
        x = x - part.astype(F32)
    return parts


def kernel(
    tiles, chans,
    feat_in, lift_in, w4_in, w8_in, frac_in, target_in, owner_in, net_e_in, weight_in, net_p_in,
    cell_in,
    out,
    feat, lift, w4, w8, frac, numbers, weight, load_sem,
    win, gath, inp, pre, hid, sec, gpre, wm1, wm2, wm3, wm4,
    fmask, dbuf, dsend, drecv, demand, gown, esend, erecv, to_cell, tile_hot, csend, crecv,
    send_sem, frecv_sem, hrecv_sem, drecv_sem, erecv_sem, crecv_sem,
):
    ti = lax.axis_index("tile")
    ci = lax.axis_index("chan")
    rows, chan_own, cols = feat.shape
    chan = chan_own * chans
    own_cols = cols // chans
    margin = (LANES - own_cols) // 2
    half = rows // 2
    some_rows = rows // PIECES
    in_rows = rows + 2 * HALO
    others = tiles * chans - 1
    entries, pins = frac.shape[0], weight.shape[1]
    cap = esend.shape[1] - META
    per = LANES // cap
    height = rows * tiles

    par = ci % 2
    alike = ti % 2 == par
    wt = ti - ti % 2 + par
    wc = ci - par + ti % 2
    near = 2 * par - 1
    top = wt * rows

    def at_work(t, c):
        return (t - t % 2 + c % 2, c - c % 2 + t % 2)

    target, owner, net_e, net_p, cell = (numbers.at[n] for n in range(5))
    loads = [
        pltpu.make_async_copy(src, dst, load_sem.at[n])
        for n, (src, dst) in enumerate(
            [
                (feat_in, feat), (weight_in, weight), (frac_in, frac), (lift_in, lift),
                (w4_in, w4), (w8_in, w8),
            ]
        )
    ]
    for load in loads:
        load.start()
    for src, dst in (
        (target_in, target), (owner_in, owner), (net_e_in, net_e), (net_p_in, net_p),
        (cell_in, cell),
    ):
        pltpu.make_async_copy(src, dst, load_sem.at[len(loads)]).start()

    barrier = pltpu.get_barrier_semaphore()

    def wrap(number, count):
        return jnp.where(number >= count, number - count, number)

    def inside(strip):
        return (strip >= 0) & (strip < tiles)

    def each(lo, hi, fn):
        if hi - lo <= 32:
            for step in range(lo, hi):
                fn(step)
        else:
            def body(step, carry):
                fn(step)
                return carry
            lax.fori_loop(lo, hi, body, 0)

    def each_peer(fn):
        def along(hop):
            for turn in range(chans):
                fn(hop * chans + turn, (wrap(ti + hop, tiles), wrap(ci + turn, chans)))
        each(1, tiles, along)
        for turn in range(1, chans):
            fn(turn, (ti, wrap(ci + turn, chans)))

    each_peer(
        lambda n, who: pl.semaphore_signal(barrier, inc=1, device_id=who, device_id_type=MESH)
    )

    loads[0].wait()

    flat = feat[...].astype(F32).reshape(rows * chan_own, cols)
    lane = lax.broadcasted_iota(jnp.int32, (1, LANES), 1)
    for k in range(chans):
        first_col = k * own_cols - margin
        turned = pltpu.roll(flat, (-first_col) % cols, 1)[:, :LANES]
        on_map = (lane + first_col >= 0) & (lane + first_col < cols)
        win[k] = jnp.where(on_map, turned, 0.0).astype(BF16).reshape(rows, chan_own, LANES)

    def span(delta):
        low = max(0, rows * delta - HALO)
        high = min(rows, rows * delta + HALO + rows)
        return low, high - low, HALO - rows * delta + low

    for delta in (1, -1, 2, -2):
        @pl.when(jnp.logical_not(inside(wt - delta)))
        def _(delta=delta):
            _, count, at = span(delta)
            inp[at : at + count] = jnp.zeros((count, chan, LANES), BF16)

    for load in loads[1:]:
        load.wait()
    pltpu.make_async_copy(numbers, numbers, load_sem.at[len(loads)]).wait()
    per_row = cols // TILE_COLS
    own, cell_no = owner[...], cell[...]
    target_row = target[...].astype(F32)
    table = jnp.concatenate(
        [
            (target[...] * (rows // TILE_ROWS) + own // per_row).astype(F32),
            (own % per_row).astype(F32),
            net_e[...].astype(F32),
            weight[...],
            net_p[...].astype(F32),
            target_row,
            jnp.zeros((2, entries), F32),
        ],
        axis=0,
    )
    columns = jnp.transpose(table)
    wpin_col, net_p_col = columns[:, 3:4], columns[:, 4:5]
    strength = jnp.sum(
        jnp.where(net_p_col == table[2:3, :], wpin_col, 0.0), axis=0, keepdims=True
    )
    src_j = lax.broadcasted_iota(jnp.int32, (LANES, TILE_ROWS * LANES), 0)
    dst_j = lax.broadcasted_iota(jnp.int32, (LANES, TILE_ROWS * LANES), 1)
    pick = src_j == (dst_j // LANES) * TILE_COLS + dst_j % TILE_COLS
    spread = jnp.dot(
        frac[...], jnp.where(pick, 1.0, 0.0).astype(BF16), preferred_element_type=F32
    )
    wide = lax.broadcasted_iota(jnp.int32, (1, TILE_ROWS * LANES), 1) % LANES
    block = (wide + ci * own_cols - margin + TILE_COLS * LANES) // TILE_COLS - LANES
    fmask[...] = jnp.where(columns[:, 1:2] == block.astype(F32), spread, 0.0).astype(BF16)
    blocks = height // TILE_ROWS
    block_row = lax.broadcasted_iota(jnp.int32, (blocks, entries), 0).astype(F32)
    placed = jnp.where(block_row == table[0:1, :], strength, 0.0)
    left = jnp.concatenate(split(placed, 2), axis=0)
    partial = jnp.dot(left, fmask[...], preferred_element_type=F32)
    partial = partial[:blocks] + partial[blocks:]
    for i in range(TILE_ROWS):
        dbuf[pl.ds(i, blocks, stride=TILE_ROWS), :] = partial[:, i * LANES : (i + 1) * LANES]
    dsend[...] = dbuf[...].astype(BF16)

    def piece(side, q):
        return (q + side * (PIECES - 1 - 2 * q)) * some_rows

    def feat_copy(turn, q, mine=False):
        low = piece(ti % 2, q)
        to = wrap(ci + turn, chans)
        src = win.at[to, pl.ds(low, some_rows)]
        dst = gath.at[
            pl.ds(low, some_rows), pl.ds(pl.multiple_of(ci * chan_own, chan_own), chan_own)
        ]
        if mine:
            return pltpu.make_async_copy(src, dst, frecv_sem.at[q])
        return pltpu.make_async_remote_copy(
            src_ref=src, dst_ref=dst,
            send_sem=send_sem.at[FEAT], recv_sem=frecv_sem.at[q],
            device_id=at_work(ti, to), device_id_type=MESH,
        )

    def came(dst, sem, n):
        return pltpu.make_async_remote_copy(
            src_ref=dst, dst_ref=dst, send_sem=send_sem.at[n], recv_sem=sem,
            device_id=(ti, wrap(ci + 1, chans)), device_id_type=MESH,
        )

    def unless_mine(fn):
        @pl.when(jnp.logical_not(alike))
        def _():
            fn(False)

        @pl.when(alike)
        def _():
            fn(True)

    def feat_send(turn, q):
        if turn:
            feat_copy(turn, q).start()
        else:
            unless_mine(lambda mine: feat_copy(0, q, mine).start())

    def feat_wait(q):
        came(gath.at[pl.ds(piece(par, q), some_rows)], frecv_sem.at[q], FEAT).wait_recv()

    def demand_copy(step, mine=False):
        to = wrap(ti + step, tiles)
        src = dsend.at[pl.ds(pl.multiple_of(to * rows, rows), rows)]
        if mine:
            return pltpu.make_async_copy(src, drecv.at[step], drecv_sem)
        return pltpu.make_async_remote_copy(
            src_ref=src, dst_ref=drecv.at[step],
            send_sem=send_sem.at[DEMAND], recv_sem=drecv_sem,
            device_id=at_work(to, ci), device_id_type=MESH,
        )

    def entry_copy(step, mine=False):
        to = wrap(ti + step, tiles)
        if mine:
            return pltpu.make_async_copy(esend.at[to], erecv.at[ti], erecv_sem)
        return pltpu.make_async_remote_copy(
            src_ref=esend.at[to], dst_ref=erecv.at[ti],
            send_sem=send_sem.at[ENTRY], recv_sem=erecv_sem,
            device_id=at_work(to, ci), device_id_type=MESH,
        )

    pl.semaphore_wait(barrier, others)
    each(1, tiles, lambda s: demand_copy(s).start())
    unless_mine(lambda mine: demand_copy(0, mine).start())
    for q in range(PIECES):
        for turn in range(chans - 1, -1, -1):
            feat_send(turn, q)

    lift_row = lift[...]
    lift_col = jnp.transpose(jnp.broadcast_to(lift_row, (LANES, chan)))
    for u in range(3):
        for v in range(3):
            at_v, at_u = slice(v * chan, (v + 1) * chan), slice(u * chan, (u + 1) * chan)
            wm1[at_v, at_u] = jnp.transpose(w4[u, v].astype(F32)).astype(BF16)
            wm2[at_v, at_u] = jnp.transpose(w8[u, v].astype(F32)).astype(BF16)
            wm3[at_v, at_u] = w8[2 - u, 2 - v]
    taps = []
    for v in range(3):
        taps.append(
            jnp.concatenate(
                [
                    jnp.sum(
                        w4[2 - u, 2 - v].astype(F32) * lift_col[:, :chan], axis=0, keepdims=True
                    )
                    for u in range(3)
                ],
                axis=1,
            )
        )
    tap_rows = jnp.concatenate(taps + [jnp.zeros((5, 3 * chan), F32)], axis=0)
    hi, mid, low_part = [p.astype(F32) for p in split(tap_rows, 3)]
    wm4[...] = jnp.concatenate(
        [hi, mid, low_part, jnp.zeros((8, 3 * chan), F32)], axis=0
    ).astype(BF16)

    before = lax.broadcasted_iota(jnp.int32, (entries, entries), 0) < lax.broadcasted_iota(
        jnp.int32, (entries, entries), 1
    )
    rank = jnp.sum(
        jnp.where((columns[:, 5:6] == target_row) & before, 1.0, 0.0), axis=0, keepdims=True
    )
    key = target_row * float(cap) + rank
    pin_rows = [
        row[:, n * LANES : (n + 1) * LANES]
        for row in (table[4:5, :], (cell_no // PART).astype(F32), (cell_no % PART).astype(F32))
        for n in range(pins // LANES)
    ]
    fixed = jnp.concatenate(
        [jnp.zeros((2, LANES), F32)] + pin_rows
        + [jnp.zeros((1, LANES), F32)] * (META - 2 - len(pin_rows)),
        axis=0,
    )
    loose = jnp.concatenate(
        [table[2:3, :], own.astype(F32), jnp.zeros((META - 2, entries), F32)], axis=0
    ).astype(BF16)
    slot = lax.broadcasted_iota(jnp.int32, (cap, entries), 0).astype(F32)
    wide_slot = lax.broadcasted_iota(jnp.int32, (LANES, entries), 0) - (ti % per) * cap
    wide_slot = jnp.where(
        (wide_slot >= 0) & (wide_slot < cap), wide_slot, -(cap * tiles + 1)
    ).astype(F32)

    def pack(to):
        base = jnp.asarray(to * cap, F32) if isinstance(to, int) else (to * cap).astype(F32)
        hot = jnp.where(slot + base == key, 1.0, 0.0).astype(BF16)
        esend[to, :cap] = jnp.dot(hot, frac[...], preferred_element_type=F32).astype(BF16)
        hot = jnp.where(wide_slot + base == key, 1.0, 0.0).astype(BF16)
        meta = lax.dot_general(
            loose, hot, (((1,), (1,)), ((), ())), preferred_element_type=F32
        )
        esend[to, cap:] = (meta + fixed).astype(BF16)

    each(0, tiles, pack)
    each(1, tiles, lambda s: entry_copy(s).start())
    unless_mine(lambda mine: entry_copy(0, mine).start())

    def rim(role, sending):
        to, h = wt - 2 * near, 1 - par
        n = RIMS.index(role)
        if sending:
            start = HALO + h * half
            if role == "R":
                start, to = HALO + rows * near + half * (1 - par), wt - near
                at = HALO + 2 * rows * near + half * (1 - par)
                there = inside(to) & inside(wt + near)
            else:
                at = HALO + (wt - to) * rows + h * half
                there = inside(to)
            copy = pltpu.make_async_remote_copy(
                src_ref=inp.at[pl.ds(start, half)], dst_ref=inp.at[pl.ds(at, half)],
                send_sem=send_sem.at[RIM], recv_sem=hrecv_sem.at[n],
                device_id=at_work(to, wc), device_id_type=MESH,
            )
        else:
            come, at = {
                "A0": (wt + near, HALO + rows * near + half * (1 - par)),
                "A1": (wt + near, HALO + rows * near + half * par),
                "B0": (wt - near, HALO - rows * near + half * (1 - par)),
                "B1": (wt - near, HALO - rows * near + half * par),
                "F": (wt + 2 * near, HALO + 2 * rows * near + half * (1 - par)),
                "R": (wt - 2 * near, HALO - 2 * rows * near + half * par),
            }[role]
            there = inside(come)
            copy = came(inp.at[pl.ds(at, half)], hrecv_sem.at[n], RIM)
        return there, copy

    def rim_start(role):
        there, copy = rim(role, True)

        @pl.when(there)
        def _():
            copy.start()

    def rim_wait(role):
        there, copy = rim(role, False)

        @pl.when(there)
        def _():
            copy.wait_recv()

    came(drecv, drecv_sem, DEMAND).wait_recv()
    demand[...] = lax.fori_loop(
        1, tiles, lambda s, t: t + drecv[s].astype(F32), drecv[0].astype(F32)
    )

    def fill(q):
        for j in range(some_rows):
            row = piece(par, q) + j
            add = lift_col * demand[pl.ds(row, 1), :]
            inp[HALO + row] = (gath[row].astype(F32) + add).astype(BF16)

    def near_start(q):
        low = piece(par, q)
        n = 2 * q // PIECES
        for role, to in (("A", wt + near), ("B", wt - near)):
            @pl.when(inside(to))
            def _(role=role, to=to):
                pltpu.make_async_remote_copy(
                    src_ref=inp.at[pl.ds(HALO + low, some_rows)],
                    dst_ref=inp.at[pl.ds(HALO + (wt - to) * rows + low, some_rows)],
                    send_sem=send_sem.at[RIM], recv_sem=hrecv_sem.at[RIMS.index(role + str(n))],
                    device_id=at_work(to, wc), device_id_type=MESH,
                ).start()

    for q in range(PIECES):
        feat_wait(q)
        fill(q)
        near_start(q)

    def in_map(row):
        return (row >= 0) & (row < height)

    col = lane + wc * own_cols - margin
    col_ok = ((col >= 0) & (col < cols)).astype(F32)

    def gathered(ref, at, dilation):
        return jnp.concatenate(
            [
                jnp.concatenate([ref[at + j + u * dilation] for u in range(3)], axis=0)
                for j in range(GROUP)
            ],
            axis=1,
        )

    def conv(ref, at, weights, dilation):
        result = jnp.dot(weights[...], gathered(ref, at, dilation), preferred_element_type=F32)
        parts = []
        for j in range(GROUP):
            one = result[:, j * LANES : (j + 1) * LANES]
            parts.append(
                one[chan : 2 * chan]
                + pltpu.roll(one[:chan], dilation, 1)
                + pltpu.roll(one[2 * chan :], LANES - dilation, 1)
            )
        return parts

    def keep_of(row):
        return col_ok * in_map(row).astype(F32)

    def first(at):
        keep = keep_of(top - 20 + at)
        for j, value in enumerate(conv(inp, at, wm1, 4)):
            pre[at + j] = value
            hid[at + j] = (value * jax.nn.sigmoid(value) * keep).astype(BF16)

    def second(at):
        keep = keep_of(top - 12 + at)
        for j, value in enumerate(conv(hid, at, wm2, 8)):
            sec[at + j] = (jax.nn.sigmoid(value) * keep).astype(BF16)

    def third(at):
        keep = keep_of(top - 4 + at)
        for j, value in enumerate(conv(sec, at, wm3, 8)):
            p = pre[at + j + 16]
            s = jax.nn.sigmoid(p)
            gpre[at + j] = (value * s * (1.0 + p * (1.0 - s)) * keep).astype(BF16)

    owned = ((lane >= margin) & (lane < margin + own_cols)).astype(F32)

    def fourth(at):
        result = jnp.dot(wm4[...], gathered(gpre, at, 4), preferred_element_type=F32)
        result = result[0:8] + result[8:16] + result[16:24]
        for j in range(GROUP):
            one = result[:, j * LANES : (j + 1) * LANES]
            line = (
                one[1:2]
                + pltpu.roll(one, 4, 1)[0:1]
                + pltpu.roll(one, LANES - 4, 1)[2:3]
            )
            gown[at + j : at + j + 1, :] = line * owned

    def groups(*work):
        for side in range(2):
            @pl.when(par == side)
            def _(side=side):
                for fn, count, which in work:
                    for g in which:
                        fn(count - GROUP - GROUP * g if side else GROUP * g)

    def stage(ones, twos=(), threes=(), fours=()):
        groups(
            (first, rows + 40, ones), (second, rows + 24, twos),
            (third, rows + 8, threes), (fourth, rows, fours),
        )

    per_tile = rows // TILE_ROWS
    n_tiles = tile_hot.shape[0]
    lane_of = lax.broadcasted_iota(jnp.int32, (1, LANES), 1)
    counted = lax.broadcasted_iota(jnp.int32, (PART, LANES), 0).astype(F32).astype(BF16)

    def cells_of(g):
        known = [erecv[g * per + n, cap:, :].astype(F32) for n in range(per)]
        meta = known[0]
        for k in known[1:]:
            meta = meta + k
        net_row = meta[0:1, :] + (lane_of // cap * SPREAD).astype(F32)
        mine = meta[1:2, :].astype(jnp.int32)
        across = mine % per_row - wc * (own_cols // TILE_COLS)
        which = across * per_tile + mine // per_row
        which = jnp.where((across >= 0) & (across < own_cols // TILE_COLS), which, -1)
        at_g = pl.multiple_of(g * LANES, LANES)
        tile_hot[:, pl.ds(at_g, LANES)] = jnp.where(
            lax.broadcasted_iota(jnp.int32, (n_tiles, LANES), 0) == which, 1.0, 0.0
        )
        count = pins // LANES

        def pin_row(n, at):
            return jnp.concatenate([known[n][2 + at + m : 3 + at + m, :] for m in range(count)], axis=1)

        net_pin = jnp.concatenate([pin_row(n, 0) + float(n * SPREAD) for n in range(per)], axis=1)
        cell_part = jnp.concatenate([pin_row(n, count) for n in range(per)], axis=1)
        cell_row = jnp.concatenate([pin_row(n, 2 * count) for n in range(per)], axis=1)
        net_col = jnp.transpose(jnp.broadcast_to(net_row, (8, LANES)))[:, 0:1]
        same = jnp.where(net_col == net_pin, 1.0, 0.0).astype(BF16)

        def some(q):
            at_q = pl.multiple_of(q * PART, PART)
            part = jnp.asarray(q, F32) if isinstance(q, int) else q.astype(F32)
            row = jnp.where(cell_part == part, cell_row, -1.0)
            hot = jnp.concatenate(
                [
                    jnp.where(
                        counted == row[:, n * LANES : (n + 1) * LANES].astype(BF16),
                        jnp.ones((), BF16), jnp.zeros((), BF16),
                    )
                    for n in range(row.shape[1] // LANES)
                ],
                axis=1,
            )
            to_cell[pl.ds(at_g, LANES), pl.ds(at_q, PART)] = lax.dot_general(
                same, hot, (((1,), (1,)), ((), ())), preferred_element_type=F32
            ).astype(BF16)

        loop(to_cell.shape[1] // PART, some)

    def loop(count, fn):
        if count <= 4:
            for n in range(count):
                fn(n)
        else:
            def body(n, carry):
                fn(n)
                return carry
            lax.fori_loop(0, count, body, 0)


    @pl.when(alike)
    def _():
        came(erecv, erecv_sem, ENTRY).wait_recv()
        loop(tiles // per, cells_of)

    rim_wait("B0")
    rim_wait("B1")
    rim_start("F")
    stage(range(6, 12))

    @pl.when(jnp.logical_not(alike))
    def _():
        came(erecv, erecv_sem, ENTRY).wait_recv()
        loop(tiles // per, cells_of)

    rim_wait("A0")
    rim_start("R")
    stage(range(4, 6), range(4, 8))
    rim_wait("R")
    stage(range(12, 14), range(8, 10), range(4, 6))
    rim_wait("A1")
    rim_wait("F")
    stage(range(0, 4), range(0, 4), range(0, 4), range(0, 4))

    grads = gown[...]
    right = lax.broadcasted_iota(jnp.int32, (TILE_ROWS, LANES), 0) == (
        lax.broadcasted_iota(jnp.int32, (TILE_ROWS, LANES), 1) // TILE_COLS
    )
    leaning = [
        pltpu.roll(
            grads[a * TILE_ROWS : (a + 1) * TILE_ROWS], 0, 1, stride=TILE_COLS, stride_axis=0
        )
        for a in range(per_tile)
    ]
    parts = []
    for b in range(own_cols // TILE_COLS):
        for a in range(per_tile):
            moved = pltpu.roll(leaning[a], (-margin - b * TILE_COLS) % LANES, 1)
            parts.append(jnp.sum(jnp.where(right, moved, 0.0), axis=0, keepdims=True))
    by_tile = jnp.concatenate(
        [p.astype(F32) for p in split(jnp.concatenate(parts, axis=0), 3)], axis=0
    ).astype(BF16)
    all_frac = erecv[:, :cap, :].reshape(tiles * cap, LANES)
    found = lax.dot_general(
        by_tile, all_frac, (((1,), (1,)), ((), ())), preferred_element_type=F32
    )
    found = found[:n_tiles] + found[n_tiles : 2 * n_tiles] + found[2 * n_tiles :]
    entry_grad = jnp.sum(found * tile_hot[...], axis=0, keepdims=True)
    pieces = jnp.concatenate(
        [p.astype(F32) for p in split(entry_grad, 3)] + [jnp.zeros((5, tiles * cap), F32)], axis=0
    ).astype(BF16)
    cells = jnp.dot(pieces, to_cell[...], preferred_element_type=F32)
    cells = cells[0:1] + cells[1:2] + cells[2:3]
    for u in range(csend.shape[0]):
        csend[u] = cells[:, u * LANES : (u + 1) * LANES]

    share = LANES // CELL_DEV

    def cell_copy(step, to):
        return pltpu.make_async_remote_copy(
            src_ref=csend.at[to[0] // share], dst_ref=crecv.at[step],
            send_sem=send_sem.at[CELL], recv_sem=crecv_sem,
            device_id=to, device_id_type=MESH,
        )

    each_peer(lambda n, who: cell_copy(n, who).start())

    def sent(n, ref):
        came(ref, crecv_sem, n).wait_send()

    unless_mine(lambda mine: sent(FEAT, win.at[pl.ds(0, chans - mine)]))
    unless_mine(lambda mine: sent(DEMAND, dsend.at[pl.ds(0, (tiles - mine) * rows)]))
    unless_mine(lambda mine: sent(ENTRY, esend.at[pl.ds(0, tiles - mine)]))
    ahead, behind = inside(wt + near), inside(wt - 2 * near)
    for there, count in (
        (ahead & behind, 6), (ahead & jnp.logical_not(behind), 5),
        (jnp.logical_not(ahead) & behind, 3), (jnp.logical_not(ahead | behind), 2),
    ):
        @pl.when(there)
        def _(count=count):
            sent(RIM, inp.at[pl.ds(0, count * half)])
    arrived = crecv.at[pl.ds(1, others)]
    came(arrived, crecv_sem, CELL).wait()
    total = csend[ti // share] + jnp.sum(crecv[1:], axis=0)
    for n in range(1, share):
        total = jnp.where(ti % share == n, pltpu.roll(total, LANES - n * CELL_DEV, 1), total)
    out[...] = total


def solution(mesh):
    tiles, chans = mesh.shape["tile"], mesh.shape["chan"]

    def local(
        feat, lift, w4, w8, frac, target, owner, net_e, weight, net_p, cell,
    ):
        rows, chan_own, cols = feat.shape
        chan = chan_own * chans
        entries = frac.shape[0]
        pins = weight.shape[0]
        in_rows = rows + 2 * HALO
        height = rows * tiles
        cap = -(-(2 * entries // tiles) // 16) * 16
        n_tiles = rows // TILE_ROWS * (cols // chans // TILE_COLS)
        vm = pltpu.VMEM
        dma = pltpu.SemaphoreType.DMA
        result = pl.pallas_call(
            functools.partial(kernel, tiles, chans),
            out_shape=pltpu.VMEM((1, LANES), F32),
            in_specs=[pl.BlockSpec(memory_space=pltpu.HBM)] * 11,
            out_specs=pl.BlockSpec(memory_space=pltpu.VMEM),
            scratch_shapes=[
                vm(feat.shape, BF16),
                vm((1, chan), F32),
                vm(w4.shape, BF16),
                vm(w8.shape, BF16),
                vm(frac.shape, BF16),
                vm((5, 1, entries), jnp.int32),
                vm((1, pins), F32),
                dma((7,)),
                vm((chans, rows, chan_own, LANES), BF16),
                vm((rows, chan, LANES), BF16),
                vm((in_rows, chan, LANES), BF16),
                vm((rows + 40, chan, LANES), F32),
                vm((rows + 40, chan, LANES), BF16),
                vm((rows + 24, chan, LANES), BF16),
                vm((rows + 8, chan, LANES), BF16),
                vm((3 * chan, 3 * chan), BF16),
                vm((3 * chan, 3 * chan), BF16),
                vm((3 * chan, 3 * chan), BF16),
                vm((32, 3 * chan), BF16),
                vm((entries, TILE_ROWS * LANES), BF16),
                vm((height, LANES), F32),
                vm((height, LANES), BF16),
                vm((tiles, rows, LANES), BF16),
                vm((rows, LANES), F32),
                vm((rows, LANES), F32),
                vm((tiles, cap + META, LANES), BF16),
                vm((tiles, cap + META, LANES), BF16),
                vm((tiles * cap, tiles * CELL_DEV), BF16),
                vm((n_tiles, tiles * cap), F32),
                vm((tiles * CELL_DEV // LANES, 1, LANES), F32),
                vm((tiles * chans, 1, LANES), F32),
                dma((5,)),
                dma((PIECES,)),
                dma((len(RIMS),)),
                dma(()),
                dma(()),
                dma(()),
            ],
            compiler_params=pltpu.CompilerParams(collective_id=0, has_side_effects=True),
        )(
            feat, lift.reshape(1, chan), w4, w8, frac, target.reshape(1, entries),
            owner.reshape(1, entries), net_e.reshape(1, entries), weight.reshape(1, pins),
            net_p.reshape(1, pins), cell.reshape(1, pins),
        )
        return result[0, :CELL_DEV]

    in_specs = (
        P("tile", "chan", None), P(), P(), P(),
        P("tile", None), P("tile", None),
        P("tile"), P("tile"), P("tile"), P("tile"), P("tile"),
    )
    return jax.shard_map(
        local, mesh=mesh, in_specs=in_specs, out_specs=P("tile"), check_vma=False
    )
```

```python
import functools

import jax
import jax.numpy as jnp
from jax import lax
from jax.experimental import pallas as pl
from jax.experimental.pallas import tpu as pltpu
from jax.sharding import PartitionSpec as P

MESH = pl.DeviceIdType.MESH
CELL_DEV = 64
TILE_ROWS = 8
TILE_COLS = 16
LANES = 128
HALO = 24
GROUP = 4
META = 8
SPREAD = 4096
RIMS = ("A0", "B0", "F", "A1", "B1", "R")
FEAT, DEMAND, ENTRY, RIM, CELL = range(5)
PART = 256
PIECES = 4
F32 = jnp.float32
BF16 = jnp.bfloat16


def split(x, terms):
    parts = []
    for _ in range(terms):
        part = x.astype(BF16)
        parts.append(part)
        x = x - part.astype(F32)
    return parts


def kernel(
    tiles, chans,
    feat_in, lift_in, w4_in, w8_in, frac_in, target_in, owner_in, net_e_in, weight_in, net_p_in,
    cell_in,
    out,
    feat, lift, w4, w8, frac, numbers, weight, load_sem,
    win, gath, inp, pre, hid, sec, gpre, wm1, wm2, wm3, wm4,
    fmask, dbuf, dsend, drecv, demand, gown, esend, erecv, to_cell, tile_hot, csend, crecv,
    send_sem, frecv_sem, hrecv_sem, drecv_sem, erecv_sem, crecv_sem,
):
    ti = lax.axis_index("tile")
    ci = lax.axis_index("chan")
    rows, chan_own, cols = feat.shape
    chan = chan_own * chans
    own_cols = cols // chans
    margin = (LANES - own_cols) // 2
    half = rows // 2
    some_rows = rows // PIECES
    in_rows = rows + 2 * HALO
    others = tiles * chans - 1
    entries, pins = frac.shape[0], weight.shape[1]
    cap = esend.shape[1] - META
    per = LANES // cap
    height = rows * tiles

    par = ci % 2
    alike = ti % 2 == par
    wt = ti - ti % 2 + par
    wc = ci - par + ti % 2
    near = 2 * par - 1
    top = wt * rows

    def at_work(t, c):
        return (t - t % 2 + c % 2, c - c % 2 + t % 2)

    target, owner, net_e, net_p, cell = (numbers.at[n] for n in range(5))
    loads = [
        pltpu.make_async_copy(src, dst, load_sem.at[n])
        for n, (src, dst) in enumerate(
            [
                (feat_in, feat), (weight_in, weight), (frac_in, frac), (lift_in, lift),
                (w4_in, w4), (w8_in, w8),
            ]
        )
    ]
    for load in loads:
        load.start()
    for src, dst in (
        (target_in, target), (owner_in, owner), (net_e_in, net_e), (net_p_in, net_p),
        (cell_in, cell),
    ):
        pltpu.make_async_copy(src, dst, load_sem.at[len(loads)]).start()

    barrier = pltpu.get_barrier_semaphore()

    def wrap(number, count):
        return jnp.where(number >= count, number - count, number)

    def inside(strip):
        return (strip >= 0) & (strip < tiles)

    def each(lo, hi, fn):
        if hi - lo <= 32:
            for step in range(lo, hi):
                fn(step)
        else:
            def body(step, carry):
                fn(step)
                return carry
            lax.fori_loop(lo, hi, body, 0)

    def each_peer(fn):
        def along(hop):
            for turn in range(chans):
                fn(hop * chans + turn, (wrap(ti + hop, tiles), wrap(ci + turn, chans)))
        each(1, tiles, along)
        for turn in range(1, chans):
            fn(turn, (ti, wrap(ci + turn, chans)))

    each_peer(
        lambda n, who: pl.semaphore_signal(barrier, inc=1, device_id=who, device_id_type=MESH)
    )

    loads[0].wait()

    flat = feat[...].astype(F32).reshape(rows * chan_own, cols)
    lane = lax.broadcasted_iota(jnp.int32, (1, LANES), 1)
    for k in range(chans):
        first_col = k * own_cols - margin
        turned = pltpu.roll(flat, (-first_col) % cols, 1)[:, :LANES]
        on_map = (lane + first_col >= 0) & (lane + first_col < cols)
        win[k] = jnp.where(on_map, turned, 0.0).astype(BF16).reshape(rows, chan_own, LANES)

    def span(delta):
        low = max(0, rows * delta - HALO)
        high = min(rows, rows * delta + HALO + rows)
        return low, high - low, HALO - rows * delta + low

    for delta in (1, -1, 2, -2):
        @pl.when(jnp.logical_not(inside(wt - delta)))
        def _(delta=delta):
            _, count, at = span(delta)
            inp[at : at + count] = jnp.zeros((count, chan, LANES), BF16)

    for load in loads[1:]:
        load.wait()
    pltpu.make_async_copy(numbers, numbers, load_sem.at[len(loads)]).wait()
    per_row = cols // TILE_COLS
    own, cell_no = owner[...], cell[...]
    target_row = target[...].astype(F32)
    table = jnp.concatenate(
        [
            (target[...] * (rows // TILE_ROWS) + own // per_row).astype(F32),
            (own % per_row).astype(F32),
            net_e[...].astype(F32),
            weight[...],
            net_p[...].astype(F32),
            target_row,
            jnp.zeros((2, entries), F32),
        ],
        axis=0,
    )
    columns = jnp.transpose(table)
    wpin_col, net_p_col = columns[:, 3:4], columns[:, 4:5]
    strength = jnp.sum(
        jnp.where(net_p_col == table[2:3, :], wpin_col, 0.0), axis=0, keepdims=True
    )
    src_j = lax.broadcasted_iota(jnp.int32, (LANES, TILE_ROWS * LANES), 0)
    dst_j = lax.broadcasted_iota(jnp.int32, (LANES, TILE_ROWS * LANES), 1)
    pick = src_j == (dst_j // LANES) * TILE_COLS + dst_j % TILE_COLS
    spread = jnp.dot(
        frac[...], jnp.where(pick, 1.0, 0.0).astype(BF16), preferred_element_type=F32
    )
    wide = lax.broadcasted_iota(jnp.int32, (1, TILE_ROWS * LANES), 1) % LANES
    block = (wide + ci * own_cols - margin + TILE_COLS * LANES) // TILE_COLS - LANES
    fmask[...] = jnp.where(columns[:, 1:2] == block.astype(F32), spread, 0.0).astype(BF16)
    blocks = height // TILE_ROWS
    block_row = lax.broadcasted_iota(jnp.int32, (blocks, entries), 0).astype(F32)
    placed = jnp.where(block_row == table[0:1, :], strength, 0.0)
    left = jnp.concatenate(split(placed, 2), axis=0)
    partial = jnp.dot(left, fmask[...], preferred_element_type=F32)
    partial = partial[:blocks] + partial[blocks:]
    for i in range(TILE_ROWS):
        dbuf[pl.ds(i, blocks, stride=TILE_ROWS), :] = partial[:, i * LANES : (i + 1) * LANES]
    dsend[...] = dbuf[...].astype(BF16)

    def piece(side, q):
        return (q + side * (PIECES - 1 - 2 * q)) * some_rows

    def feat_copy(turn, q, mine=False):
        low = piece(ti % 2, q)
        to = wrap(ci + turn, chans)
        src = win.at[to, pl.ds(low, some_rows)]
        dst = gath.at[
            pl.ds(low, some_rows), pl.ds(pl.multiple_of(ci * chan_own, chan_own), chan_own)
        ]
        if mine:
            return pltpu.make_async_copy(src, dst, frecv_sem.at[q])
        return pltpu.make_async_remote_copy(
            src_ref=src, dst_ref=dst,
            send_sem=send_sem.at[FEAT], recv_sem=frecv_sem.at[q],
            device_id=at_work(ti, to), device_id_type=MESH,
        )

    def came(dst, sem, n):
        return pltpu.make_async_remote_copy(
            src_ref=dst, dst_ref=dst, send_sem=send_sem.at[n], recv_sem=sem,
            device_id=(ti, wrap(ci + 1, chans)), device_id_type=MESH,
        )

    def unless_mine(fn):
        @pl.when(jnp.logical_not(alike))
        def _():
            fn(False)

        @pl.when(alike)
        def _():
            fn(True)

    def feat_send(turn, q):
        if turn:
            feat_copy(turn, q).start()
        else:
            unless_mine(lambda mine: feat_copy(0, q, mine).start())

    def feat_wait(q):
        came(gath.at[pl.ds(piece(par, q), some_rows)], frecv_sem.at[q], FEAT).wait_recv()

    def demand_copy(step, mine=False):
        to = wrap(ti + step, tiles)
        src = dsend.at[pl.ds(pl.multiple_of(to * rows, rows), rows)]
        if mine:
            return pltpu.make_async_copy(src, drecv.at[step], drecv_sem)
        return pltpu.make_async_remote_copy(
            src_ref=src, dst_ref=drecv.at[step],
            send_sem=send_sem.at[DEMAND], recv_sem=drecv_sem,
            device_id=at_work(to, ci), device_id_type=MESH,
        )

    def entry_copy(step, mine=False):
        to = wrap(ti + step, tiles)
        if mine:
            return pltpu.make_async_copy(esend.at[to], erecv.at[ti], erecv_sem)
        return pltpu.make_async_remote_copy(
            src_ref=esend.at[to], dst_ref=erecv.at[ti],
            send_sem=send_sem.at[ENTRY], recv_sem=erecv_sem,
            device_id=at_work(to, ci), device_id_type=MESH,
        )

    pl.semaphore_wait(barrier, others)
    each(1, tiles, lambda s: demand_copy(s).start())
    unless_mine(lambda mine: demand_copy(0, mine).start())
    for q in range(PIECES):
        for turn in range(chans - 1, -1, -1):
            feat_send(turn, q)

    lift_row = lift[...]
    lift_col = jnp.transpose(jnp.broadcast_to(lift_row, (LANES, chan)))
    for u in range(3):
        for v in range(3):
            at_v, at_u = slice(v * chan, (v + 1) * chan), slice(u * chan, (u + 1) * chan)
            wm1[at_v, at_u] = jnp.transpose(w4[u, v].astype(F32)).astype(BF16)
            wm2[at_v, at_u] = jnp.transpose(w8[u, v].astype(F32)).astype(BF16)
            wm3[at_v, at_u] = w8[2 - u, 2 - v]
    taps = []
    for v in range(3):
        taps.append(
            jnp.concatenate(
                [
                    jnp.sum(
                        w4[2 - u, 2 - v].astype(F32) * lift_col[:, :chan], axis=0, keepdims=True
                    )
                    for u in range(3)
                ],
                axis=1,
            )
        )
    tap_rows = jnp.concatenate(taps + [jnp.zeros((5, 3 * chan), F32)], axis=0)
    hi, mid, low_part = [p.astype(F32) for p in split(tap_rows, 3)]
    wm4[...] = jnp.concatenate(
        [hi, mid, low_part, jnp.zeros((8, 3 * chan), F32)], axis=0
    ).astype(BF16)

    before = lax.broadcasted_iota(jnp.int32, (entries, entries), 0) < lax.broadcasted_iota(
        jnp.int32, (entries, entries), 1
    )
    rank = jnp.sum(
        jnp.where((columns[:, 5:6] == target_row) & before, 1.0, 0.0), axis=0, keepdims=True
    )
    key = target_row * float(cap) + rank
    pin_rows = [
        row[:, n * LANES : (n + 1) * LANES]
        for row in (table[4:5, :], (cell_no // PART).astype(F32), (cell_no % PART).astype(F32))
        for n in range(pins // LANES)
    ]
    fixed = jnp.concatenate(
        [jnp.zeros((2, LANES), F32)] + pin_rows
        + [jnp.zeros((1, LANES), F32)] * (META - 2 - len(pin_rows)),
        axis=0,
    )
    loose = jnp.concatenate(
        [table[2:3, :], own.astype(F32), jnp.zeros((META - 2, entries), F32)], axis=0
    ).astype(BF16)
    slot = lax.broadcasted_iota(jnp.int32, (cap, entries), 0).astype(F32)
    wide_slot = lax.broadcasted_iota(jnp.int32, (LANES, entries), 0) - (ti % per) * cap
    wide_slot = jnp.where(
        (wide_slot >= 0) & (wide_slot < cap), wide_slot, -(cap * tiles + 1)
    ).astype(F32)

    def pack(to):
        base = jnp.asarray(to * cap, F32) if isinstance(to, int) else (to * cap).astype(F32)
        hot = jnp.where(slot + base == key, 1.0, 0.0).astype(BF16)
        esend[to, :cap] = jnp.dot(hot, frac[...], preferred_element_type=F32).astype(BF16)
        hot = jnp.where(wide_slot + base == key, 1.0, 0.0).astype(BF16)
        meta = lax.dot_general(
            loose, hot, (((1,), (1,)), ((), ())), preferred_element_type=F32
        )
        esend[to, cap:] = (meta + fixed).astype(BF16)

    each(0, tiles, pack)
    each(1, tiles, lambda s: entry_copy(s).start())
    unless_mine(lambda mine: entry_copy(0, mine).start())

    def rim(role, sending):
        to, h = wt - 2 * near, 1 - par
        n = RIMS.index(role)
        if sending:
            start = HALO + h * half
            if role == "R":
                start, to = HALO + rows * near + half * (1 - par), wt - near
                at = HALO + 2 * rows * near + half * (1 - par)
                there = inside(to) & inside(wt + near)
            else:
                at = HALO + (wt - to) * rows + h * half
                there = inside(to)
            copy = pltpu.make_async_remote_copy(
                src_ref=inp.at[pl.ds(start, half)], dst_ref=inp.at[pl.ds(at, half)],
                send_sem=send_sem.at[RIM], recv_sem=hrecv_sem.at[n],
                device_id=at_work(to, wc), device_id_type=MESH,
            )
        else:
            come, at = {
                "A0": (wt + near, HALO + rows * near + half * (1 - par)),
                "A1": (wt + near, HALO + rows * near + half * par),
                "B0": (wt - near, HALO - rows * near + half * (1 - par)),
                "B1": (wt - near, HALO - rows * near + half * par),
                "F": (wt + 2 * near, HALO + 2 * rows * near + half * (1 - par)),
                "R": (wt - 2 * near, HALO - 2 * rows * near + half * par),
            }[role]
            there = inside(come)
            copy = came(inp.at[pl.ds(at, half)], hrecv_sem.at[n], RIM)
        return there, copy

    def rim_start(role):
        there, copy = rim(role, True)

        @pl.when(there)
        def _():
            copy.start()

    def rim_wait(role):
        there, copy = rim(role, False)

        @pl.when(there)
        def _():
            copy.wait_recv()

    came(drecv, drecv_sem, DEMAND).wait_recv()
    demand[...] = lax.fori_loop(
        1, tiles, lambda s, t: t + drecv[s].astype(F32), drecv[0].astype(F32)
    )

    def fill(q):
        for j in range(some_rows):
            row = piece(par, q) + j
            add = lift_col * demand[pl.ds(row, 1), :]
            inp[HALO + row] = (gath[row].astype(F32) + add).astype(BF16)

    def near_start(q):
        low = piece(par, q)
        n = 2 * q // PIECES
        for role, to in (("A", wt + near), ("B", wt - near)):
            @pl.when(inside(to))
            def _(role=role, to=to):
                pltpu.make_async_remote_copy(
                    src_ref=inp.at[pl.ds(HALO + low, some_rows)],
                    dst_ref=inp.at[pl.ds(HALO + (wt - to) * rows + low, some_rows)],
                    send_sem=send_sem.at[RIM], recv_sem=hrecv_sem.at[RIMS.index(role + str(n))],
                    device_id=at_work(to, wc), device_id_type=MESH,
                ).start()

    for q in range(PIECES):
        feat_wait(q)
        fill(q)
        near_start(q)

    def in_map(row):
        return (row >= 0) & (row < height)

    col = lane + wc * own_cols - margin
    col_ok = ((col >= 0) & (col < cols)).astype(F32)

    def gathered(ref, at, dilation):
        return jnp.concatenate(
            [
                jnp.concatenate([ref[at + j + u * dilation] for u in range(3)], axis=0)
                for j in range(GROUP)
            ],
            axis=1,
        )

    def conv(ref, at, weights, dilation):
        result = jnp.dot(weights[...], gathered(ref, at, dilation), preferred_element_type=F32)
        parts = []
        for j in range(GROUP):
            one = result[:, j * LANES : (j + 1) * LANES]
            parts.append(
                one[chan : 2 * chan]
                + pltpu.roll(one[:chan].astype(BF16), dilation, 1).astype(F32)
                + pltpu.roll(one[2 * chan :].astype(BF16), LANES - dilation, 1).astype(F32)
            )
        return parts

    def keep_of(row):
        return col_ok * in_map(row).astype(F32)

    def first(at):
        keep = keep_of(top - 20 + at)
        for j, value in enumerate(conv(inp, at, wm1, 4)):
            pre[at + j] = value
            hid[at + j] = (value * jax.nn.sigmoid(value) * keep).astype(BF16)

    def second(at):
        keep = keep_of(top - 12 + at)
        for j, value in enumerate(conv(hid, at, wm2, 8)):
            sec[at + j] = (jax.nn.sigmoid(value) * keep).astype(BF16)

    def third(at):
        keep = keep_of(top - 4 + at)
        for j, value in enumerate(conv(sec, at, wm3, 8)):
            p = pre[at + j + 16]
            s = jax.nn.sigmoid(p)
            gpre[at + j] = (value * s * (1.0 + p * (1.0 - s)) * keep).astype(BF16)

    owned = ((lane >= margin) & (lane < margin + own_cols)).astype(F32)

    def fourth(at):
        result = jnp.dot(wm4[...], gathered(gpre, at, 4), preferred_element_type=F32)
        result = result[0:8] + result[8:16] + result[16:24]
        for j in range(GROUP):
            one = result[:, j * LANES : (j + 1) * LANES]
            line = (
                one[1:2]
                + pltpu.roll(one, 4, 1)[0:1]
                + pltpu.roll(one, LANES - 4, 1)[2:3]
            )
            gown[at + j : at + j + 1, :] = line * owned

    def groups(*work):
        for side in range(2):
            @pl.when(par == side)
            def _(side=side):
                for fn, count, which in work:
                    for g in which:
                        fn(count - GROUP - GROUP * g if side else GROUP * g)

    def stage(ones, twos=(), threes=(), fours=()):
        groups(
            (first, rows + 40, ones), (second, rows + 24, twos),
            (third, rows + 8, threes), (fourth, rows, fours),
        )

    per_tile = rows // TILE_ROWS
    n_tiles = tile_hot.shape[0]
    lane_of = lax.broadcasted_iota(jnp.int32, (1, LANES), 1)
    counted = lax.broadcasted_iota(jnp.int32, (PART, LANES), 0).astype(F32).astype(BF16)

    def cells_of(g):
        known = [erecv[g * per + n, cap:, :].astype(F32) for n in range(per)]
        meta = known[0]
        for k in known[1:]:
            meta = meta + k
        net_row = meta[0:1, :] + (lane_of // cap * SPREAD).astype(F32)
        mine = meta[1:2, :].astype(jnp.int32)
        across = mine % per_row - wc * (own_cols // TILE_COLS)
        which = across * per_tile + mine // per_row
        which = jnp.where((across >= 0) & (across < own_cols // TILE_COLS), which, -1)
        at_g = pl.multiple_of(g * LANES, LANES)
        tile_hot[:, pl.ds(at_g, LANES)] = jnp.where(
            lax.broadcasted_iota(jnp.int32, (n_tiles, LANES), 0) == which, 1.0, 0.0
        )
        count = pins // LANES

        def pin_row(n, at):
            return jnp.concatenate([known[n][2 + at + m : 3 + at + m, :] for m in range(count)], axis=1)

        net_pin = jnp.concatenate([pin_row(n, 0) + float(n * SPREAD) for n in range(per)], axis=1)
        cell_part = jnp.concatenate([pin_row(n, count) for n in range(per)], axis=1)
        cell_row = jnp.concatenate([pin_row(n, 2 * count) for n in range(per)], axis=1)
        net_col = jnp.transpose(jnp.broadcast_to(net_row, (8, LANES)))[:, 0:1]
        same = jnp.where(net_col == net_pin, 1.0, 0.0).astype(BF16)

        def some(q):
            at_q = pl.multiple_of(q * PART, PART)
            part = jnp.asarray(q, F32) if isinstance(q, int) else q.astype(F32)
            row = jnp.where(cell_part == part, cell_row, -1.0)
            hot = jnp.concatenate(
                [
                    jnp.where(
                        counted == row[:, n * LANES : (n + 1) * LANES].astype(BF16),
                        jnp.ones((), BF16), jnp.zeros((), BF16),
                    )
                    for n in range(row.shape[1] // LANES)
                ],
                axis=1,
            )
            to_cell[pl.ds(at_g, LANES), pl.ds(at_q, PART)] = lax.dot_general(
                same, hot, (((1,), (1,)), ((), ())), preferred_element_type=F32
            ).astype(BF16)

        loop(to_cell.shape[1] // PART, some)

    def loop(count, fn):
        if count <= 4:
            for n in range(count):
                fn(n)
        else:
            def body(n, carry):
                fn(n)
                return carry
            lax.fori_loop(0, count, body, 0)


    @pl.when(alike)
    def _():
        came(erecv, erecv_sem, ENTRY).wait_recv()
        loop(tiles // per, cells_of)

    rim_wait("B0")
    rim_wait("B1")
    rim_start("F")
    stage(range(6, 12))

    @pl.when(jnp.logical_not(alike))
    def _():
        came(erecv, erecv_sem, ENTRY).wait_recv()
        loop(tiles // per, cells_of)

    rim_wait("A0")
    rim_start("R")
    stage(range(4, 6), range(4, 8))
    rim_wait("R")
    stage(range(12, 14), range(8, 10), range(4, 6))
    rim_wait("A1")
    rim_wait("F")
    stage(range(0, 4), range(0, 4), range(0, 4), range(0, 4))

    grads = gown[...]
    right = lax.broadcasted_iota(jnp.int32, (TILE_ROWS, LANES), 0) == (
        lax.broadcasted_iota(jnp.int32, (TILE_ROWS, LANES), 1) // TILE_COLS
    )
    leaning = [
        pltpu.roll(
            grads[a * TILE_ROWS : (a + 1) * TILE_ROWS], 0, 1, stride=TILE_COLS, stride_axis=0
        )
        for a in range(per_tile)
    ]
    parts = []
    for b in range(own_cols // TILE_COLS):
        for a in range(per_tile):
            moved = pltpu.roll(leaning[a], (-margin - b * TILE_COLS) % LANES, 1)
            parts.append(jnp.sum(jnp.where(right, moved, 0.0), axis=0, keepdims=True))
    by_tile = jnp.concatenate(
        [p.astype(F32) for p in split(jnp.concatenate(parts, axis=0), 3)], axis=0
    ).astype(BF16)
    all_frac = erecv[:, :cap, :].reshape(tiles * cap, LANES)
    found = lax.dot_general(
        by_tile, all_frac, (((1,), (1,)), ((), ())), preferred_element_type=F32
    )
    found = found[:n_tiles] + found[n_tiles : 2 * n_tiles] + found[2 * n_tiles :]
    entry_grad = jnp.sum(found * tile_hot[...], axis=0, keepdims=True)
    pieces = jnp.concatenate(
        [p.astype(F32) for p in split(entry_grad, 3)] + [jnp.zeros((5, tiles * cap), F32)], axis=0
    ).astype(BF16)
    cells = jnp.dot(pieces, to_cell[...], preferred_element_type=F32)
    cells = cells[0:1] + cells[1:2] + cells[2:3]
    for u in range(csend.shape[0]):
        csend[u] = cells[:, u * LANES : (u + 1) * LANES]

    share = LANES // CELL_DEV

    def cell_copy(step, to):
        return pltpu.make_async_remote_copy(
            src_ref=csend.at[to[0] // share], dst_ref=crecv.at[step],
            send_sem=send_sem.at[CELL], recv_sem=crecv_sem,
            device_id=to, device_id_type=MESH,
        )

    each_peer(lambda n, who: cell_copy(n, who).start())

    def sent(n, ref):
        came(ref, crecv_sem, n).wait_send()

    unless_mine(lambda mine: sent(FEAT, win.at[pl.ds(0, chans - mine)]))
    unless_mine(lambda mine: sent(DEMAND, dsend.at[pl.ds(0, (tiles - mine) * rows)]))
    unless_mine(lambda mine: sent(ENTRY, esend.at[pl.ds(0, tiles - mine)]))
    ahead, behind = inside(wt + near), inside(wt - 2 * near)
    for there, count in (
        (ahead & behind, 6), (ahead & jnp.logical_not(behind), 5),
        (jnp.logical_not(ahead) & behind, 3), (jnp.logical_not(ahead | behind), 2),
    ):
        @pl.when(there)
        def _(count=count):
            sent(RIM, inp.at[pl.ds(0, count * half)])
    arrived = crecv.at[pl.ds(1, others)]
    came(arrived, crecv_sem, CELL).wait()
    total = csend[ti // share] + jnp.sum(crecv[1:], axis=0)
    for n in range(1, share):
        total = jnp.where(ti % share == n, pltpu.roll(total, LANES - n * CELL_DEV, 1), total)
    out[...] = total


def solution(mesh):
    tiles, chans = mesh.shape["tile"], mesh.shape["chan"]

    def local(
        feat, lift, w4, w8, frac, target, owner, net_e, weight, net_p, cell,
    ):
        rows, chan_own, cols = feat.shape
        chan = chan_own * chans
        entries = frac.shape[0]
        pins = weight.shape[0]
        in_rows = rows + 2 * HALO
        height = rows * tiles
        cap = -(-(2 * entries // tiles) // 16) * 16
        n_tiles = rows // TILE_ROWS * (cols // chans // TILE_COLS)
        vm = pltpu.VMEM
        dma = pltpu.SemaphoreType.DMA
        result = pl.pallas_call(
            functools.partial(kernel, tiles, chans),
            out_shape=pltpu.VMEM((1, LANES), F32),
            in_specs=[pl.BlockSpec(memory_space=pltpu.HBM)] * 11,
            out_specs=pl.BlockSpec(memory_space=pltpu.VMEM),
            scratch_shapes=[
                vm(feat.shape, BF16),
                vm((1, chan), F32),
                vm(w4.shape, BF16),
                vm(w8.shape, BF16),
                vm(frac.shape, BF16),
                vm((5, 1, entries), jnp.int32),
                vm((1, pins), F32),
                dma((7,)),
                vm((chans, rows, chan_own, LANES), BF16),
                vm((rows, chan, LANES), BF16),
                vm((in_rows, chan, LANES), BF16),
                vm((rows + 40, chan, LANES), F32),
                vm((rows + 40, chan, LANES), BF16),
                vm((rows + 24, chan, LANES), BF16),
                vm((rows + 8, chan, LANES), BF16),
                vm((3 * chan, 3 * chan), BF16),
                vm((3 * chan, 3 * chan), BF16),
                vm((3 * chan, 3 * chan), BF16),
                vm((32, 3 * chan), BF16),
                vm((entries, TILE_ROWS * LANES), BF16),
                vm((height, LANES), F32),
                vm((height, LANES), BF16),
                vm((tiles, rows, LANES), BF16),
                vm((rows, LANES), F32),
                vm((rows, LANES), F32),
                vm((tiles, cap + META, LANES), BF16),
                vm((tiles, cap + META, LANES), BF16),
                vm((tiles * cap, tiles * CELL_DEV), BF16),
                vm((n_tiles, tiles * cap), F32),
                vm((tiles * CELL_DEV // LANES, 1, LANES), F32),
                vm((tiles * chans, 1, LANES), F32),
                dma((5,)),
                dma((PIECES,)),
                dma((len(RIMS),)),
                dma(()),
                dma(()),
                dma(()),
            ],
            compiler_params=pltpu.CompilerParams(collective_id=0, has_side_effects=True),
        )(
            feat, lift.reshape(1, chan), w4, w8, frac, target.reshape(1, entries),
            owner.reshape(1, entries), net_e.reshape(1, entries), weight.reshape(1, pins),
            net_p.reshape(1, pins), cell.reshape(1, pins),
        )
        return result[0, :CELL_DEV]

    in_specs = (
        P("tile", "chan", None), P(), P(), P(),
        P("tile", None), P("tile", None),
        P("tile"), P("tile"), P("tile"), P("tile"), P("tile"),
    )
    return jax.shard_map(
        local, mesh=mesh, in_specs=in_specs, out_specs=P("tile"), check_vma=False
    )
```

```python
import functools

import jax
import jax.numpy as jnp
from jax import lax
from jax.experimental import pallas as pl
from jax.experimental.pallas import tpu as pltpu
from jax.sharding import PartitionSpec as P

MESH = pl.DeviceIdType.MESH
CELL_DEV = 64
TILE_ROWS = 8
TILE_COLS = 16
LANES = 128
HALO = 24
GROUP = 4
META = 8
SPREAD = 4096
RIMS = ("A0", "B0", "F", "A1", "B1", "R")
FEAT, DEMAND, ENTRY, RIM, CELL = range(5)
PART = 256
PIECES = 4
F32 = jnp.float32
BF16 = jnp.bfloat16


def split(x, terms):
    parts = []
    for _ in range(terms):
        part = x.astype(BF16)
        parts.append(part)
        x = x - part.astype(F32)
    return parts


def kernel(
    tiles, chans,
    feat_in, lift_in, w4_in, w8_in, frac_in, target_in, owner_in, net_e_in, weight_in, net_p_in,
    cell_in,
    out,
    feat, lift, w4, w8, frac, numbers, weight, load_sem,
    win, gath, inp, pre, hid, sec, gpre, wm1, wm2, wm3, wm4,
    fmask, dbuf, dsend, drecv, demand, gown, esend, erecv, to_cell, tile_hot, csend, crecv,
    send_sem, frecv_sem, hrecv_sem, drecv_sem, erecv_sem, crecv_sem,
):
    ti = lax.axis_index("tile")
    ci = lax.axis_index("chan")
    rows, chan_own, cols = feat.shape
    chan = chan_own * chans
    own_cols = cols // chans
    margin = (LANES - own_cols) // 2
    half = rows // 2
    some_rows = rows // PIECES
    in_rows = rows + 2 * HALO
    others = tiles * chans - 1
    entries, pins = frac.shape[0], weight.shape[1]
    cap = esend.shape[1] - META
    per = LANES // cap
    height = rows * tiles

    par = ci % 2
    alike = ti % 2 == par
    wt = ti - ti % 2 + par
    wc = ci - par + ti % 2
    near = 2 * par - 1
    top = wt * rows

    def at_work(t, c):
        return (t - t % 2 + c % 2, c - c % 2 + t % 2)

    target, owner, net_e, net_p, cell = (numbers.at[n] for n in range(5))
    loads = [
        pltpu.make_async_copy(src, dst, load_sem.at[n])
        for n, (src, dst) in enumerate(
            [
                (feat_in, feat), (weight_in, weight), (frac_in, frac), (lift_in, lift),
                (w4_in, w4), (w8_in, w8),
            ]
        )
    ]
    for load in loads:
        load.start()
    for src, dst in (
        (target_in, target), (owner_in, owner), (net_e_in, net_e), (net_p_in, net_p),
        (cell_in, cell),
    ):
        pltpu.make_async_copy(src, dst, load_sem.at[len(loads)]).start()

    barrier = pltpu.get_barrier_semaphore()

    def wrap(number, count):
        return jnp.where(number >= count, number - count, number)

    def inside(strip):
        return (strip >= 0) & (strip < tiles)

    def each(lo, hi, fn):
        if hi - lo <= 32:
            for step in range(lo, hi):
                fn(step)
        else:
            def body(step, carry):
                fn(step)
                return carry
            lax.fori_loop(lo, hi, body, 0)

    def each_peer(fn):
        def along(hop):
            for turn in range(chans):
                fn(hop * chans + turn, (wrap(ti + hop, tiles), wrap(ci + turn, chans)))
        each(1, tiles, along)
        for turn in range(1, chans):
            fn(turn, (ti, wrap(ci + turn, chans)))

    each_peer(
        lambda n, who: pl.semaphore_signal(barrier, inc=1, device_id=who, device_id_type=MESH)
    )

    loads[0].wait()

    flat = feat[...].astype(F32).reshape(rows * chan_own, cols)
    lane = lax.broadcasted_iota(jnp.int32, (1, LANES), 1)
    for k in range(chans):
        first_col = k * own_cols - margin
        turned = pltpu.roll(flat, (-first_col) % cols, 1)[:, :LANES]
        on_map = (lane + first_col >= 0) & (lane + first_col < cols)
        win[k] = jnp.where(on_map, turned, 0.0).astype(BF16).reshape(rows, chan_own, LANES)

    def span(delta):
        low = max(0, rows * delta - HALO)
        high = min(rows, rows * delta + HALO + rows)
        return low, high - low, HALO - rows * delta + low

    for delta in (1, -1, 2, -2):
        @pl.when(jnp.logical_not(inside(wt - delta)))
        def _(delta=delta):
            _, count, at = span(delta)
            inp[at : at + count] = jnp.zeros((count, chan, LANES), BF16)

    for load in loads[1:]:
        load.wait()
    pltpu.make_async_copy(numbers, numbers, load_sem.at[len(loads)]).wait()
    per_row = cols // TILE_COLS
    own, cell_no = owner[...], cell[...]
    target_row = target[...].astype(F32)
    table = jnp.concatenate(
        [
            (target[...] * (rows // TILE_ROWS) + own // per_row).astype(F32),
            (own % per_row).astype(F32),
            net_e[...].astype(F32),
            weight[...],
            net_p[...].astype(F32),
            target_row,
            jnp.zeros((2, entries), F32),
        ],
        axis=0,
    )
    columns = jnp.transpose(table)
    wpin_col, net_p_col = columns[:, 3:4], columns[:, 4:5]
    strength = jnp.sum(
        jnp.where(net_p_col == table[2:3, :], wpin_col, 0.0), axis=0, keepdims=True
    )
    src_j = lax.broadcasted_iota(jnp.int32, (LANES, TILE_ROWS * LANES), 0)
    dst_j = lax.broadcasted_iota(jnp.int32, (LANES, TILE_ROWS * LANES), 1)
    pick = src_j == (dst_j // LANES) * TILE_COLS + dst_j % TILE_COLS
    spread = jnp.dot(
        frac[...], jnp.where(pick, 1.0, 0.0).astype(BF16), preferred_element_type=F32
    )
    wide = lax.broadcasted_iota(jnp.int32, (1, TILE_ROWS * LANES), 1) % LANES
    block = (wide + ci * own_cols - margin + TILE_COLS * LANES) // TILE_COLS - LANES
    fmask[...] = jnp.where(columns[:, 1:2] == block.astype(F32), spread, 0.0).astype(BF16)
    blocks = height // TILE_ROWS
    block_row = lax.broadcasted_iota(jnp.int32, (blocks, entries), 0).astype(F32)
    placed = jnp.where(block_row == table[0:1, :], strength, 0.0)
    left = jnp.concatenate(split(placed, 2), axis=0)
    partial = jnp.dot(left, fmask[...], preferred_element_type=F32)
    partial = partial[:blocks] + partial[blocks:]
    for i in range(TILE_ROWS):
        dbuf[pl.ds(i, blocks, stride=TILE_ROWS), :] = partial[:, i * LANES : (i + 1) * LANES]
    dsend[...] = dbuf[...].astype(BF16)

    def piece(side, q):
        return (q + side * (PIECES - 1 - 2 * q)) * some_rows

    def feat_copy(turn, q, mine=False):
        low = piece(ti % 2, q)
        to = wrap(ci + turn, chans)
        src = win.at[to, pl.ds(low, some_rows)]
        dst = gath.at[
            pl.ds(low, some_rows), pl.ds(pl.multiple_of(ci * chan_own, chan_own), chan_own)
        ]
        if mine:
            return pltpu.make_async_copy(src, dst, frecv_sem.at[q])
        return pltpu.make_async_remote_copy(
            src_ref=src, dst_ref=dst,
            send_sem=send_sem.at[FEAT], recv_sem=frecv_sem.at[q],
            device_id=at_work(ti, to), device_id_type=MESH,
        )

    def came(dst, sem, n):
        return pltpu.make_async_remote_copy(
            src_ref=dst, dst_ref=dst, send_sem=send_sem.at[n], recv_sem=sem,
            device_id=(ti, wrap(ci + 1, chans)), device_id_type=MESH,
        )

    def unless_mine(fn):
        @pl.when(jnp.logical_not(alike))
        def _():
            fn(False)

        @pl.when(alike)
        def _():
            fn(True)

    def feat_send(turn, q):
        if turn:
            feat_copy(turn, q).start()
        else:
            unless_mine(lambda mine: feat_copy(0, q, mine).start())

    def feat_wait(q):
        came(gath.at[pl.ds(piece(par, q), some_rows)], frecv_sem.at[q], FEAT).wait_recv()

    def demand_copy(step, mine=False):
        to = wrap(ti + step, tiles)
        src = dsend.at[pl.ds(pl.multiple_of(to * rows, rows), rows)]
        if mine:
            return pltpu.make_async_copy(src, drecv.at[step], drecv_sem)
        return pltpu.make_async_remote_copy(
            src_ref=src, dst_ref=drecv.at[step],
            send_sem=send_sem.at[DEMAND], recv_sem=drecv_sem,
            device_id=at_work(to, ci), device_id_type=MESH,
        )

    def entry_copy(step, mine=False):
        to = wrap(ti + step, tiles)
        if mine:
            return pltpu.make_async_copy(esend.at[to], erecv.at[ti], erecv_sem)
        return pltpu.make_async_remote_copy(
            src_ref=esend.at[to], dst_ref=erecv.at[ti],
            send_sem=send_sem.at[ENTRY], recv_sem=erecv_sem,
            device_id=at_work(to, ci), device_id_type=MESH,
        )

    pl.semaphore_wait(barrier, others)
    each(1, tiles, lambda s: demand_copy(s).start())
    unless_mine(lambda mine: demand_copy(0, mine).start())
    for q in range(PIECES):
        for turn in range(chans - 1, -1, -1):
            feat_send(turn, q)

    lift_row = lift[...]
    lift_col = jnp.transpose(jnp.broadcast_to(lift_row, (LANES, chan)))
    for u in range(3):
        for v in range(3):
            at_v, at_u = slice(v * chan, (v + 1) * chan), slice(u * chan, (u + 1) * chan)
            wm1[at_v, at_u] = jnp.transpose(w4[u, v].astype(F32)).astype(BF16)
            wm2[at_v, at_u] = jnp.transpose(w8[u, v].astype(F32)).astype(BF16)
            wm3[at_v, at_u] = w8[2 - u, 2 - v]
    taps = []
    for v in range(3):
        taps.append(
            jnp.concatenate(
                [
                    jnp.sum(
                        w4[2 - u, 2 - v].astype(F32) * lift_col[:, :chan], axis=0, keepdims=True
                    )
                    for u in range(3)
                ],
                axis=1,
            )
        )
    tap_rows = jnp.concatenate(taps + [jnp.zeros((5, 3 * chan), F32)], axis=0)
    hi, mid, low_part = [p.astype(F32) for p in split(tap_rows, 3)]
    wm4[...] = jnp.concatenate(
        [hi, mid, low_part, jnp.zeros((8, 3 * chan), F32)], axis=0
    ).astype(BF16)

    before = lax.broadcasted_iota(jnp.int32, (entries, entries), 0) < lax.broadcasted_iota(
        jnp.int32, (entries, entries), 1
    )
    rank = jnp.sum(
        jnp.where((columns[:, 5:6] == target_row) & before, 1.0, 0.0), axis=0, keepdims=True
    )
    key = target_row * float(cap) + rank
    pin_rows = [
        row[:, n * LANES : (n + 1) * LANES]
        for row in (table[4:5, :], (cell_no // PART).astype(F32), (cell_no % PART).astype(F32))
        for n in range(pins // LANES)
    ]
    fixed = jnp.concatenate(
        [jnp.zeros((2, LANES), F32)] + pin_rows
        + [jnp.zeros((1, LANES), F32)] * (META - 2 - len(pin_rows)),
        axis=0,
    )
    loose = jnp.concatenate(
        [table[2:3, :], own.astype(F32), jnp.zeros((META - 2, entries), F32)], axis=0
    ).astype(BF16)
    slot = lax.broadcasted_iota(jnp.int32, (cap, entries), 0).astype(F32)
    wide_slot = lax.broadcasted_iota(jnp.int32, (LANES, entries), 0) - (ti % per) * cap
    wide_slot = jnp.where(
        (wide_slot >= 0) & (wide_slot < cap), wide_slot, -(cap * tiles + 1)
    ).astype(F32)

    def pack(to):
        base = jnp.asarray(to * cap, F32) if isinstance(to, int) else (to * cap).astype(F32)
        hot = jnp.where(slot + base == key, 1.0, 0.0).astype(BF16)
        esend[to, :cap] = jnp.dot(hot, frac[...], preferred_element_type=F32).astype(BF16)
        hot = jnp.where(wide_slot + base == key, 1.0, 0.0).astype(BF16)
        meta = lax.dot_general(
            loose, hot, (((1,), (1,)), ((), ())), preferred_element_type=F32
        )
        esend[to, cap:] = (meta + fixed).astype(BF16)

    each(0, tiles, pack)
    each(1, tiles, lambda s: entry_copy(s).start())
    unless_mine(lambda mine: entry_copy(0, mine).start())

    def rim(role, sending):
        to, h = wt - 2 * near, 1 - par
        n = RIMS.index(role)
        if sending:
            start = HALO + h * half
            if role == "R":
                start, to = HALO + rows * near + half * (1 - par), wt - near
                at = HALO + 2 * rows * near + half * (1 - par)
                there = inside(to) & inside(wt + near)
            else:
                at = HALO + (wt - to) * rows + h * half
                there = inside(to)
            copy = pltpu.make_async_remote_copy(
                src_ref=inp.at[pl.ds(start, half)], dst_ref=inp.at[pl.ds(at, half)],
                send_sem=send_sem.at[RIM], recv_sem=hrecv_sem.at[n],
                device_id=at_work(to, wc), device_id_type=MESH,
            )
        else:
            come, at = {
                "A0": (wt + near, HALO + rows * near + half * (1 - par)),
                "A1": (wt + near, HALO + rows * near + half * par),
                "B0": (wt - near, HALO - rows * near + half * (1 - par)),
                "B1": (wt - near, HALO - rows * near + half * par),
                "F": (wt + 2 * near, HALO + 2 * rows * near + half * (1 - par)),
                "R": (wt - 2 * near, HALO - 2 * rows * near + half * par),
            }[role]
            there = inside(come)
            copy = came(inp.at[pl.ds(at, half)], hrecv_sem.at[n], RIM)
        return there, copy

    def rim_start(role):
        there, copy = rim(role, True)

        @pl.when(there)
        def _():
            copy.start()

    def rim_wait(role):
        there, copy = rim(role, False)

        @pl.when(there)
        def _():
            copy.wait_recv()

    came(drecv, drecv_sem, DEMAND).wait_recv()
    demand[...] = lax.fori_loop(
        1, tiles, lambda s, t: t + drecv[s].astype(F32), drecv[0].astype(F32)
    )

    def fill(q):
        for j in range(some_rows):
            row = piece(par, q) + j
            add = lift_col * demand[pl.ds(row, 1), :]
            inp[HALO + row] = (gath[row].astype(F32) + add).astype(BF16)

    def near_start(q):
        low = piece(par, q)
        n = 2 * q // PIECES
        for role, to in (("A", wt + near), ("B", wt - near)):
            @pl.when(inside(to))
            def _(role=role, to=to):
                pltpu.make_async_remote_copy(
                    src_ref=inp.at[pl.ds(HALO + low, some_rows)],
                    dst_ref=inp.at[pl.ds(HALO + (wt - to) * rows + low, some_rows)],
                    send_sem=send_sem.at[RIM], recv_sem=hrecv_sem.at[RIMS.index(role + str(n))],
                    device_id=at_work(to, wc), device_id_type=MESH,
                ).start()

    for q in range(PIECES):
        feat_wait(q)
        fill(q)
        near_start(q)

    def in_map(row):
        return (row >= 0) & (row < height)

    col = lane + wc * own_cols - margin
    col_ok = ((col >= 0) & (col < cols)).astype(F32)

    def gathered(ref, at, dilation):
        return jnp.concatenate(
            [
                jnp.concatenate([ref[at + j + u * dilation] for u in range(3)], axis=0)
                for j in range(GROUP)
            ],
            axis=1,
        )

    def conv(ref, at, weights, dilation):
        result = jnp.dot(weights[...], gathered(ref, at, dilation), preferred_element_type=F32)
        parts = []
        for j in range(GROUP):
            one = result[:, j * LANES : (j + 1) * LANES]
            parts.append(
                one[chan : 2 * chan]
                + pltpu.roll(one[:chan].astype(BF16), dilation, 1).astype(F32)
                + pltpu.roll(one[2 * chan :].astype(BF16), LANES - dilation, 1).astype(F32)
            )
        return parts

    def keep_of(row):
        return col_ok * in_map(row).astype(F32)

    def first(at):
        keep = keep_of(top - 20 + at)
        for j, value in enumerate(conv(inp, at, wm1, 4)):
            pre[at + j] = value
            hid[at + j] = (value * jax.nn.sigmoid(value) * keep).astype(BF16)

    def second(at):
        keep = keep_of(top - 12 + at)
        for j, value in enumerate(conv(hid, at, wm2, 8)):
            sec[at + j] = (jax.nn.sigmoid(value) * keep).astype(BF16)

    def third(at):
        keep = keep_of(top - 4 + at)
        for j, value in enumerate(conv(sec, at, wm3, 8)):
            p = pre[at + j + 16]
            s = jax.nn.sigmoid(p)
            gpre[at + j] = (value * s * (1.0 + p * (1.0 - s)) * keep).astype(BF16)

    owned = ((lane >= margin) & (lane < margin + own_cols)).astype(F32)

    def fourth(at):
        result = jnp.dot(wm4[...], gathered(gpre, at, 4), preferred_element_type=F32)
        result = result[0:8] + result[8:16] + result[16:24]
        for j in range(GROUP):
            one = result[:, j * LANES : (j + 1) * LANES]
            line = (
                one[1:2]
                + pltpu.roll(one, 4, 1)[0:1]
                + pltpu.roll(one, LANES - 4, 1)[2:3]
            )
            gown[at + j : at + j + 1, :] = line * owned

    def groups(*work):
        for side in range(2):
            @pl.when(par == side)
            def _(side=side):
                for fn, count, which in work:
                    for g in which:
                        fn(count - GROUP - GROUP * g if side else GROUP * g)

    def stage(ones, twos=(), threes=(), fours=()):
        groups(
            (first, rows + 40, ones), (second, rows + 24, twos),
            (third, rows + 8, threes), (fourth, rows, fours),
        )

    per_tile = rows // TILE_ROWS
    n_tiles = tile_hot.shape[0]
    lane_of = lax.broadcasted_iota(jnp.int32, (1, LANES), 1)
    counted = lax.broadcasted_iota(jnp.int32, (PART, LANES), 0).astype(F32).astype(BF16)

    def cells_of(g):
        known = [erecv[g * per + n, cap:, :].astype(F32) for n in range(per)]
        meta = known[0]
        for k in known[1:]:
            meta = meta + k
        net_row = meta[0:1, :] + (lane_of // cap * SPREAD).astype(F32)
        mine = meta[1:2, :].astype(jnp.int32)
        across = mine % per_row - wc * (own_cols // TILE_COLS)
        which = across * per_tile + mine // per_row
        which = jnp.where((across >= 0) & (across < own_cols // TILE_COLS), which, -1)
        at_g = pl.multiple_of(g * LANES, LANES)
        tile_hot[:, pl.ds(at_g, LANES)] = jnp.where(
            lax.broadcasted_iota(jnp.int32, (n_tiles, LANES), 0) == which, 1.0, 0.0
        )
        count = pins // LANES

        def pin_row(n, at):
            return jnp.concatenate([known[n][2 + at + m : 3 + at + m, :] for m in range(count)], axis=1)

        net_pin = jnp.concatenate([pin_row(n, 0) + float(n * SPREAD) for n in range(per)], axis=1)
        cell_part = jnp.concatenate([pin_row(n, count) for n in range(per)], axis=1)
        cell_row = jnp.concatenate([pin_row(n, 2 * count) for n in range(per)], axis=1)
        net_col = jnp.transpose(jnp.broadcast_to(net_row, (8, LANES)))[:, 0:1]
        same = jnp.where(net_col == net_pin, 1.0, 0.0).astype(BF16)

        def some(q):
            at_q = pl.multiple_of(q * PART, PART)
            part = jnp.asarray(q, F32) if isinstance(q, int) else q.astype(F32)
            row = jnp.where(cell_part == part, cell_row, -1.0)
            hot = jnp.concatenate(
                [
                    jnp.where(
                        counted == row[:, n * LANES : (n + 1) * LANES].astype(BF16),
                        jnp.ones((), BF16), jnp.zeros((), BF16),
                    )
                    for n in range(row.shape[1] // LANES)
                ],
                axis=1,
            )
            to_cell[pl.ds(at_g, LANES), pl.ds(at_q, PART)] = lax.dot_general(
                same, hot, (((1,), (1,)), ((), ())), preferred_element_type=F32
            ).astype(BF16)

        loop(to_cell.shape[1] // PART, some)

    def loop(count, fn):
        if count <= 4:
            for n in range(count):
                fn(n)
        else:
            def body(n, carry):
                fn(n)
                return carry
            lax.fori_loop(0, count, body, 0)


    @pl.when(alike)
    def _():
        came(erecv, erecv_sem, ENTRY).wait_recv()
        loop(tiles // per, cells_of)

    rim_wait("B0")
    rim_wait("B1")
    rim_start("F")
    stage(range(6, 12))

    @pl.when(jnp.logical_not(alike))
    def _():
        came(erecv, erecv_sem, ENTRY).wait_recv()
        loop(tiles // per, cells_of)

    rim_wait("A0")
    rim_start("R")
    stage(range(4, 6), range(4, 8))
    rim_wait("R")
    stage(range(12, 14), range(8, 10), range(4, 6))
    rim_wait("A1")
    rim_wait("F")
    stage(range(0, 4), range(0, 4), range(0, 4), range(0, 4))

    grads = gown[...]
    right = lax.broadcasted_iota(jnp.int32, (TILE_ROWS, LANES), 0) == (
        lax.broadcasted_iota(jnp.int32, (TILE_ROWS, LANES), 1) // TILE_COLS
    )
    leaning = [
        pltpu.roll(
            grads[a * TILE_ROWS : (a + 1) * TILE_ROWS], 0, 1, stride=TILE_COLS, stride_axis=0
        )
        for a in range(per_tile)
    ]
    parts = []
    for b in range(own_cols // TILE_COLS):
        for a in range(per_tile):
            moved = pltpu.roll(leaning[a], (-margin - b * TILE_COLS) % LANES, 1)
            parts.append(jnp.sum(jnp.where(right, moved, 0.0), axis=0, keepdims=True))
    by_tile = jnp.concatenate(
        [p.astype(F32) for p in split(jnp.concatenate(parts, axis=0), 3)], axis=0
    ).astype(BF16)
    all_frac = erecv[:, :cap, :].reshape(tiles * cap, LANES)
    found = lax.dot_general(
        by_tile, all_frac, (((1,), (1,)), ((), ())), preferred_element_type=F32
    )
    found = found[:n_tiles] + found[n_tiles : 2 * n_tiles] + found[2 * n_tiles :]
    entry_grad = jnp.sum(found * tile_hot[...], axis=0, keepdims=True)
    pieces = jnp.concatenate(
        [p.astype(F32) for p in split(entry_grad, 3)] + [jnp.zeros((5, tiles * cap), F32)], axis=0
    ).astype(BF16)
    cells = jnp.dot(pieces, to_cell[...], preferred_element_type=F32)
    cells = cells[0:1] + cells[1:2] + cells[2:3]
    for u in range(csend.shape[0]):
        csend[u] = cells[:, u * LANES : (u + 1) * LANES]

    share = LANES // CELL_DEV

    def cell_copy(step, to):
        return pltpu.make_async_remote_copy(
            src_ref=csend.at[to[0] // share], dst_ref=crecv.at[step],
            send_sem=send_sem.at[CELL], recv_sem=crecv_sem,
            device_id=to, device_id_type=MESH,
        )

    each_peer(lambda n, who: cell_copy(n, who).start())

    def sent(n, ref):
        came(ref, crecv_sem, n).wait_send()

    unless_mine(lambda mine: sent(FEAT, win.at[pl.ds(0, chans - mine)]))
    unless_mine(lambda mine: sent(DEMAND, dsend.at[pl.ds(0, (tiles - mine) * rows)]))
    unless_mine(lambda mine: sent(ENTRY, esend.at[pl.ds(0, tiles - mine)]))
    ahead, behind = inside(wt + near), inside(wt - 2 * near)
    for there, count in (
        (ahead & behind, 6), (ahead & jnp.logical_not(behind), 5),
        (jnp.logical_not(ahead) & behind, 3), (jnp.logical_not(ahead | behind), 2),
    ):
        @pl.when(there)
        def _(count=count):
            sent(RIM, inp.at[pl.ds(0, count * half)])
    arrived = crecv.at[pl.ds(1, others)]
    came(arrived, crecv_sem, CELL).wait()
    chain = -(-others // 4)
    sums = [
        jnp.sum(crecv[low : min(low + chain, others + 1)], axis=0)
        for low in range(1, others + 1, chain)
    ]
    total = csend[ti // share] + ((sums[0] + sums[1]) + (sums[2] + sums[3]))
    for n in range(1, share):
        total = jnp.where(ti % share == n, pltpu.roll(total, LANES - n * CELL_DEV, 1), total)
    out[...] = total


def solution(mesh):
    tiles, chans = mesh.shape["tile"], mesh.shape["chan"]

    def local(
        feat, lift, w4, w8, frac, target, owner, net_e, weight, net_p, cell,
    ):
        rows, chan_own, cols = feat.shape
        chan = chan_own * chans
        entries = frac.shape[0]
        pins = weight.shape[0]
        in_rows = rows + 2 * HALO
        height = rows * tiles
        cap = -(-(2 * entries // tiles) // 16) * 16
        n_tiles = rows // TILE_ROWS * (cols // chans // TILE_COLS)
        vm = pltpu.VMEM
        dma = pltpu.SemaphoreType.DMA
        result = pl.pallas_call(
            functools.partial(kernel, tiles, chans),
            out_shape=pltpu.VMEM((1, LANES), F32),
            in_specs=[pl.BlockSpec(memory_space=pltpu.HBM)] * 11,
            out_specs=pl.BlockSpec(memory_space=pltpu.VMEM),
            scratch_shapes=[
                vm(feat.shape, BF16),
                vm((1, chan), F32),
                vm(w4.shape, BF16),
                vm(w8.shape, BF16),
                vm(frac.shape, BF16),
                vm((5, 1, entries), jnp.int32),
                vm((1, pins), F32),
                dma((7,)),
                vm((chans, rows, chan_own, LANES), BF16),
                vm((rows, chan, LANES), BF16),
                vm((in_rows, chan, LANES), BF16),
                vm((rows + 40, chan, LANES), F32),
                vm((rows + 40, chan, LANES), BF16),
                vm((rows + 24, chan, LANES), BF16),
                vm((rows + 8, chan, LANES), BF16),
                vm((3 * chan, 3 * chan), BF16),
                vm((3 * chan, 3 * chan), BF16),
                vm((3 * chan, 3 * chan), BF16),
                vm((32, 3 * chan), BF16),
                vm((entries, TILE_ROWS * LANES), BF16),
                vm((height, LANES), F32),
                vm((height, LANES), BF16),
                vm((tiles, rows, LANES), BF16),
                vm((rows, LANES), F32),
                vm((rows, LANES), F32),
                vm((tiles, cap + META, LANES), BF16),
                vm((tiles, cap + META, LANES), BF16),
                vm((tiles * cap, tiles * CELL_DEV), BF16),
                vm((n_tiles, tiles * cap), F32),
                vm((tiles * CELL_DEV // LANES, 1, LANES), F32),
                vm((tiles * chans, 1, LANES), F32),
                dma((5,)),
                dma((PIECES,)),
                dma((len(RIMS),)),
                dma(()),
                dma(()),
                dma(()),
            ],
            compiler_params=pltpu.CompilerParams(collective_id=0, has_side_effects=True),
        )(
            feat, lift.reshape(1, chan), w4, w8, frac, target.reshape(1, entries),
            owner.reshape(1, entries), net_e.reshape(1, entries), weight.reshape(1, pins),
            net_p.reshape(1, pins), cell.reshape(1, pins),
        )
        return result[0, :CELL_DEV]

    in_specs = (
        P("tile", "chan", None), P(), P(), P(),
        P("tile", None), P("tile", None),
        P("tile"), P("tile"), P("tile"), P("tile"), P("tile"),
    )
    return jax.shard_map(
        local, mesh=mesh, in_specs=in_specs, out_specs=P("tile"), check_vma=False
    )
```
